32 devices in a mesh: gx: 8 (over z, x), gy: 4 (over y, core).
Axes of the slice: x: 2, y: 2, z: 4, core: 2. Of those that a mesh axis runs over, the one named last changes fastest.
Arguments:
- fields: float32 [13, 8, 64, 512], P(None, None, 'gx', 'gy'), may hold values from -6 to 6
- density: float32 [8, 64, 512], P(None, 'gx', 'gy'), may hold values from 1.8 to 2.6
- fluid_density: float32 [8, 64, 512], P(None, 'gx', 'gy'), may hold values from 0.8 to 1.2
- mobility: float32 [8, 64, 512], P(None, 'gx', 'gy'), may hold values from 0.5 to 4
- lame_lambda: float32 [8, 64, 512], P(None, 'gx', 'gy'), may hold values from 2.5 to 4
- shear_modulus: float32 [8, 64, 512], P(None, 'gx', 'gy'), may hold values from 0.5 to 1.5
- biot_modulus: float32 [8, 64, 512], P(None, 'gx', 'gy'), may hold values from 1 to 3
- biot_coef: float32 [8, 64, 512], P(None, 'gx', 'gy'), may hold values from 0.3 to 0.9
- region_mask: int32 [8, 64, 512], P(None, 'gx', 'gy'), may hold values 0 or 1
- profile_index: int32 [8, 64, 512], P(None, 'gx', 'gy'), may hold values from 0 to 7
- profile_table: float32 [8], replicated, may hold values from 0.05 to 0.4
- source_cells: int32 [64], replicated, may hold values from 0 to 262143
- source_amp: float32 [4, 64], replicated, may hold values from -6 to 6
- receiver_cells: int32 [512], replicated, may hold values from 0 to 262143
- field_cot: float32 [13, 8, 64, 512], P(None, None, 'gx', 'gy'), may hold values from -6 to 6
- receiver_cot: float32 [4, 512], replicated, may hold values from -6 to 6
Outputs:
- field_grad: float32 [13, 8, 64, 512], P(None, None, 'gx', 'gy')
- param_grad: float32 [7, 8, 64, 512], P(None, None, 'gx', 'gy')
The draws below stay inside these ranges and needn't reach their ends.
Inputs may be any that keep to these rules, and one draw needn't show every extreme that they name: `source_cells`: flat index z * 64 * 512 + x * 512 + y; cells may repeat. `receiver_cells`: flat index z * 64 * 512 + x * 512 + y; cells may repeat.
All inputs are finite; a program needn't handle non-finite values. No bound on the sum of `region_mask` on one device may be relied on, other than what follows from the above.
Results may differ from the reference program's by a relative error of at most 0.000062.
Values sent between devices are 32-bit elements; how exact they have to be, the bound alone decides.
No kernel may reach another device: no remote copies, remote signals or barrier semaphores. Data moves between devices by JAX's collectives and lax.ppermute only.
A program may use at most 64 MiB of HBM per device.

```python
import math
import jax
import jax.numpy as jnp

NZ = 8
STEPS = 4
NSRC = 64
NREC = 512
NPROF = 8
NX = 64
NY = 512


def plant(result, rng, low, top_value):
    shape = result.shape
    index_at = [jax.random.randint(jax.random.fold_in(rng, axis), (), 0, shape[axis]) for axis in range(len(shape))]
    result = result.at[tuple(index_at)].set(low)
    longest = shape.index(max(shape))
    index_at[longest] = (index_at[longest] + 1) % shape[longest]
    return result.at[tuple(index_at)].set(top_value)


def levels(rng, dims, split, smallest, top_value):
    loudness = 1.0
    for position, shards_of in split:
        steps = jax.random.uniform(jax.random.fold_in(jax.random.fold_in(rng, 6), position), (shards_of,), jnp.float32, smallest / len(split), top_value / len(split))
        loudness = loudness * jnp.repeat(jnp.exp(steps), dims[position] // shards_of).reshape((-1,) + (1,) * (len(dims) - 1 - position))
    return loudness


def gaussian(own_key, shape, scale, most, split=(), dtype=jnp.bfloat16):
    values = scale * jax.random.normal(own_key, shape, jnp.float32)
    if split:
        values = values * levels(own_key, shape, split, -0.22, 0.18)
    return jnp.clip(values, -most, most).astype(dtype)


def setup_inputs(seed: int = 0) -> dict:
    key_of = jax.random.split(jax.random.key(seed), 17)
    fields = gaussian(key_of[0], (13, NZ, NX, NY), 1.0, 6.0, ((2, 8), (3, 4)), jnp.float32)
    density = jnp.clip(1.8 + 0.79999995 * jax.random.uniform(key_of[1], (NZ, NX, NY), jnp.float32) ** levels(key_of[1], (NZ, NX, NY), ((1, 8), (2, 4)), -0.2, 0.2), 1.8, 2.6)
    fluid_density = jnp.clip(0.8 + 0.40000004 * jax.random.uniform(key_of[2], (NZ, NX, NY), jnp.float32) ** levels(key_of[2], (NZ, NX, NY), ((1, 8), (2, 4)), -0.2, 0.2), 0.8, 1.2)
    mobility = jnp.clip(jnp.exp(math.log(4.0) - 2.0794415 * jax.random.uniform(key_of[3], (NZ, NX, NY), jnp.float32) ** levels(key_of[3], (NZ, NX, NY), ((1, 8), (2, 4)), -0.2, 0.2)), 0.5, 4.0)
    lame_lambda = jnp.clip(2.5 + 1.5 * jax.random.uniform(key_of[4], (NZ, NX, NY), jnp.float32) ** levels(key_of[4], (NZ, NX, NY), ((1, 8), (2, 4)), -0.2, 0.2), 2.5, 4.0)
    shear_modulus = jnp.clip(0.5 + 1.0 * jax.random.uniform(key_of[5], (NZ, NX, NY), jnp.float32) ** levels(key_of[5], (NZ, NX, NY), ((1, 8), (2, 4)), -0.2, 0.2), 0.5, 1.5)
    biot_modulus = jnp.clip(1.0 + 2.0 * jax.random.uniform(key_of[6], (NZ, NX, NY), jnp.float32) ** levels(key_of[6], (NZ, NX, NY), ((1, 8), (2, 4)), -0.2, 0.2), 1.0, 3.0)
    biot_coef = jnp.clip(0.3 + 0.59999996 * jax.random.uniform(key_of[7], (NZ, NX, NY), jnp.float32) ** levels(key_of[7], (NZ, NX, NY), ((1, 8), (2, 4)), -0.2, 0.2), 0.3, 0.9)
    region_mask = plant((jax.random.randint(key_of[8], (NZ, NX, NY), 0, 3) < 1).astype(jnp.int32), jax.random.fold_in(key_of[8], 1), 0, 1)
    profile_index = plant(jax.random.randint(key_of[9], (NZ, NX, NY), 0, NPROF), jax.random.fold_in(key_of[9], 1), 0, NPROF - 1).astype(jnp.int32)
    profile_table = jnp.clip(jax.random.uniform(key_of[10], (NPROF,), jnp.float32, 0.05, 0.4), 0.05, 0.4)
    source_cells = plant(jax.random.randint(key_of[11], (NSRC,), 0, NZ * NX * NY), jax.random.fold_in(key_of[11], 1), 0, (NZ * NX * NY) - 1).astype(jnp.int32)
    source_amp = gaussian(key_of[12], (STEPS, NSRC), 1.0, 6.0, (), jnp.float32)
    receiver_cells = plant(jax.random.randint(key_of[13], (NREC,), 0, NZ * NX * NY), jax.random.fold_in(key_of[13], 1), 0, (NZ * NX * NY) - 1).astype(jnp.int32)
    field_cot = gaussian(key_of[14], (13, NZ, NX, NY), 1.0, 6.0, ((2, 8), (3, 4)), jnp.float32)
    receiver_cot = gaussian(key_of[15], (STEPS, NREC), 1.0, 6.0, (), jnp.float32)
    return dict(fields=fields, density=density, fluid_density=fluid_density, mobility=mobility, lame_lambda=lame_lambda, shear_modulus=shear_modulus, biot_modulus=biot_modulus, biot_coef=biot_coef, region_mask=region_mask, profile_index=profile_index, profile_table=profile_table, source_cells=source_cells, source_amp=source_amp, receiver_cells=receiver_cells, field_cot=field_cot, receiver_cot=receiver_cot)


courant = 0.5

def diff_x(field):
    return (field[..., 2:, 1:-1] - field[..., :-2, 1:-1]) * 0.5

def diff_y(field):
    return (field[..., 1:-1, 2:] - field[..., 1:-1, :-2]) * 0.5

def inner(field):
    return field[..., 1:-1, 1:-1]

def diff_z(field):
    padded = jnp.pad(field, ((1, 1), (0, 0), (0, 0)))
    return (padded[2:] - padded[:-2]) * 0.5

def velocity_update(velocity, stress_pad, params):
    stress_xx, stress_yy, stress_zz, stress_yz, stress_xz, stress_xy, pressure = [stress_pad[member] for member in range(7)]
    forces = [diff_x(stress_xx) + diff_y(stress_xy) + diff_z(inner(stress_xz)), diff_x(stress_xy) + diff_y(stress_yy) + diff_z(inner(stress_yz)), diff_x(stress_xz) + diff_y(stress_yz) + diff_z(inner(stress_zz))]
    pushes = [-diff_x(pressure), -diff_y(pressure), -diff_z(inner(pressure))]
    density, fluid, mobility = (params[0], params[1], params[2])
    inertia = 3.0 * fluid
    determinant = density * inertia - fluid * fluid
    solid_new, fluid_new = ([], [])
    for direction in range(3):
        drive = pushes[direction] - mobility * velocity[3 + direction]
        solid_new.append(velocity[direction] + courant * (inertia * forces[direction] - fluid * drive) / determinant)
        fluid_new.append(velocity[3 + direction] + courant * (density * drive - fluid * forces[direction]) / determinant)
    return jnp.stack(solid_new + fluid_new)

def stress_update(stress, velocity_pad, params):
    solid_x, solid_y, solid_z, fluid_x, fluid_y, fluid_z = [velocity_pad[member] for member in range(6)]
    strain_xx = diff_x(solid_x)
    strain_yy = diff_y(solid_y)
    strain_zz = diff_z(inner(solid_z))
    div_solid = strain_xx + strain_yy + strain_zz
    div_fluid = diff_x(fluid_x) + diff_y(fluid_y) + diff_z(inner(fluid_z))
    lame, shear, modulus, coupling = (params[3], params[4], params[5], params[6])
    common = lame * div_solid + coupling * modulus * div_fluid
    return jnp.stack([stress[0] + courant * (common + 2.0 * shear * strain_xx), stress[1] + courant * (common + 2.0 * shear * strain_yy), stress[2] + courant * (common + 2.0 * shear * strain_zz), stress[3] + courant * shear * (diff_z(inner(solid_y)) + diff_y(solid_z)), stress[4] + courant * shear * (diff_z(inner(solid_x)) + diff_x(solid_z)), stress[5] + courant * shear * (diff_y(solid_x) + diff_x(solid_y)), stress[6] - courant * modulus * (coupling * div_solid + div_fluid)])

def pad_plane(block):
    return jnp.pad(block, ((0, 0), (0, 0), (1, 1), (1, 1)))

def one_step(state, params, amounts, source_cells, factor):
    velocity = velocity_update(state[0:6], pad_plane(state[6:13]), params)
    stress = stress_update(state[6:13], pad_plane(velocity), params)
    pressure = stress[6].reshape(-1).at[source_cells].add(amounts).reshape(stress[6].shape)
    stress = stress.at[6].set(pressure)
    return jnp.concatenate([velocity, stress], axis=0) * factor

def reference(fields, density, fluid_density, mobility, lame_lambda, shear_modulus, biot_modulus, biot_coef, region_mask, profile_index, profile_table, source_cells, source_amp, receiver_cells, field_cot, receiver_cot):
    factor = 1.0 - region_mask.astype(jnp.float32) * profile_table[profile_index]
    params = jnp.stack([density, fluid_density, mobility, lame_lambda, shear_modulus, biot_modulus, biot_coef])
    stepper = jax.checkpoint(one_step)

    def forward(start, coeffs):
        state = start
        records = []
        for step_index in range(STEPS):
            state = stepper(state, coeffs, source_amp[step_index], source_cells, factor)
            records.append(state[12].reshape(-1)[receiver_cells])
        return (state, jnp.stack(records))
    _, pullback = jax.vjp(forward, fields, params)
    field_grad, param_grad = pullback((field_cot, receiver_cot))
    return (field_grad, param_grad)
```

```python
import functools

import jax
import jax.numpy as jnp
from jax import lax
from jax.experimental import pallas as pl
from jax.experimental.pallas import tpu as pltpu
from jax.sharding import PartitionSpec as P


VX, VY, VZ, WX, WY, WZ, XX, YY, ZZ, YZ, XZ, XY, PP = range(13)
PH, PK, PM, PL, PS, PB, PA, PF = range(8)
EDGE = 8


class W:
    __slots__ = ("m", "h")

    def __init__(self, m, h):
        self.m, self.h = m, h

    def __add__(self, o):
        return W(self.m + o.m, self.h + o.h)

    def __sub__(self, o):
        return W(self.m - o.m, self.h - o.h)

    def __mul__(self, o):
        if isinstance(o, W):
            return W(self.m * o.m, self.h * o.h)
        return W(self.m * o, self.h * o)

    __rmul__ = __mul__

    def __neg__(self):
        return W(-self.m, -self.h)


def roll(x, shift, axis):
    shift %= x.shape[axis]
    return pltpu.roll(x, shift, axis) if shift else x


class Tile:
    def __init__(self, planes, columns, halo):
        self.shape = (planes, columns)
        self.planes, self.columns, self.halo = planes, columns, halo
        self.lane = lax.broadcasted_iota(jnp.int32, self.shape, 1)
        sub = lax.broadcasted_iota(jnp.int32, self.shape, 0)
        self.first, self.last = self.lane == 0, self.lane == columns - 1
        self.bottom, self.top = sub == 0, sub == planes - 1
        self.zero = jnp.zeros(self.shape, jnp.float32)

    def dy(self, w):
        a, b = roll(w.m, -1, 1), roll(w.h, -1, 1)
        c, d = roll(w.m, 1, 1), roll(w.h, 1, 1)
        return W(
            jnp.where(self.last, b, a) - jnp.where(self.first, d, c),
            jnp.where(self.last, a, b) - jnp.where(self.first, c, d),
        )

    def dz1(self, a):
        return jnp.where(self.top, 0.0, roll(a, -1, 0)) - jnp.where(self.bottom, 0.0, roll(a, 1, 0))

    def dz(self, w):
        return W(self.dz1(w.m), self.dz1(w.h))

    def pack(self, tiles):
        width = 2 * self.halo
        group = self.lane // width
        out = []
        per = self.columns // width
        for base in range(0, len(tiles), per):
            total = self.zero
            for j, tile in enumerate(tiles[base : base + per]):
                total = jnp.where(group == j, roll(tile, self.halo + width * j, 1), total)
            out.append(total)
        return out

    def unpack(self, tiles, index):
        width = 2 * self.halo
        per = self.columns // width
        return roll(tiles[index // per], -(self.halo + width * (index % per)), 1)


def dx(get, name, r, low=True, high=True):
    if low and high:
        return get(name, r + 1) - get(name, r - 1)
    return get(name, r + 1) if high else -get(name, r - 1)


def read(ref, *at):
    planes = ref.shape[-2] // 2
    return W(ref[(*at, pl.ds(0, planes))], ref[(*at, pl.ds(planes, planes))])


def write(ref, value, *at):
    planes = ref.shape[-2] // 2
    ref[(*at, pl.ds(0, planes))] = value.m
    ref[(*at, pl.ds(planes, planes))] = value.h


def memo(fn):
    return functools.lru_cache(maxsize=None)(fn)


def momentum(tile, s, r, low=True, high=True):
    forces = [
        dx(s, XX, r, low, high) + tile.dy(s(XY, r)) + tile.dz(s(XZ, r)),
        dx(s, XY, r, low, high) + tile.dy(s(YY, r)) + tile.dz(s(YZ, r)),
        dx(s, XZ, r, low, high) + tile.dy(s(YZ, r)) + tile.dz(s(ZZ, r)),
    ]
    slopes = [dx(s, PP, r, low, high), tile.dy(s(PP, r)), tile.dz(s(PP, r))]
    return forces, slopes


def forward_edge(tile, s, v, p, r, low, high):
    forces, slopes = momentum(tile, s, r, low, high)
    h, k, m = p(PH, r), p(PK, r), p(PM, r)
    out = []
    for i in range(3):
        g = -(slopes[i] + m * v(WX + i, r))
        out.append(v(VX + i, r) + h * (3.0 * forces[i] - g))
        if i == 0:
            drive = v(WX, r) + h * (k * g - forces[0])
    return [s(XX, r), s(XY, r), s(XZ, r), s(PP, r)] + out + [drive]


def adjoint_stress(p, a, r):
    trace = a(XX, r) + a(YY, r) + a(ZZ, r)
    b, pi = p(PB, r), a(PP, r)
    cross = p(PA, r) * b
    common = p(PL, r) * trace - cross * pi
    s = p(PS, r)
    s2 = 2.0 * s
    return {
        XX: common + s2 * a(XX, r),
        YY: common + s2 * a(YY, r),
        ZZ: common + s2 * a(ZZ, r),
        YZ: s * a(YZ, r),
        XZ: s * a(XZ, r),
        XY: s * a(XY, r),
        PP: cross * trace - b * pi,
    }


def adjoint_edge(tile, q, a, p, r, low, high):
    forces, slopes = momentum(tile, q, r, low, high)
    h, k = p(PH, r), p(PK, r)
    out = []
    for i in range(3):
        lv, lw = a(VX + i, r) - forces[i], a(WX + i, r) - slopes[i]
        out.append(h * (3.0 * lv - lw))
        if i == 0:
            drive = h * (k * lw - lv)
    return [q(XX, r), q(XY, r), q(XZ, r), q(PP, r)] + out + [drive]


def send(tile, even, first_rows, last_rows, a_ref, b_ref):
    ups = [w.m for w in first_rows] + tile.pack([w.h for w in first_rows])
    downs = [w.m for w in last_rows] + tile.pack([w.h for w in last_rows])
    for n, (up, down) in enumerate(zip(ups, downs)):
        a_ref[n] = jnp.where(even, down, up)
        b_ref[n] = jnp.where(even, up, down)


def receive(tile, even, a_ref, b_ref, count):
    total = a_ref.shape[0]
    first = [jnp.where(even, b_ref[n], a_ref[n]) for n in range(total)]
    last = [jnp.where(even, a_ref[n], b_ref[n]) for n in range(total)]
    sides = []
    for got in (first, last):
        sides.append([W(got[n], tile.unpack(got[count:], n)) for n in range(count)])
    return sides


def start_kernel(halo, mx_axis, my_axis, fields_ref, cot_ref, par_ref, mask_ref, index_ref, table_ref, p_ref, a_ref, b_ref):
    even = lax.rem(lax.axis_index(my_axis), 2) == 0
    rows = p_ref.shape[1]
    planes, columns = p_ref.shape[2], p_ref.shape[3]
    lane = lax.broadcasted_iota(jnp.int32, (planes, columns), 1)
    group = lane // halo
    per = columns // halo

    def at(r):
        return pl.ds(r, planes, stride=rows)

    for r in range(rows):
        density, fluid, mobility, lame, shear, modulus, coupling = [par_ref[n][0, at(r), :] for n in range(7)]
        lookup = jnp.zeros((planes, columns), jnp.float32)
        index = index_ref[0, at(r), :]
        for n in range(table_ref.shape[1]):
            lookup = jnp.where(index == n, table_ref[0, n], lookup)
        p_ref[PH, r] = 0.25 / (3.0 * density - fluid)
        p_ref[PK, r] = density / fluid
        p_ref[PM, r] = 2.0 * mobility
        p_ref[PL, r] = 0.25 * lame
        p_ref[PS, r] = 0.25 * shear
        p_ref[PB, r] = 0.25 * modulus
        p_ref[PA, r] = coupling
        p_ref[PF, r] = 1.0 - mask_ref[0, at(r), :].astype(jnp.float32) * lookup
    sources = []
    for ref in (fields_ref, cot_ref):
        for f in range(ref.shape[0]):
            for r in range(rows):
                sources.append(lambda ref=ref, f=f, r=r: ref[f, at(r), :])
    for f in range(p_ref.shape[0]):
        for r in range(rows):
            sources.append(lambda f=f, r=r: p_ref[f, r])
    for n in range(a_ref.shape[0]):
        left = jnp.zeros((planes, columns), jnp.float32)
        right = left
        for g in range(per):
            if n * per + g < len(sources):
                x = sources[n * per + g]()
                left = jnp.where(group == g, roll(x, halo * g, 1), left)
                right = jnp.where(group == g, roll(x, halo * g + halo, 1), right)
        a_ref[n] = jnp.where(even, right, left)
        b_ref[n] = jnp.where(even, left, right)


def inject_kernel(halo, rec_ref, cot_ref, src_ref, amp_ref, rec_out, src_out):
    for cells_ref, amounts_ref, out in ((rec_ref, cot_ref, rec_out), (src_ref, amp_ref, src_out)):
        steps, rows, planes2, columns = out.shape
        planes = planes2 // 2
        count = amounts_ref.shape[1]
        row, col = cells_ref[0:1, :], cells_ref[1:2, :]
        row_at = lax.broadcasted_iota(jnp.int32, (rows * planes, count), 0)
        here = row_at == row
        lhs = jnp.concatenate([jnp.where(here, amounts_ref[t : t + 1, :], 0.0) for t in range(steps)], axis=0)
        lane = lax.broadcasted_iota(jnp.int32, (columns, count), 0)
        side = jnp.where(lane < halo, lane + columns, jnp.where(lane >= columns - halo, lane - columns, -columns))
        for half, where in enumerate((lane, side)):
            rhs = (where == col).astype(jnp.float32)
            got = lax.dot_general(
                lhs, rhs, (((1,), (1,)), ((), ())), precision=lax.Precision.HIGHEST, preferred_element_type=jnp.float32
            )
            for t in range(steps):
                for r in range(rows):
                    base = (t * rows + r) * planes
                    out[t, r, pl.ds(half * planes, planes)] = got[base : base + planes]


def spread_kernel(halo, gx_axis, gy_axis, fields_ref, cot_ref, pm_ref, ay_ref, by_ref, rec_ref,
                  f_out, a_out, p_out, a_msg, b_msg):
    even_x = lax.rem(lax.axis_index(gx_axis), 2) == 0
    even_y = lax.rem(lax.axis_index(gy_axis), 2) == 0
    rows, planes, columns = pm_ref.shape[1:]
    tile = Tile(planes, columns, halo)
    per = columns // halo
    packs = ay_ref.shape[0]
    right = [jnp.where(even_y, ay_ref[n], by_ref[n]) for n in range(packs)]
    left = [jnp.where(even_y, by_ref[n], ay_ref[n]) for n in range(packs)]
    on_right, on_left = tile.lane < halo, tile.lane >= columns - halo

    def side(n):
        g = n % per
        a = roll(right[n // per], -halo * g, 1)
        b = roll(left[n // per], columns - halo - halo * g, 1)
        return jnp.where(on_right, a, jnp.where(on_left, b, 0.0))

    def at(r):
        return pl.ds(r, planes, stride=rows)

    count = fields_ref.shape[0]
    for f in range(p_out.shape[0]):
        for r in range(rows):
            write(p_out, W(pm_ref[f, r], side((2 * count + f) * rows + r)), f, r)
    for f in range(count):
        for r in range(rows):
            write(f_out, W(fields_ref[f, at(r), :], side(f * rows + r)), f, r)
            value = W(cot_ref[f, at(r), :], side((count + f) * rows + r))
            if f == PP:
                value = value + read(rec_ref, rec_ref.shape[0] - 1, r)
            write(a_out, value * read(p_out, PF, r), f, r)
    messages(tile, even_x, f_out, a_out, p_out, a_msg, b_msg, True)


def messages(tile, even, f_ref, a_ref, p_ref, a_msg, b_msg, with_params):
    rows = f_ref.shape[1]
    s = lambda f, r: read(f_ref, f, r)
    a = lambda f, r: read(a_ref, f, r)
    p = lambda f, r: read(p_ref, f, r)
    qs = memo(lambda r: adjoint_stress(p, a, r))
    q = lambda f, r: qs(r)[f]
    sides = []
    for r, low, high in ((0, False, True), (rows - 1, True, False)):
        got = forward_edge(tile, s, s, p, r, low, high) + adjoint_edge(tile, q, a, p, r, low, high)
        if with_params:
            got += [p(PH, r), p(PK, r)]
        sides.append(got)
    send(tile, even, *sides, a_msg, b_msg)


def step_kernel(gx_axis, halo, j, steps, *refs):
    refs = list(refs)
    take = lambda n: [refs.pop(0) for _ in range(n)]
    f_ref, a_ref, p_ref, am_ref, bm_ref = take(5)
    first, final = j == 0, j == steps - 1
    store = 2 * j < steps - 1 or False
    keep_f, keep_a = j < steps - 1 - j, j < steps - 1 - j
    hk_ref = None if first else take(1)[0]
    src_ref = rec_ref = None
    if not final:
        src_ref, rec_ref = take(2)
    old_f_ref = old_a_ref = acc_ref = None
    if not keep_f:
        old_f_ref, old_a_ref = take(2)
        if j - 1 >= steps - j:
            acc_ref = take(1)[0]
    rho_ref = None
    if final:
        grad_out, par_out = take(2)
        f_out = a_out = None
    else:
        f_out, a_out, a_msg, b_msg = take(4)
    hk_out = take(1)[0] if first else None
    save_f = save_a = acc_out = None
    if keep_f:
        save_f, save_a = take(2)
    elif not final:
        acc_out = take(1)[0]
    assert not refs

    even = lax.rem(lax.axis_index(gx_axis), 2) == 0
    rows, planes, columns = f_ref.shape[1], f_ref.shape[2] // 2, f_ref.shape[3]
    tile = Tile(planes, columns, halo)
    sides = receive(tile, even, am_ref, bm_ref, 2 * EDGE + (2 if first else 0))
    p = lambda f, r: read(p_ref, f, r)
    old = lambda f, r: read(f_ref, f, r)
    lam = lambda f, r: read(a_ref, f, r)
    hk = []
    for n in range(2):
        if first:
            pair = sides[n][2 * EDGE : 2 * EDGE + 2]
            for m in range(2):
                write(hk_out, pair[m], n, m)
        else:
            pair = [read(hk_ref, n, m) for m in range(2)]
        hk.append(pair)
    slot = {XX: 0, XY: 1, XZ: 2, PP: 3}

    def end(r):
        return 0 if r < 0 else 1

    def s(f, r):
        return old(f, r) if 0 <= r < rows else sides[end(r)][slot[f]]

    @memo
    def velocity(r):
        if 0 <= r < rows:
            forces, slopes = momentum(tile, s, r)
            h, k, m = p(PH, r), p(PK, r), p(PM, r)
            out, pushes = {}, []
            for i in range(3):
                w = old(WX + i, r)
                g = -(slopes[i] + m * w)
                pushes.append(g)
                out[VX + i] = old(VX + i, r) + h * (3.0 * forces[i] - g)
                out[WX + i] = w + h * (k * g - forces[i])
            return out, forces, pushes
        n = end(r)
        got = sides[n][4:8]
        edge = 0 if n == 0 else rows - 1
        h, k = hk[n]
        t = h if n == 0 else -h
        xx, pp = t * old(XX, edge), t * old(PP, edge)
        return {
            VX: got[0] + (3.0 * xx + pp),
            VY: got[1] + 3.0 * (t * old(XY, edge)),
            VZ: got[2] + 3.0 * (t * old(XZ, edge)),
            WX: got[3] - (k * pp + xx),
        }, None, None

    v = lambda f, r: velocity(r)[0][f]

    def strain(r):
        e = [dx(v, VX, r), tile.dy(v(VY, r)), tile.dz(v(VZ, r))]
        g = [
            tile.dz(v(VY, r)) + tile.dy(v(VZ, r)),
            tile.dz(v(VX, r)) + dx(v, VZ, r),
            tile.dy(v(VX, r)) + dx(v, VY, r),
        ]
        dw = dx(v, WX, r) + tile.dy(v(WY, r)) + tile.dz(v(WZ, r))
        return e, g, dw

    qs = memo(lambda r: adjoint_stress(p, lam, r))

    def q(f, r):
        return qs(r)[f] if 0 <= r < rows else sides[end(r)][EDGE + slot[f]]

    @memo
    def cots(r):
        if 0 <= r < rows:
            forces, slopes = momentum(tile, q, r)
            h, k = p(PH, r), p(PK, r)
            cf, cg, vel = [], [], {}
            for i in range(3):
                lv, lw = lam(VX + i, r) - forces[i], lam(WX + i, r) - slopes[i]
                cf.append(h * (3.0 * lv - lw))
                cg.append(h * (k * lw - lv))
                vel[VX + i] = lv
                vel[WX + i] = lw - p(PM, r) * cg[i]
            return cf, cg, vel
        n = end(r)
        got = sides[n][EDGE + 4 : EDGE + 8]
        edge = 0 if n == 0 else rows - 1
        h, k = hk[n]
        t = -h if n == 0 else h
        xx, pp = t * q(XX, edge), t * q(PP, edge)
        return [
            got[0] + (3.0 * xx - pp),
            got[1] + 3.0 * (t * q(XY, edge)),
            got[2] + 3.0 * (t * q(XZ, edge)),
        ], [got[3] + (k * pp - xx)], None

    cF = lambda i, r: cots(r)[0][i]
    cG = lambda i, r: cots(r)[1][i]

    def adjoint_row(r):
        out = dict(cots(r)[2])
        out[XX] = lam(XX, r) - dx(cF, 0, r)
        out[YY] = lam(YY, r) - tile.dy(cF(1, r))
        out[ZZ] = lam(ZZ, r) - tile.dz(cF(2, r))
        out[YZ] = lam(YZ, r) - (tile.dz(cF(1, r)) + tile.dy(cF(2, r)))
        out[XZ] = lam(XZ, r) - (tile.dz(cF(0, r)) + dx(cF, 2, r))
        out[XY] = lam(XY, r) - (tile.dy(cF(0, r)) + dx(cF, 1, r))
        out[PP] = lam(PP, r) + (dx(cG, 0, r) + tile.dy(cG(1, r)) + tile.dz(cG(2, r)))
        return out

    stress_names = (XX, YY, ZZ, YZ, XZ, XY, PP)
    for r in range(rows):
        e, g, dw = strain(r)
        dv = e[0] + e[1] + e[2]
        new, forces, pushes = velocity(r)
        here_f = [x.m for x in forces + pushes] + [old(WX + i, r).m for i in range(3)]
        here_f += [x.m for x in e + g] + [dw.m]
        if not final:
            new = dict(new)
            sh, b = p(PS, r), p(PB, r)
            ab = p(PA, r) * b
            common = p(PL, r) * dv + ab * dw
            for i in range(3):
                new[XX + i] = old(XX + i, r) + (common + 2.0 * (sh * e[i]))
                new[YZ + i] = old(YZ + i, r) + sh * g[i]
            new[PP] = old(PP, r) - (ab * dv + b * dw) + read(src_ref, j, r)
            factor = p(PF, r)
            for f, value in new.items():
                write(f_out, value * factor, f, r)
        back = adjoint_row(r)
        cf, cg = cots(r)[0], cots(r)[1]
        here_a = [x.m for x in cf + cg] + [lam(f, r).m for f in stress_names]
        if final:
            for f, value in back.items():
                grad_out[f, pl.ds(r, planes, stride=rows), :] = value.m
        else:
            back[PP] = back[PP] + read(rec_ref, steps - 2 - j, r)
            for f, value in back.items():
                write(a_out, value * p(PF, r), f, r)
        if keep_f:
            for n, x in enumerate(here_f):
                save_f[n, r] = x
            for n, x in enumerate(here_a):
                save_a[n, r] = x
            continue
        acc = [0.0] * 9 if acc_ref is None else [acc_ref[n, r] for n in range(9)]
        pairs = [(here_f, [old_a_ref[n, r] for n in range(13)])]
        if 2 * j != steps - 1:
            pairs.append(([old_f_ref[n, r] for n in range(16)], here_a))
        for ff, aa in pairs:
            fo, pu, wo, ee, gg, w_ = ff[0:3], ff[3:6], ff[6:9], ff[9:12], ff[12:15], ff[15]
            af, ag, sg, pi = aa[0:3], aa[3:6], aa[6:12], aa[12]
            tr, dd = sg[0] + sg[1] + sg[2], ee[0] + ee[1] + ee[2]
            dot = lambda x, y: x[0] * y[0] + x[1] * y[1] + x[2] * y[2]
            adds = [
                dot(af, fo), dot(ag, pu), dot(af, pu), dot(ag, wo),
                tr * dd, tr * w_, 2.0 * dot(sg[0:3], ee) + dot(sg[3:6], gg), pi * dd, pi * w_,
            ]
            acc = [x + y for x, y in zip(acc, adds)]
        if not final:
            for n, x in enumerate(acc):
                acc_out[n, r] = x
            continue
        a1, a2, a3, a4, b1, b2, b3, b4, b5 = acc
        h4, k, b, al = 4.0 * p_ref[PH, r, pl.ds(0, planes)], p_ref[PK, r, pl.ds(0, planes)], p_ref[PB, r, pl.ds(0, planes)], p_ref[PA, r, pl.ds(0, planes)]
        grads = [
            h4 * (a3 - 3.0 * a1),
            h4 * (a1 + a2 - k * (3.0 * a2 + a3)),
            -2.0 * a4,
            0.25 * b1,
            0.25 * b3,
            0.25 * (al * (b2 - b4) - b5),
            b * (b2 - b4),
        ]
        for n, x in enumerate(grads):
            par_out[n, pl.ds(r, planes, stride=rows), :] = x
    if not final:
        messages(tile, even, f_out, a_out, p_ref, a_msg, b_msg, False)


def pairs(count, odd):
    out = []
    for i in range(odd, count - 1, 2):
        out += [(i, i + 1), (i + 1, i)]
    return out


def exchange(axis, a, b):
    count = lax.axis_size(axis)
    return lax.ppermute(a, axis, pairs(count, 0)), lax.ppermute(b, axis, pairs(count, 1))


def call(kernel, outs, *args, smem=()):
    specs = [
        pl.BlockSpec(memory_space=pltpu.SMEM if n in smem else pltpu.VMEM) for n in range(len(args))
    ]
    return pl.pallas_call(
        kernel,
        out_shape=[jax.ShapeDtypeStruct(s, jnp.float32) for s in outs],
        in_specs=specs,
        out_specs=[pl.BlockSpec(memory_space=pltpu.VMEM)] * len(outs),
        compiler_params=pltpu.CompilerParams(vmem_limit_bytes=48 << 20),
    )(*args)


def local(cells, planes, rows, columns):
    total_x, total_y = rows * lax.axis_size("gx"), columns * lax.axis_size("gy")
    depth, rest = cells // (total_x * total_y), cells % (total_x * total_y)
    x = rest // total_y - lax.axis_index("gx") * rows
    y = rest % total_y - lax.axis_index("gy") * columns
    inside = (x >= 0) & (x < rows)
    return jnp.stack([jnp.where(inside, x * planes + depth, -1), y])


def per_device(
    fields, density, fluid_density, mobility, lame_lambda, shear_modulus, biot_modulus, biot_coef,
    region_mask, profile_index, profile_table, source_cells, source_amp, receiver_cells, field_cot, receiver_cot,
):
    planes, rows, columns = region_mask.shape
    steps = source_amp.shape[0]
    count = fields.shape[0]
    halo = 2 * steps
    assert planes == 8 and columns == 128 and columns % (2 * halo) == 0 and rows > 1
    flat = lambda x: x.reshape(-1, planes * rows, columns)
    fields, field_cot = flat(fields), flat(field_cot)
    raw = [flat(x) for x in (density, fluid_density, mobility, lame_lambda, shear_modulus, biot_modulus, biot_coef)]
    packs = -(-(2 * count + 8) * rows * halo // columns)
    own, wide = (rows, planes, columns), (rows, 2 * planes, columns)

    def start(fields_ref, cot_ref, *refs):
        start_kernel(halo, "gx", "gy", fields_ref, cot_ref, refs[:7], *refs[7:])

    p_own, ay, by = call(
        start, [(8, *own)] + [(packs, planes, columns)] * 2,
        fields, field_cot, *raw, flat(region_mask), flat(profile_index), profile_table[None], smem=(11,),
    )
    ay, by = exchange("gy", ay, by)
    rec, src = call(
        functools.partial(inject_kernel, halo), [(steps, *wide)] * 2,
        local(receiver_cells, planes, rows, columns), receiver_cot,
        local(source_cells, planes, rows, columns), source_amp,
    )
    tiles = lambda n: n + -(-n * 2 * halo // columns)
    f, a, p, am, bm = call(
        functools.partial(spread_kernel, halo, "gx", "gy"),
        [(count, *wide)] * 2 + [(8, *wide)] + [(tiles(2 * EDGE + 2), planes, columns)] * 2,
        fields, field_cot, p_own, ay, by, rec,
    )
    saved, hk, acc = [], None, None
    for j in range(steps):
        am, bm = exchange("gx", am, bm)
        args, outs = [f, a, p, am, bm], []
        final, keep = j == steps - 1, j < steps - 1 - j
        if j:
            args.append(hk)
        if not final:
            args += [src, rec]
            outs += [(count, *wide)] * 2 + [(tiles(2 * EDGE), planes, columns)] * 2
        else:
            outs += [(count, planes * rows, columns), (7, planes * rows, columns)]
        if j == 0:
            outs.append((2, 2, 2 * planes, columns))
        if keep:
            outs += [(16, *own), (13, *own)]
        else:
            args += saved[steps - 1 - j]
            if acc is not None:
                args.append(acc)
            if not final:
                outs.append((9, *own))
        got = list(call(functools.partial(step_kernel, "gx", halo, j, steps), outs, *args))
        if final:
            return got[0].reshape(count, planes, rows, columns), got[1].reshape(7, planes, rows, columns)
        f, a, am, bm = got[:4]
        got = got[4:]
        if j == 0:
            hk = got.pop(0)
        if keep:
            saved.append(got)
        else:
            saved.append(None)
            acc = got[0]


def solution(mesh):
    plane, field = P(None, "gx", "gy"), P(None, None, "gx", "gy")
    in_specs = (field,) + (plane,) * 9 + (P(),) * 4 + (field, P())
    return jax.shard_map(per_device, mesh=mesh, in_specs=in_specs, out_specs=(field, field), check_vma=False)
```

```python
import functools

import jax
import jax.numpy as jnp
from jax import lax
from jax.experimental import pallas as pl
from jax.experimental.pallas import tpu as pltpu
from jax.sharding import PartitionSpec as P


VX, VY, VZ, WX, WY, WZ, XX, YY, ZZ, YZ, XZ, XY, PP = range(13)
PH, PK, PM, PL, PS, PB, PA, PF = range(8)
EDGE = 8


class W:
    __slots__ = ("m", "h")

    def __init__(self, m, h):
        self.m, self.h = m, h

    def __add__(self, o):
        return W(self.m + o.m, self.h + o.h)

    def __sub__(self, o):
        return W(self.m - o.m, self.h - o.h)

    def __mul__(self, o):
        if isinstance(o, W):
            return W(self.m * o.m, self.h * o.h)
        return W(self.m * o, self.h * o)

    __rmul__ = __mul__

    def __neg__(self):
        return W(-self.m, -self.h)


def roll(x, shift, axis):
    shift %= x.shape[axis]
    return pltpu.roll(x, shift, axis) if shift else x


class Tile:
    def __init__(self, planes, columns, halo):
        self.shape = (planes, columns)
        self.planes, self.columns, self.halo = planes, columns, halo
        self.lane = lax.broadcasted_iota(jnp.int32, self.shape, 1)
        sub = lax.broadcasted_iota(jnp.int32, self.shape, 0)
        self.first, self.last = self.lane == 0, self.lane == columns - 1
        self.bottom, self.top = sub == 0, sub == planes - 1
        self.zero = jnp.zeros(self.shape, jnp.float32)

    def dy(self, w):
        a, b = roll(w.m, -1, 1), roll(w.h, -1, 1)
        c, d = roll(w.m, 1, 1), roll(w.h, 1, 1)
        return W(
            jnp.where(self.last, b, a) - jnp.where(self.first, d, c),
            jnp.where(self.last, a, b) - jnp.where(self.first, c, d),
        )

    def dz1(self, a):
        return jnp.where(self.top, 0.0, roll(a, -1, 0)) - jnp.where(self.bottom, 0.0, roll(a, 1, 0))

    def dz(self, w):
        return W(self.dz1(w.m), self.dz1(w.h))

    def pack(self, tiles):
        width = 2 * self.halo
        group = self.lane // width
        out = []
        per = self.columns // width
        for base in range(0, len(tiles), per):
            total = self.zero
            for j, tile in enumerate(tiles[base : base + per]):
                total = jnp.where(group == j, roll(tile, self.halo + width * j, 1), total)
            out.append(total)
        return out

    def unpack(self, tiles, index):
        width = 2 * self.halo
        per = self.columns // width
        return roll(tiles[index // per], -(self.halo + width * (index % per)), 1)


def dx(get, name, r, low=True, high=True):
    if low and high:
        return get(name, r + 1) - get(name, r - 1)
    return get(name, r + 1) if high else -get(name, r - 1)


def read(ref, *at):
    planes = ref.shape[-2] // 2
    return W(ref[(*at, pl.ds(0, planes))], ref[(*at, pl.ds(planes, planes))])


def write(ref, value, *at):
    planes = ref.shape[-2] // 2
    ref[(*at, pl.ds(0, planes))] = value.m
    ref[(*at, pl.ds(planes, planes))] = value.h


def memo(fn):
    return functools.lru_cache(maxsize=None)(fn)


def momentum(tile, s, r, low=True, high=True):
    forces = [
        dx(s, XX, r, low, high) + tile.dy(s(XY, r)) + tile.dz(s(XZ, r)),
        dx(s, XY, r, low, high) + tile.dy(s(YY, r)) + tile.dz(s(YZ, r)),
        dx(s, XZ, r, low, high) + tile.dy(s(YZ, r)) + tile.dz(s(ZZ, r)),
    ]
    slopes = [dx(s, PP, r, low, high), tile.dy(s(PP, r)), tile.dz(s(PP, r))]
    return forces, slopes


def forward_edge(tile, s, v, p, r, low, high):
    forces, slopes = momentum(tile, s, r, low, high)
    h, k, m = p(PH, r), p(PK, r), p(PM, r)
    out = []
    for i in range(3):
        g = -(slopes[i] + m * v(WX + i, r))
        out.append(v(VX + i, r) + h * (3.0 * forces[i] - g))
        if i == 0:
            drive = v(WX, r) + h * (k * g - forces[0])
    return [s(XX, r), s(XY, r), s(XZ, r), s(PP, r)] + out + [drive]


def adjoint_stress(p, a, r):
    trace = a(XX, r) + a(YY, r) + a(ZZ, r)
    b, pi = p(PB, r), a(PP, r)
    cross = p(PA, r) * b
    common = p(PL, r) * trace - cross * pi
    s = p(PS, r)
    s2 = 2.0 * s
    return {
        XX: common + s2 * a(XX, r),
        YY: common + s2 * a(YY, r),
        ZZ: common + s2 * a(ZZ, r),
        YZ: s * a(YZ, r),
        XZ: s * a(XZ, r),
        XY: s * a(XY, r),
        PP: cross * trace - b * pi,
    }


def adjoint_edge(tile, q, a, p, r, low, high):
    forces, slopes = momentum(tile, q, r, low, high)
    h, k = p(PH, r), p(PK, r)
    out = []
    for i in range(3):
        lv, lw = a(VX + i, r) - forces[i], a(WX + i, r) - slopes[i]
        out.append(h * (3.0 * lv - lw))
        if i == 0:
            drive = h * (k * lw - lv)
    return [q(XX, r), q(XY, r), q(XZ, r), q(PP, r)] + out + [drive]


def send(tile, even, first_rows, last_rows, a_ref, b_ref):
    ups = [w.m for w in first_rows] + tile.pack([w.h for w in first_rows])
    downs = [w.m for w in last_rows] + tile.pack([w.h for w in last_rows])
    for n, (up, down) in enumerate(zip(ups, downs)):
        a_ref[n] = jnp.where(even, down, up)
        b_ref[n] = jnp.where(even, up, down)


def receive(tile, even, a_ref, b_ref, count):
    total = a_ref.shape[0]
    first = [jnp.where(even, b_ref[n], a_ref[n]) for n in range(total)]
    last = [jnp.where(even, a_ref[n], b_ref[n]) for n in range(total)]
    sides = []
    for got in (first, last):
        sides.append([W(got[n], tile.unpack(got[count:], n)) for n in range(count)])
    return sides


def start_kernel(halo, my_axis, inputs, outs, scratch):
    par_hbm, (mask_hbm, index_hbm, table_hbm), rest_hbm = inputs[:7], inputs[7:10], inputs[10:]
    p_ref, a_ref, b_ref, *rest = outs
    par_ref, mask_ref, index_ref, table_ref, sems = scratch
    fields_ref, cot_ref = rest[:2]
    copies = [pltpu.make_async_copy(src, par_ref.at[n], sems.at[n]) for n, src in enumerate(par_hbm)]
    for src, dst in zip((table_hbm, mask_hbm, index_hbm, *rest_hbm), (table_ref, mask_ref, index_ref, *rest)):
        copies.append(pltpu.make_async_copy(src, dst, sems.at[len(copies)]))
    for copy in copies:
        copy.start()
    for copy in copies[:10]:
        copy.wait()

    even = lax.rem(lax.axis_index(my_axis), 2) == 0
    rows = p_ref.shape[1]
    planes, columns = p_ref.shape[2], p_ref.shape[3]
    lane = lax.broadcasted_iota(jnp.int32, (planes, columns), 1)
    group = lane // halo
    per = columns // halo

    def at(r):
        return pl.ds(r, planes, stride=rows)

    for r in range(rows):
        density, fluid, mobility, lame, shear, modulus, coupling = [par_ref[n, 0, at(r), :] for n in range(7)]
        lookup = jnp.zeros((planes, columns), jnp.float32)
        index = index_ref[0, at(r), :]
        for n in range(table_ref.shape[1]):
            lookup = jnp.where(index == n, table_ref[0, n], lookup)
        p_ref[PH, r] = 0.25 / (3.0 * density - fluid)
        p_ref[PK, r] = density / fluid
        p_ref[PM, r] = 2.0 * mobility
        p_ref[PL, r] = 0.25 * lame
        p_ref[PS, r] = 0.25 * shear
        p_ref[PB, r] = 0.25 * modulus
        p_ref[PA, r] = coupling
        p_ref[PF, r] = 1.0 - mask_ref[0, at(r), :].astype(jnp.float32) * lookup
    sources = []
    for f in range(p_ref.shape[0]):
        for r in range(rows):
            sources.append(lambda f=f, r=r: p_ref[f, r])
    for ref in (fields_ref, cot_ref):
        for f in range(ref.shape[0]):
            for r in range(rows):
                sources.append(lambda ref=ref, f=f, r=r: ref[f, at(r), :])
    waited = False
    for n in range(a_ref.shape[0]):
        if (n + 1) * per > p_ref.shape[0] * rows and not waited:
            for copy in copies[10:]:
                copy.wait()
            waited = True
        left = jnp.zeros((planes, columns), jnp.float32)
        right = left
        for g in range(per):
            if n * per + g < len(sources):
                x = sources[n * per + g]()
                left = jnp.where(group == g, roll(x, halo * g, 1), left)
                right = jnp.where(group == g, roll(x, halo * g + halo, 1), right)
        a_ref[n] = jnp.where(even, right, left)
        b_ref[n] = jnp.where(even, left, right)


def inject_kernel(halo, gx_axis, gy_axis, rec_ref, cot_ref, src_ref, amp_ref, rec_out, src_out):
    for cells_ref, amounts_ref, out in ((rec_ref, cot_ref, rec_out), (src_ref, amp_ref, src_out)):
        steps, rows, planes2, columns = out.shape
        planes = planes2 // 2
        count = amounts_ref.shape[1]
        total_x, total_y = rows * lax.axis_size(gx_axis), columns * lax.axis_size(gy_axis)
        cells = cells_ref[...]
        line = lax.div(cells, jnp.full_like(cells, total_y))
        depth = lax.div(line, jnp.full_like(cells, total_x))
        col = cells - line * total_y - lax.axis_index(gy_axis) * columns
        x = line - depth * total_x - lax.axis_index(gx_axis) * rows
        row = jnp.where((x >= 0) & (x < rows), x * planes + depth, -1)
        row_at = lax.broadcasted_iota(jnp.int32, (rows * planes, count), 0)
        here = row_at == row
        lhs = jnp.concatenate([jnp.where(here, amounts_ref[t : t + 1, :], 0.0) for t in range(steps)], axis=0)
        lane = lax.broadcasted_iota(jnp.int32, (columns, count), 0)
        side = jnp.where(lane < halo, lane + columns, jnp.where(lane >= columns - halo, lane - columns, -columns))
        for half, where in enumerate((lane, side)):
            rhs = (where == col).astype(jnp.float32)
            got = lax.dot_general(
                lhs, rhs, (((1,), (1,)), ((), ())), precision=lax.Precision.HIGHEST, preferred_element_type=jnp.float32
            )
            for t in range(steps):
                for r in range(rows):
                    base = (t * rows + r) * planes
                    out[t, r, pl.ds(half * planes, planes)] = got[base : base + planes]


def spread_kernel(halo, gx_axis, gy_axis, fields_ref, cot_ref, pm_ref, ay_ref, by_ref, rec_ref,
                  f_out, a_out, p_out, a_msg, b_msg):
    even_x = lax.rem(lax.axis_index(gx_axis), 2) == 0
    even_y = lax.rem(lax.axis_index(gy_axis), 2) == 0
    rows, planes, columns = pm_ref.shape[1:]
    tile = Tile(planes, columns, halo)
    per = columns // halo
    packs = ay_ref.shape[0]
    right = [jnp.where(even_y, ay_ref[n], by_ref[n]) for n in range(packs)]
    left = [jnp.where(even_y, by_ref[n], ay_ref[n]) for n in range(packs)]
    on_right, on_left = tile.lane < halo, tile.lane >= columns - halo

    def side(n):
        g = n % per
        a = roll(right[n // per], -halo * g, 1)
        b = roll(left[n // per], columns - halo - halo * g, 1)
        return jnp.where(on_right, a, jnp.where(on_left, b, 0.0))

    def at(r):
        return pl.ds(r, planes, stride=rows)

    count, base = fields_ref.shape[0], p_out.shape[0]
    for f in range(p_out.shape[0]):
        for r in range(rows):
            write(p_out, W(pm_ref[f, r], side(f * rows + r)), f, r)
    for f in range(count):
        for r in range(rows):
            write(f_out, W(fields_ref[f, at(r), :], side((base + f) * rows + r)), f, r)
            value = W(cot_ref[f, at(r), :], side((base + count + f) * rows + r))
            if f == PP:
                value = value + read(rec_ref, rec_ref.shape[0] - 1, r)
            write(a_out, value * read(p_out, PF, r), f, r)
    messages(tile, even_x, f_out, a_out, p_out, a_msg, b_msg, True)


def messages(tile, even, f_ref, a_ref, p_ref, a_msg, b_msg, with_params):
    rows = f_ref.shape[1]
    s = lambda f, r: read(f_ref, f, r)
    a = lambda f, r: read(a_ref, f, r)
    p = lambda f, r: read(p_ref, f, r)
    qs = memo(lambda r: adjoint_stress(p, a, r))
    q = lambda f, r: qs(r)[f]
    sides = []
    for r, low, high in ((0, False, True), (rows - 1, True, False)):
        got = forward_edge(tile, s, s, p, r, low, high) + adjoint_edge(tile, q, a, p, r, low, high)
        if with_params:
            got += [p(PH, r), p(PK, r)]
        sides.append(got)
    send(tile, even, *sides, a_msg, b_msg)


def step_kernel(gx_axis, halo, j, steps, *refs):
    refs = list(refs)
    take = lambda n: [refs.pop(0) for _ in range(n)]
    f_ref, a_ref, p_ref, am_ref, bm_ref = take(5)
    first, final = j == 0, j == steps - 1
    keep_f, keep_a = j < steps - 1 - j, j < steps - 1 - j
    hk_ref = None if first else take(1)[0]
    src_ref = rec_ref = None
    if not final:
        src_ref, rec_ref = take(2)
    old_f_ref = old_a_ref = acc_ref = None
    if not keep_f:
        old_f_ref, old_a_ref = take(2)
        if j - 1 >= steps - j:
            acc_ref = take(1)[0]
    if final:
        grad_out, par_out = take(2)
        f_out = a_out = None
    else:
        f_out, a_out, a_msg, b_msg = take(4)
    hk_out = take(1)[0] if first else None
    save_f = save_a = acc_out = None
    if keep_f:
        save_f, save_a = take(2)
    elif not final:
        acc_out = take(1)[0]
    assert not refs

    even = lax.rem(lax.axis_index(gx_axis), 2) == 0
    rows, planes, columns = f_ref.shape[1], f_ref.shape[2] // 2, f_ref.shape[3]
    tile = Tile(planes, columns, halo)
    sides = receive(tile, even, am_ref, bm_ref, 2 * EDGE + (2 if first else 0))
    p = lambda f, r: read(p_ref, f, r)
    old = lambda f, r: read(f_ref, f, r)
    lam = lambda f, r: read(a_ref, f, r)
    hk = []
    for n in range(2):
        if first:
            pair = sides[n][2 * EDGE : 2 * EDGE + 2]
            for m in range(2):
                write(hk_out, pair[m], n, m)
        else:
            pair = [read(hk_ref, n, m) for m in range(2)]
        hk.append(pair)
    slot = {XX: 0, XY: 1, XZ: 2, PP: 3}

    def end(r):
        return 0 if r < 0 else 1

    def s(f, r):
        return old(f, r) if 0 <= r < rows else sides[end(r)][slot[f]]

    @memo
    def velocity(r):
        if 0 <= r < rows:
            forces, slopes = momentum(tile, s, r)
            h, k, m = p(PH, r), p(PK, r), p(PM, r)
            out, pushes = {}, []
            for i in range(3):
                w = old(WX + i, r)
                g = -(slopes[i] + m * w)
                pushes.append(g)
                out[VX + i] = old(VX + i, r) + h * (3.0 * forces[i] - g)
                out[WX + i] = w + h * (k * g - forces[i])
            return out, forces, pushes
        n = end(r)
        got = sides[n][4:8]
        edge = 0 if n == 0 else rows - 1
        h, k = hk[n]
        t = h if n == 0 else -h
        xx, pp = t * old(XX, edge), t * old(PP, edge)
        return {
            VX: got[0] + (3.0 * xx + pp),
            VY: got[1] + 3.0 * (t * old(XY, edge)),
            VZ: got[2] + 3.0 * (t * old(XZ, edge)),
            WX: got[3] - (k * pp + xx),
        }, None, None

    v = lambda f, r: velocity(r)[0][f]

    def strain(r):
        e = [dx(v, VX, r), tile.dy(v(VY, r)), tile.dz(v(VZ, r))]
        g = [
            tile.dz(v(VY, r)) + tile.dy(v(VZ, r)),
            tile.dz(v(VX, r)) + dx(v, VZ, r),
            tile.dy(v(VX, r)) + dx(v, VY, r),
        ]
        dw = dx(v, WX, r) + tile.dy(v(WY, r)) + tile.dz(v(WZ, r))
        return e, g, dw

    qs = memo(lambda r: adjoint_stress(p, lam, r))

    def q(f, r):
        return qs(r)[f] if 0 <= r < rows else sides[end(r)][EDGE + slot[f]]

    @memo
    def cots(r):
        if 0 <= r < rows:
            forces, slopes = momentum(tile, q, r)
            h, k = p(PH, r), p(PK, r)
            cf, cg, vel = [], [], {}
            for i in range(3):
                lv, lw = lam(VX + i, r) - forces[i], lam(WX + i, r) - slopes[i]
                cf.append(h * (3.0 * lv - lw))
                cg.append(h * (k * lw - lv))
                vel[VX + i] = lv
                vel[WX + i] = lw - p(PM, r) * cg[i]
            return cf, cg, vel
        n = end(r)
        got = sides[n][EDGE + 4 : EDGE + 8]
        edge = 0 if n == 0 else rows - 1
        h, k = hk[n]
        t = -h if n == 0 else h
        xx, pp = t * q(XX, edge), t * q(PP, edge)
        return [
            got[0] + (3.0 * xx - pp),
            got[1] + 3.0 * (t * q(XY, edge)),
            got[2] + 3.0 * (t * q(XZ, edge)),
        ], [got[3] + (k * pp - xx)], None

    cF = lambda i, r: cots(r)[0][i]
    cG = lambda i, r: cots(r)[1][i]

    def adjoint_row(r):
        out = dict(cots(r)[2])
        out[XX] = lam(XX, r) - dx(cF, 0, r)
        out[YY] = lam(YY, r) - tile.dy(cF(1, r))
        out[ZZ] = lam(ZZ, r) - tile.dz(cF(2, r))
        out[YZ] = lam(YZ, r) - (tile.dz(cF(1, r)) + tile.dy(cF(2, r)))
        out[XZ] = lam(XZ, r) - (tile.dz(cF(0, r)) + dx(cF, 2, r))
        out[XY] = lam(XY, r) - (tile.dy(cF(0, r)) + dx(cF, 1, r))
        out[PP] = lam(PP, r) + (dx(cG, 0, r) + tile.dy(cG(1, r)) + tile.dz(cG(2, r)))
        return out

    stress_names = (XX, YY, ZZ, YZ, XZ, XY, PP)
    for r in range(rows):
        e, g, dw = strain(r)
        dv = e[0] + e[1] + e[2]
        new, forces, pushes = velocity(r)
        here_f = [x.m for x in forces + pushes] + [old(WX + i, r).m for i in range(3)]
        here_f += [x.m for x in e + g] + [dw.m]
        if not final:
            new = dict(new)
            sh, b = p(PS, r), p(PB, r)
            ab = p(PA, r) * b
            common = p(PL, r) * dv + ab * dw
            for i in range(3):
                new[XX + i] = old(XX + i, r) + (common + 2.0 * (sh * e[i]))
                new[YZ + i] = old(YZ + i, r) + sh * g[i]
            new[PP] = old(PP, r) - (ab * dv + b * dw) + read(src_ref, j, r)
            factor = p(PF, r)
            for f, value in new.items():
                write(f_out, value * factor, f, r)
        back = adjoint_row(r)
        cf, cg = cots(r)[0], cots(r)[1]
        here_a = [x.m for x in cf + cg] + [lam(f, r).m for f in stress_names]
        if final:
            for f, value in back.items():
                grad_out[f, pl.ds(r, planes, stride=rows), :] = value.m
        else:
            back[PP] = back[PP] + read(rec_ref, steps - 2 - j, r)
            for f, value in back.items():
                write(a_out, value * p(PF, r), f, r)
        if keep_f:
            for n, x in enumerate(here_f):
                save_f[n, r] = x
            for n, x in enumerate(here_a):
                save_a[n, r] = x
            continue
        acc = [0.0] * 9 if acc_ref is None else [acc_ref[n, r] for n in range(9)]
        pairs = [(here_f, [old_a_ref[n, r] for n in range(13)])]
        if 2 * j != steps - 1:
            pairs.append(([old_f_ref[n, r] for n in range(16)], here_a))
        for ff, aa in pairs:
            fo, pu, wo, ee, gg, w_ = ff[0:3], ff[3:6], ff[6:9], ff[9:12], ff[12:15], ff[15]
            af, ag, sg, pi = aa[0:3], aa[3:6], aa[6:12], aa[12]
            tr, dd = sg[0] + sg[1] + sg[2], ee[0] + ee[1] + ee[2]
            dot = lambda x, y: x[0] * y[0] + x[1] * y[1] + x[2] * y[2]
            adds = [
                dot(af, fo), dot(ag, pu), dot(af, pu), dot(ag, wo),
                tr * dd, tr * w_, 2.0 * dot(sg[0:3], ee) + dot(sg[3:6], gg), pi * dd, pi * w_,
            ]
            acc = [x + y for x, y in zip(acc, adds)]
        if not final:
            for n, x in enumerate(acc):
                acc_out[n, r] = x
            continue
        a1, a2, a3, a4, b1, b2, b3, b4, b5 = acc
        h4, k, b, al = 4.0 * p_ref[PH, r, pl.ds(0, planes)], p_ref[PK, r, pl.ds(0, planes)], p_ref[PB, r, pl.ds(0, planes)], p_ref[PA, r, pl.ds(0, planes)]
        grads = [
            h4 * (a3 - 3.0 * a1),
            h4 * (a1 + a2 - k * (3.0 * a2 + a3)),
            -2.0 * a4,
            0.25 * b1,
            0.25 * b3,
            0.25 * (al * (b2 - b4) - b5),
            b * (b2 - b4),
        ]
        for n, x in enumerate(grads):
            par_out[n, pl.ds(r, planes, stride=rows), :] = x
    if not final:
        messages(tile, even, f_out, a_out, p_ref, a_msg, b_msg, False)


def pairs(count, odd):
    out = []
    for i in range(odd, count - 1, 2):
        out += [(i, i + 1), (i + 1, i)]
    return out


def exchange(axis, a, b):
    count = lax.axis_size(axis)
    return lax.ppermute(a, axis, pairs(count, 0)), lax.ppermute(b, axis, pairs(count, 1))


def call(kernel, outs, *args):
    shapes = [o if isinstance(o, jax.ShapeDtypeStruct) else jax.ShapeDtypeStruct(o, jnp.float32) for o in outs]
    return pl.pallas_call(
        kernel,
        out_shape=shapes,
        in_specs=[pl.BlockSpec(memory_space=pltpu.VMEM)] * len(args),
        out_specs=[pl.BlockSpec(memory_space=pltpu.VMEM)] * len(outs),
        compiler_params=pltpu.CompilerParams(vmem_limit_bytes=48 << 20),
    )(*args)


def per_device(
    fields, density, fluid_density, mobility, lame_lambda, shear_modulus, biot_modulus, biot_coef,
    region_mask, profile_index, profile_table, source_cells, source_amp, receiver_cells, field_cot, receiver_cot,
):
    planes, rows, columns = region_mask.shape
    steps = source_amp.shape[0]
    count = fields.shape[0]
    halo = 2 * steps
    assert steps % 2 == 0 and planes == 8 and columns == 128 and columns % (2 * halo) == 0 and rows > 1
    flat = lambda x: x.reshape(-1, planes * rows, columns)
    fields, field_cot = flat(fields), flat(field_cot)
    raw = [flat(x) for x in (density, fluid_density, mobility, lame_lambda, shear_modulus, biot_modulus, biot_coef)]
    packs = -(-(2 * count + 8) * rows * halo // columns)
    own, wide = (rows, planes, columns), (rows, 2 * planes, columns)

    table = profile_table[None]
    small = [receiver_cells[None], receiver_cot, source_cells[None], source_amp]
    inputs = [*raw, table, flat(region_mask), flat(profile_index), fields, field_cot, *small]
    whole = [fields, field_cot, *small]
    plane = (planes * rows, columns)

    def start(*refs):
        refs = list(refs)
        hbm = refs[:7] + refs[8:10] + refs[7:8] + refs[10:16]
        start_kernel(halo, "gy", hbm, refs[16:25], refs[25:])

    p_own, ay, by, fields, field_cot, *small = pl.pallas_call(
        start,
        out_shape=[jax.ShapeDtypeStruct(s, jnp.float32) for s in [(8, *own)] + [(packs, planes, columns)] * 2]
        + [jax.ShapeDtypeStruct(x.shape, x.dtype) for x in whole],
        in_specs=[pl.BlockSpec(memory_space=pltpu.HBM)] * 16,
        out_specs=[pl.BlockSpec(memory_space=pltpu.VMEM)] * 9,
        scratch_shapes=[
            pltpu.VMEM((7, 1, *plane), jnp.float32), pltpu.VMEM((1, *plane), jnp.int32),
            pltpu.VMEM((1, *plane), jnp.int32), pltpu.SMEM(table.shape, jnp.float32),
            pltpu.SemaphoreType.DMA((16,)),
        ],
        compiler_params=pltpu.CompilerParams(vmem_limit_bytes=48 << 20),
    )(*[pltpu.with_memory_space_constraint(x, pltpu.HBM) for x in inputs])
    ay, by = exchange("gy", ay, by)
    rec, src = call(functools.partial(inject_kernel, halo, "gx", "gy"), [(steps, *wide)] * 2, *small)
    tiles = lambda n: n + -(-n * 2 * halo // columns)
    f, a, p, am, bm = call(
        functools.partial(spread_kernel, halo, "gx", "gy"),
        [(count, *wide)] * 2 + [(8, *wide)] + [(tiles(2 * EDGE + 2), planes, columns)] * 2,
        fields, field_cot, p_own, ay, by, rec,
    )
    saved, hk, acc = [], None, None
    for j in range(steps):
        am, bm = exchange("gx", am, bm)
        args, outs = [f, a, p, am, bm], []
        final, keep = j == steps - 1, j < steps - 1 - j
        if j:
            args.append(hk)
        if not final:
            args += [src, rec]
            outs += [(count, *wide)] * 2 + [(tiles(2 * EDGE), planes, columns)] * 2
        else:
            outs += [(count, planes * rows, columns), (7, planes * rows, columns)]
        if j == 0:
            outs.append((2, 2, 2 * planes, columns))
        if keep:
            outs += [(16, *own), (13, *own)]
        else:
            args += saved[steps - 1 - j]
            if acc is not None:
                args.append(acc)
            if not final:
                outs.append((9, *own))
        got = list(call(functools.partial(step_kernel, "gx", halo, j, steps), outs, *args))
        if final:
            return got[0].reshape(count, planes, rows, columns), got[1].reshape(7, planes, rows, columns)
        f, a, am, bm = got[:4]
        got = got[4:]
        if j == 0:
            hk = got.pop(0)
        if keep:
            saved.append(got)
        else:
            saved.append(None)
            acc = got[0]


def solution(mesh):
    plane, field = P(None, "gx", "gy"), P(None, None, "gx", "gy")
    in_specs = (field,) + (plane,) * 9 + (P(),) * 4 + (field, P())
    return jax.shard_map(per_device, mesh=mesh, in_specs=in_specs, out_specs=(field, field), check_vma=False)
```

```python
import functools

import jax
import jax.numpy as jnp
from jax import lax
from jax.experimental import pallas as pl
from jax.experimental.pallas import tpu as pltpu
from jax.sharding import PartitionSpec as P


VX, VY, VZ, WX, WY, WZ, XX, YY, ZZ, YZ, XZ, XY, PP = range(13)
PH, PK, PM, PL, PS, PB, PA, PF = range(8)
EDGE = 8


class W:
    __slots__ = ("m", "h")

    def __init__(self, m, h):
        self.m, self.h = m, h

    def __add__(self, o):
        return W(self.m + o.m, self.h + o.h)

    def __sub__(self, o):
        return W(self.m - o.m, self.h - o.h)

    def __mul__(self, o):
        if isinstance(o, W):
            return W(self.m * o.m, self.h * o.h)
        return W(self.m * o, self.h * o)

    __rmul__ = __mul__

    def __neg__(self):
        return W(-self.m, -self.h)


def roll(x, shift, axis):
    shift %= x.shape[axis]
    return pltpu.roll(x, shift, axis) if shift else x


class Tile:
    def __init__(self, planes, columns, halo):
        self.shape = (planes, columns)
        self.planes, self.columns, self.halo = planes, columns, halo
        self.lane = lax.broadcasted_iota(jnp.int32, self.shape, 1)
        sub = lax.broadcasted_iota(jnp.int32, self.shape, 0)
        self.first, self.last = self.lane == 0, self.lane == columns - 1
        self.bottom, self.top = sub == 0, sub == planes - 1
        self.zero = jnp.zeros(self.shape, jnp.float32)

    def dy(self, w):
        a, b = roll(w.m, -1, 1), roll(w.h, -1, 1)
        c, d = roll(w.m, 1, 1), roll(w.h, 1, 1)
        return W(
            jnp.where(self.last, b, a) - jnp.where(self.first, d, c),
            jnp.where(self.last, a, b) - jnp.where(self.first, c, d),
        )

    def dz1(self, a):
        return jnp.where(self.top, 0.0, roll(a, -1, 0)) - jnp.where(self.bottom, 0.0, roll(a, 1, 0))

    def dz(self, w):
        return W(self.dz1(w.m), self.dz1(w.h))

    def pack(self, tiles):
        width = 2 * self.halo
        group = self.lane // width
        out = []
        per = self.columns // width
        for base in range(0, len(tiles), per):
            total = self.zero
            for j, tile in enumerate(tiles[base : base + per]):
                total = jnp.where(group == j, roll(tile, self.halo + width * j, 1), total)
            out.append(total)
        return out

    def unpack(self, tiles, index):
        width = 2 * self.halo
        per = self.columns // width
        return roll(tiles[index // per], -(self.halo + width * (index % per)), 1)


def dx(get, name, r, low=True, high=True):
    if low and high:
        return get(name, r + 1) - get(name, r - 1)
    return get(name, r + 1) if high else -get(name, r - 1)


def read(ref, *at):
    planes = ref.shape[-2] // 2
    return W(ref[(*at, pl.ds(0, planes))], ref[(*at, pl.ds(planes, planes))])


def write(ref, value, *at):
    planes = ref.shape[-2] // 2
    ref[(*at, pl.ds(0, planes))] = value.m
    ref[(*at, pl.ds(planes, planes))] = value.h


def memo(fn):
    return functools.lru_cache(maxsize=None)(fn)


def momentum(tile, s, r, low=True, high=True):
    forces = [
        dx(s, XX, r, low, high) + tile.dy(s(XY, r)) + tile.dz(s(XZ, r)),
        dx(s, XY, r, low, high) + tile.dy(s(YY, r)) + tile.dz(s(YZ, r)),
        dx(s, XZ, r, low, high) + tile.dy(s(YZ, r)) + tile.dz(s(ZZ, r)),
    ]
    slopes = [dx(s, PP, r, low, high), tile.dy(s(PP, r)), tile.dz(s(PP, r))]
    return forces, slopes


def forward_edge(tile, s, v, p, r, low, high):
    forces, slopes = momentum(tile, s, r, low, high)
    h, k, m = p(PH, r), p(PK, r), p(PM, r)
    out = []
    for i in range(3):
        g = -(slopes[i] + m * v(WX + i, r))
        out.append(v(VX + i, r) + h * (3.0 * forces[i] - g))
        if i == 0:
            drive = v(WX, r) + h * (k * g - forces[0])
    return [s(XX, r), s(XY, r), s(XZ, r), s(PP, r)] + out + [drive]


def adjoint_stress(p, a, r):
    trace = a(XX, r) + a(YY, r) + a(ZZ, r)
    b, pi = p(PB, r), a(PP, r)
    cross = p(PA, r) * b
    common = p(PL, r) * trace - cross * pi
    s = p(PS, r)
    s2 = 2.0 * s
    return {
        XX: common + s2 * a(XX, r),
        YY: common + s2 * a(YY, r),
        ZZ: common + s2 * a(ZZ, r),
        YZ: s * a(YZ, r),
        XZ: s * a(XZ, r),
        XY: s * a(XY, r),
        PP: cross * trace - b * pi,
    }


def adjoint_edge(tile, q, a, p, r, low, high):
    forces, slopes = momentum(tile, q, r, low, high)
    h, k = p(PH, r), p(PK, r)
    out = []
    for i in range(3):
        lv, lw = a(VX + i, r) - forces[i], a(WX + i, r) - slopes[i]
        out.append(h * (3.0 * lv - lw))
        if i == 0:
            drive = h * (k * lw - lv)
    return [q(XX, r), q(XY, r), q(XZ, r), q(PP, r)] + out + [drive]


def send(tile, even, first_rows, last_rows, a_ref, b_ref):
    ups = [w.m for w in first_rows] + tile.pack([w.h for w in first_rows])
    downs = [w.m for w in last_rows] + tile.pack([w.h for w in last_rows])
    for n, (up, down) in enumerate(zip(ups, downs)):
        a_ref[n] = jnp.where(even, down, up)
        b_ref[n] = jnp.where(even, up, down)


def receive(tile, axis, a_ref, b_ref, count):
    total = a_ref.shape[0]
    at = lax.axis_index(axis)
    even = lax.rem(at, 2) == 0
    before, after = at > 0, at < lax.axis_size(axis) - 1
    first = [jnp.where(before, jnp.where(even, b_ref[n], a_ref[n]), 0.0) for n in range(total)]
    last = [jnp.where(after, jnp.where(even, a_ref[n], b_ref[n]), 0.0) for n in range(total)]
    sides = []
    for got in (first, last):
        sides.append([W(got[n], tile.unpack(got[count:], n)) for n in range(count)])
    return sides


def start_kernel(halo, my_axis, inputs, outs, scratch):
    par_hbm, (mask_hbm, index_hbm, table_hbm), rest_hbm = inputs[:7], inputs[7:10], inputs[10:]
    p_ref, a_ref, b_ref, *rest = outs
    par_ref, mask_ref, index_ref, table_ref, sems = scratch
    fields_ref, cot_ref = rest[:2]
    copies = [pltpu.make_async_copy(src, par_ref.at[n], sems.at[n]) for n, src in enumerate(par_hbm)]
    for src, dst in zip((table_hbm, mask_hbm, index_hbm, *rest_hbm), (table_ref, mask_ref, index_ref, *rest)):
        copies.append(pltpu.make_async_copy(src, dst, sems.at[len(copies)]))
    for copy in copies:
        copy.start()
    for copy in copies[:10]:
        copy.wait()

    even = lax.rem(lax.axis_index(my_axis), 2) == 0
    rows = p_ref.shape[1]
    planes, columns = p_ref.shape[2], p_ref.shape[3]
    lane = lax.broadcasted_iota(jnp.int32, (planes, columns), 1)
    group = lane // halo
    per = columns // halo

    def at(r):
        return pl.ds(r, planes, stride=rows)

    for r in range(rows):
        density, fluid, mobility, lame, shear, modulus, coupling = [par_ref[n, 0, at(r), :] for n in range(7)]
        lookup = jnp.zeros((planes, columns), jnp.float32)
        index = index_ref[0, at(r), :]
        for n in range(table_ref.shape[1]):
            lookup = jnp.where(index == n, table_ref[0, n], lookup)
        p_ref[PH, r] = 0.25 / (3.0 * density - fluid)
        p_ref[PK, r] = density / fluid
        p_ref[PM, r] = 2.0 * mobility
        p_ref[PL, r] = 0.25 * lame
        p_ref[PS, r] = 0.25 * shear
        p_ref[PB, r] = 0.25 * modulus
        p_ref[PA, r] = coupling
        p_ref[PF, r] = 1.0 - mask_ref[0, at(r), :].astype(jnp.float32) * lookup
    sources = []
    for f in range(p_ref.shape[0]):
        for r in range(rows):
            sources.append(lambda f=f, r=r: p_ref[f, r])
    for ref in (fields_ref, cot_ref):
        for f in range(ref.shape[0]):
            for r in range(rows):
                sources.append(lambda ref=ref, f=f, r=r: ref[f, at(r), :])
    waited = False
    for n in range(a_ref.shape[0]):
        if (n + 1) * per > p_ref.shape[0] * rows and not waited:
            for copy in copies[10:]:
                copy.wait()
            waited = True
        left = jnp.zeros((planes, columns), jnp.float32)
        right = left
        for g in range(per):
            if n * per + g < len(sources):
                x = sources[n * per + g]()
                left = jnp.where(group == g, roll(x, halo * g, 1), left)
                right = jnp.where(group == g, roll(x, halo * g + halo, 1), right)
        a_ref[n] = jnp.where(even, right, left)
        b_ref[n] = jnp.where(even, left, right)


def inject_kernel(halo, gx_axis, gy_axis, rec_ref, cot_ref, src_ref, amp_ref, rec_out, src_out):
    for cells_ref, amounts_ref, out in ((rec_ref, cot_ref, rec_out), (src_ref, amp_ref, src_out)):
        steps, rows, planes2, columns = out.shape
        planes = planes2 // 2
        count = amounts_ref.shape[1]
        total_x, total_y = rows * lax.axis_size(gx_axis), columns * lax.axis_size(gy_axis)
        cells = cells_ref[...]
        line = lax.div(cells, jnp.full_like(cells, total_y))
        depth = lax.div(line, jnp.full_like(cells, total_x))
        col = cells - line * total_y - lax.axis_index(gy_axis) * columns
        x = line - depth * total_x - lax.axis_index(gx_axis) * rows
        row = jnp.where((x >= 0) & (x < rows), x * planes + depth, -1)
        row_at = lax.broadcasted_iota(jnp.int32, (rows * planes, count), 0)
        here = row_at == row
        lhs = jnp.concatenate([jnp.where(here, amounts_ref[t : t + 1, :], 0.0) for t in range(steps)], axis=0)
        lane = lax.broadcasted_iota(jnp.int32, (columns, count), 0)
        side = jnp.where(lane < halo, lane + columns, jnp.where(lane >= columns - halo, lane - columns, -columns))
        for half, where in enumerate((lane, side)):
            rhs = (where == col).astype(jnp.float32)
            got = lax.dot_general(
                lhs, rhs, (((1,), (1,)), ((), ())), precision=lax.Precision.HIGHEST, preferred_element_type=jnp.float32
            )
            for t in range(steps):
                for r in range(rows):
                    base = (t * rows + r) * planes
                    out[t, r, pl.ds(half * planes, planes)] = got[base : base + planes]


def spread_kernel(halo, gx_axis, gy_axis, fields_ref, cot_ref, pm_ref, ay_ref, by_ref, rec_ref,
                  f_out, a_out, p_out, a_msg, b_msg):
    even_x = lax.rem(lax.axis_index(gx_axis), 2) == 0
    even_y = lax.rem(lax.axis_index(gy_axis), 2) == 0
    rows, planes, columns = pm_ref.shape[1:]
    tile = Tile(planes, columns, halo)
    per = columns // halo
    packs = ay_ref.shape[0]
    right = [jnp.where(even_y, ay_ref[n], by_ref[n]) for n in range(packs)]
    left = [jnp.where(even_y, by_ref[n], ay_ref[n]) for n in range(packs)]
    at_y = lax.axis_index(gy_axis)
    on_right = (tile.lane < halo) & (at_y < lax.axis_size(gy_axis) - 1)
    on_left = (tile.lane >= columns - halo) & (at_y > 0)

    def side(n):
        g = n % per
        a = roll(right[n // per], -halo * g, 1)
        b = roll(left[n // per], columns - halo - halo * g, 1)
        return jnp.where(on_right, a, jnp.where(on_left, b, 0.0))

    def at(r):
        return pl.ds(r, planes, stride=rows)

    count, base = fields_ref.shape[0], p_out.shape[0]
    for f in range(p_out.shape[0]):
        for r in range(rows):
            write(p_out, W(pm_ref[f, r], side(f * rows + r)), f, r)
    for f in range(count):
        for r in range(rows):
            write(f_out, W(fields_ref[f, at(r), :], side((base + f) * rows + r)), f, r)
            value = W(cot_ref[f, at(r), :], side((base + count + f) * rows + r))
            if f == PP:
                value = value + read(rec_ref, rec_ref.shape[0] - 1, r)
            write(a_out, value * read(p_out, PF, r), f, r)
    messages(tile, even_x, f_out, a_out, p_out, a_msg, b_msg, True)


def messages(tile, even, f_ref, a_ref, p_ref, a_msg, b_msg, with_params):
    rows = f_ref.shape[1]
    s = lambda f, r: read(f_ref, f, r)
    a = lambda f, r: read(a_ref, f, r)
    p = lambda f, r: read(p_ref, f, r)
    qs = memo(lambda r: adjoint_stress(p, a, r))
    q = lambda f, r: qs(r)[f]
    sides = []
    for r, low, high in ((0, False, True), (rows - 1, True, False)):
        got = forward_edge(tile, s, s, p, r, low, high) + adjoint_edge(tile, q, a, p, r, low, high)
        if with_params:
            got += [p(PH, r), p(PK, r)]
        sides.append(got)
    send(tile, even, *sides, a_msg, b_msg)


def step_kernel(gx_axis, halo, j, steps, *refs):
    refs = list(refs)
    take = lambda n: [refs.pop(0) for _ in range(n)]
    f_ref, a_ref, p_ref, am_ref, bm_ref = take(5)
    first, final = j == 0, j == steps - 1
    keep_f, keep_a = j < steps - 1 - j, j < steps - 1 - j
    hk_ref = None if first else take(1)[0]
    src_ref = rec_ref = None
    if not final:
        src_ref, rec_ref = take(2)
    old_f_ref = old_a_ref = acc_ref = None
    if not keep_f:
        old_f_ref, old_a_ref = take(2)
        if j - 1 >= steps - j:
            acc_ref = take(1)[0]
    if final:
        grad_out, par_out = take(2)
        f_out = a_out = None
    else:
        f_out, a_out, a_msg, b_msg = take(4)
    hk_out = take(1)[0] if first else None
    save_f = save_a = acc_out = None
    if keep_f:
        save_f, save_a = take(2)
    elif not final:
        acc_out = take(1)[0]
    assert not refs

    even = lax.rem(lax.axis_index(gx_axis), 2) == 0
    rows, planes, columns = f_ref.shape[1], f_ref.shape[2] // 2, f_ref.shape[3]
    tile = Tile(planes, columns, halo)
    sides = receive(tile, gx_axis, am_ref, bm_ref, 2 * EDGE + (2 if first else 0))
    p = lambda f, r: read(p_ref, f, r)
    old = lambda f, r: read(f_ref, f, r)
    lam = lambda f, r: read(a_ref, f, r)
    hk = []
    for n in range(2):
        if first:
            pair = sides[n][2 * EDGE : 2 * EDGE + 2]
            for m in range(2):
                write(hk_out, pair[m], n, m)
        else:
            pair = [read(hk_ref, n, m) for m in range(2)]
        hk.append(pair)
    slot = {XX: 0, XY: 1, XZ: 2, PP: 3}

    def end(r):
        return 0 if r < 0 else 1

    def s(f, r):
        return old(f, r) if 0 <= r < rows else sides[end(r)][slot[f]]

    @memo
    def velocity(r):
        if 0 <= r < rows:
            forces, slopes = momentum(tile, s, r)
            h, k, m = p(PH, r), p(PK, r), p(PM, r)
            out, pushes = {}, []
            for i in range(3):
                w = old(WX + i, r)
                g = -(slopes[i] + m * w)
                pushes.append(g)
                out[VX + i] = old(VX + i, r) + h * (3.0 * forces[i] - g)
                out[WX + i] = w + h * (k * g - forces[i])
            return out, forces, pushes
        n = end(r)
        got = sides[n][4:8]
        edge = 0 if n == 0 else rows - 1
        h, k = hk[n]
        t = h if n == 0 else -h
        xx, pp = t * old(XX, edge), t * old(PP, edge)
        return {
            VX: got[0] + (3.0 * xx + pp),
            VY: got[1] + 3.0 * (t * old(XY, edge)),
            VZ: got[2] + 3.0 * (t * old(XZ, edge)),
            WX: got[3] - (k * pp + xx),
        }, None, None

    v = lambda f, r: velocity(r)[0][f]

    def strain(r):
        e = [dx(v, VX, r), tile.dy(v(VY, r)), tile.dz(v(VZ, r))]
        g = [
            tile.dz(v(VY, r)) + tile.dy(v(VZ, r)),
            tile.dz(v(VX, r)) + dx(v, VZ, r),
            tile.dy(v(VX, r)) + dx(v, VY, r),
        ]
        dw = dx(v, WX, r) + tile.dy(v(WY, r)) + tile.dz(v(WZ, r))
        return e, g, dw

    qs = memo(lambda r: adjoint_stress(p, lam, r))

    def q(f, r):
        return qs(r)[f] if 0 <= r < rows else sides[end(r)][EDGE + slot[f]]

    @memo
    def cots(r):
        if 0 <= r < rows:
            forces, slopes = momentum(tile, q, r)
            h, k = p(PH, r), p(PK, r)
            cf, cg, vel = [], [], {}
            for i in range(3):
                lv, lw = lam(VX + i, r) - forces[i], lam(WX + i, r) - slopes[i]
                cf.append(h * (3.0 * lv - lw))
                cg.append(h * (k * lw - lv))
                vel[VX + i] = lv
                vel[WX + i] = lw - p(PM, r) * cg[i]
            return cf, cg, vel
        n = end(r)
        got = sides[n][EDGE + 4 : EDGE + 8]
        edge = 0 if n == 0 else rows - 1
        h, k = hk[n]
        t = -h if n == 0 else h
        xx, pp = t * q(XX, edge), t * q(PP, edge)
        return [
            got[0] + (3.0 * xx - pp),
            got[1] + 3.0 * (t * q(XY, edge)),
            got[2] + 3.0 * (t * q(XZ, edge)),
        ], [got[3] + (k * pp - xx)], None

    cF = lambda i, r: cots(r)[0][i]
    cG = lambda i, r: cots(r)[1][i]

    def adjoint_row(r):
        out = dict(cots(r)[2])
        out[XX] = lam(XX, r) - dx(cF, 0, r)
        out[YY] = lam(YY, r) - tile.dy(cF(1, r))
        out[ZZ] = lam(ZZ, r) - tile.dz(cF(2, r))
        out[YZ] = lam(YZ, r) - (tile.dz(cF(1, r)) + tile.dy(cF(2, r)))
        out[XZ] = lam(XZ, r) - (tile.dz(cF(0, r)) + dx(cF, 2, r))
        out[XY] = lam(XY, r) - (tile.dy(cF(0, r)) + dx(cF, 1, r))
        out[PP] = lam(PP, r) + (dx(cG, 0, r) + tile.dy(cG(1, r)) + tile.dz(cG(2, r)))
        return out

    stress_names = (XX, YY, ZZ, YZ, XZ, XY, PP)
    for r in range(rows):
        e, g, dw = strain(r)
        dv = e[0] + e[1] + e[2]
        new, forces, pushes = velocity(r)
        here_f = [x.m for x in forces + pushes] + [old(WX + i, r).m for i in range(3)]
        here_f += [x.m for x in e + g] + [dw.m]
        if not final:
            new = dict(new)
            sh, b = p(PS, r), p(PB, r)
            ab = p(PA, r) * b
            common = p(PL, r) * dv + ab * dw
            for i in range(3):
                new[XX + i] = old(XX + i, r) + (common + 2.0 * (sh * e[i]))
                new[YZ + i] = old(YZ + i, r) + sh * g[i]
            new[PP] = old(PP, r) - (ab * dv + b * dw) + read(src_ref, j, r)
            factor = p(PF, r)
            for f, value in new.items():
                write(f_out, value * factor, f, r)
        back = adjoint_row(r)
        cf, cg = cots(r)[0], cots(r)[1]
        here_a = [x.m for x in cf + cg] + [lam(f, r).m for f in stress_names]
        if final:
            for f, value in back.items():
                grad_out[f, pl.ds(r, planes, stride=rows), :] = value.m
        else:
            back[PP] = back[PP] + read(rec_ref, steps - 2 - j, r)
            for f, value in back.items():
                write(a_out, value * p(PF, r), f, r)
        if keep_f:
            for n, x in enumerate(here_f):
                save_f[n, r] = x
            for n, x in enumerate(here_a):
                save_a[n, r] = x
            continue
        acc = [0.0] * 9 if acc_ref is None else [acc_ref[n, r] for n in range(9)]
        pairs = [(here_f, [old_a_ref[n, r] for n in range(13)])]
        if 2 * j != steps - 1:
            pairs.append(([old_f_ref[n, r] for n in range(16)], here_a))
        for ff, aa in pairs:
            fo, pu, wo, ee, gg, w_ = ff[0:3], ff[3:6], ff[6:9], ff[9:12], ff[12:15], ff[15]
            af, ag, sg, pi = aa[0:3], aa[3:6], aa[6:12], aa[12]
            tr, dd = sg[0] + sg[1] + sg[2], ee[0] + ee[1] + ee[2]
            dot = lambda x, y: x[0] * y[0] + x[1] * y[1] + x[2] * y[2]
            adds = [
                dot(af, fo), dot(ag, pu), dot(af, pu), dot(ag, wo),
                tr * dd, tr * w_, 2.0 * dot(sg[0:3], ee) + dot(sg[3:6], gg), pi * dd, pi * w_,
            ]
            acc = [x + y for x, y in zip(acc, adds)]
        if not final:
            for n, x in enumerate(acc):
                acc_out[n, r] = x
            continue
        a1, a2, a3, a4, b1, b2, b3, b4, b5 = acc
        h4, k, b, al = 4.0 * p_ref[PH, r, pl.ds(0, planes)], p_ref[PK, r, pl.ds(0, planes)], p_ref[PB, r, pl.ds(0, planes)], p_ref[PA, r, pl.ds(0, planes)]
        grads = [
            h4 * (a3 - 3.0 * a1),
            h4 * (a1 + a2 - k * (3.0 * a2 + a3)),
            -2.0 * a4,
            0.25 * b1,
            0.25 * b3,
            0.25 * (al * (b2 - b4) - b5),
            b * (b2 - b4),
        ]
        for n, x in enumerate(grads):
            par_out[n, pl.ds(r, planes, stride=rows), :] = x
    if not final:
        messages(tile, even, f_out, a_out, p_ref, a_msg, b_msg, False)


def swaps(axis, odd):
    nx, ny = lax.axis_size("gx"), lax.axis_size("gy")
    count, other = (nx, ny) if axis == "gx" else (ny, nx)
    place = (lambda i, k: i * ny + k) if axis == "gx" else (lambda i, k: k * ny + i)
    out, met = [], set()
    for i in range(odd, count - 1, 2):
        met |= {i, i + 1}
        for k in range(other):
            out += [(place(i, k), place(i + 1, k)), (place(i + 1, k), place(i, k))]
    for i in set(range(count)) - met:
        for k in range(0, other - 1, 2):
            out += [(place(i, k), place(i, k + 1)), (place(i, k + 1), place(i, k))]
    return sorted(out)


def exchange(axis, a, b):
    mesh = ("gx", "gy")
    b = lax.ppermute(b, mesh, swaps(axis, 1))
    a = lax.ppermute(a, mesh, swaps(axis, 0))
    return a, b


def call(kernel, outs, *args):
    shapes = [o if isinstance(o, jax.ShapeDtypeStruct) else jax.ShapeDtypeStruct(o, jnp.float32) for o in outs]
    return pl.pallas_call(
        kernel,
        out_shape=shapes,
        in_specs=[pl.BlockSpec(memory_space=pltpu.VMEM)] * len(args),
        out_specs=[pl.BlockSpec(memory_space=pltpu.VMEM)] * len(outs),
        compiler_params=pltpu.CompilerParams(vmem_limit_bytes=48 << 20),
    )(*args)


def per_device(
    fields, density, fluid_density, mobility, lame_lambda, shear_modulus, biot_modulus, biot_coef,
    region_mask, profile_index, profile_table, source_cells, source_amp, receiver_cells, field_cot, receiver_cot,
):
    planes, rows, columns = region_mask.shape
    steps = source_amp.shape[0]
    count = fields.shape[0]
    halo = 2 * steps
    assert steps % 2 == 0 and planes == 8 and columns == 128 and columns % (2 * halo) == 0 and rows > 1
    flat = lambda x: x.reshape(-1, planes * rows, columns)
    fields, field_cot = flat(fields), flat(field_cot)
    raw = [flat(x) for x in (density, fluid_density, mobility, lame_lambda, shear_modulus, biot_modulus, biot_coef)]
    packs = -(-(2 * count + 8) * rows * halo // columns)
    own, wide = (rows, planes, columns), (rows, 2 * planes, columns)

    table = profile_table[None]
    small = [receiver_cells[None], receiver_cot, source_cells[None], source_amp]
    inputs = [*raw, table, flat(region_mask), flat(profile_index), fields, field_cot, *small]
    whole = [fields, field_cot, *small]
    plane = (planes * rows, columns)

    def start(*refs):
        refs = list(refs)
        hbm = refs[:7] + refs[8:10] + refs[7:8] + refs[10:16]
        start_kernel(halo, "gy", hbm, refs[16:25], refs[25:])

    p_own, ay, by, fields, field_cot, *small = pl.pallas_call(
        start,
        out_shape=[jax.ShapeDtypeStruct(s, jnp.float32) for s in [(8, *own)] + [(packs, planes, columns)] * 2]
        + [jax.ShapeDtypeStruct(x.shape, x.dtype) for x in whole],
        in_specs=[pl.BlockSpec(memory_space=pltpu.HBM)] * 16,
        out_specs=[pl.BlockSpec(memory_space=pltpu.VMEM)] * 9,
        scratch_shapes=[
            pltpu.VMEM((7, 1, *plane), jnp.float32), pltpu.VMEM((1, *plane), jnp.int32),
            pltpu.VMEM((1, *plane), jnp.int32), pltpu.SMEM(table.shape, jnp.float32),
            pltpu.SemaphoreType.DMA((16,)),
        ],
        compiler_params=pltpu.CompilerParams(vmem_limit_bytes=48 << 20),
    )(*[pltpu.with_memory_space_constraint(x, pltpu.HBM) for x in inputs])
    ay, by = exchange("gy", ay, by)
    rec, src = call(functools.partial(inject_kernel, halo, "gx", "gy"), [(steps, *wide)] * 2, *small)
    tiles = lambda n: n + -(-n * 2 * halo // columns)
    f, a, p, am, bm = call(
        functools.partial(spread_kernel, halo, "gx", "gy"),
        [(count, *wide)] * 2 + [(8, *wide)] + [(tiles(2 * EDGE + 2), planes, columns)] * 2,
        fields, field_cot, p_own, ay, by, rec,
    )
    saved, hk, acc = [], None, None
    for j in range(steps):
        am, bm = exchange("gx", am, bm)
        args, outs = [f, a, p, am, bm], []
        final, keep = j == steps - 1, j < steps - 1 - j
        if j:
            args.append(hk)
        if not final:
            args += [src, rec]
            outs += [(count, *wide)] * 2 + [(tiles(2 * EDGE), planes, columns)] * 2
        else:
            outs += [(count, planes * rows, columns), (7, planes * rows, columns)]
        if j == 0:
            outs.append((2, 2, 2 * planes, columns))
        if keep:
            outs += [(16, *own), (13, *own)]
        else:
            args += saved[steps - 1 - j]
            if acc is not None:
                args.append(acc)
            if not final:
                outs.append((9, *own))
        got = list(call(functools.partial(step_kernel, "gx", halo, j, steps), outs, *args))
        if final:
            return got[0].reshape(count, planes, rows, columns), got[1].reshape(7, planes, rows, columns)
        f, a, am, bm = got[:4]
        got = got[4:]
        if j == 0:
            hk = got.pop(0)
        if keep:
            saved.append(got)
        else:
            saved.append(None)
            acc = got[0]


def solution(mesh):
    plane, field = P(None, "gx", "gy"), P(None, None, "gx", "gy")
    in_specs = (field,) + (plane,) * 9 + (P(),) * 4 + (field, P())
    return jax.shard_map(per_device, mesh=mesh, in_specs=in_specs, out_specs=(field, field), check_vma=False)
```

```python
import functools

import jax
import jax.numpy as jnp
from jax import lax
from jax.experimental import pallas as pl
from jax.experimental.pallas import tpu as pltpu
from jax.sharding import PartitionSpec as P


VX, VY, VZ, WX, WY, WZ, XX, YY, ZZ, YZ, XZ, XY, PP = range(13)
PH, PK, PM, PL, PS, PB, PA, PF = range(8)
EDGE = 8


class W:
    __slots__ = ("m", "h")

    def __init__(self, m, h):
        self.m, self.h = m, h

    def __add__(self, o):
        return W(self.m + o.m, self.h + o.h)

    def __sub__(self, o):
        return W(self.m - o.m, self.h - o.h)

    def __mul__(self, o):
        if isinstance(o, W):
            return W(self.m * o.m, self.h * o.h)
        return W(self.m * o, self.h * o)

    __rmul__ = __mul__

    def __neg__(self):
        return W(-self.m, -self.h)


def roll(x, shift, axis):
    shift %= x.shape[axis]
    return pltpu.roll(x, shift, axis) if shift else x


class Tile:
    def __init__(self, planes, columns, halo):
        self.shape = (planes, columns)
        self.planes, self.columns, self.halo = planes, columns, halo
        self.lane = lax.broadcasted_iota(jnp.int32, self.shape, 1)
        sub = lax.broadcasted_iota(jnp.int32, self.shape, 0)
        self.first, self.last = self.lane == 0, self.lane == columns - 1
        self.bottom, self.top = sub == 0, sub == planes - 1
        self.zero = jnp.zeros(self.shape, jnp.float32)

    def dy(self, w):
        a, b = roll(w.m, -1, 1), roll(w.h, -1, 1)
        c, d = roll(w.m, 1, 1), roll(w.h, 1, 1)
        return W(
            jnp.where(self.last, b, a) - jnp.where(self.first, d, c),
            jnp.where(self.last, a, b) - jnp.where(self.first, c, d),
        )

    def dz1(self, a):
        return jnp.where(self.top, 0.0, roll(a, -1, 0)) - jnp.where(self.bottom, 0.0, roll(a, 1, 0))

    def dz(self, w):
        return W(self.dz1(w.m), self.dz1(w.h))

    def pack(self, tiles):
        width = 2 * self.halo
        group = self.lane // width
        out = []
        per = self.columns // width
        for base in range(0, len(tiles), per):
            total = self.zero
            for j, tile in enumerate(tiles[base : base + per]):
                total = jnp.where(group == j, roll(tile, self.halo + width * j, 1), total)
            out.append(total)
        return out

    def unpack(self, tiles, index):
        width = 2 * self.halo
        per = self.columns // width
        return roll(tiles[index // per], -(self.halo + width * (index % per)), 1)


def dx(get, name, r, low=True, high=True):
    if low and high:
        return get(name, r + 1) - get(name, r - 1)
    return get(name, r + 1) if high else -get(name, r - 1)


def read(ref, *at):
    planes = ref.shape[-2] // 2
    return W(ref[(*at, pl.ds(0, planes))], ref[(*at, pl.ds(planes, planes))])


def write(ref, value, *at):
    planes = ref.shape[-2] // 2
    ref[(*at, pl.ds(0, planes))] = value.m
    ref[(*at, pl.ds(planes, planes))] = value.h


def memo(fn):
    return functools.lru_cache(maxsize=None)(fn)


def momentum(tile, s, r, low=True, high=True):
    forces = [
        dx(s, XX, r, low, high) + tile.dy(s(XY, r)) + tile.dz(s(XZ, r)),
        dx(s, XY, r, low, high) + tile.dy(s(YY, r)) + tile.dz(s(YZ, r)),
        dx(s, XZ, r, low, high) + tile.dy(s(YZ, r)) + tile.dz(s(ZZ, r)),
    ]
    slopes = [dx(s, PP, r, low, high), tile.dy(s(PP, r)), tile.dz(s(PP, r))]
    return forces, slopes


def forward_edge(tile, s, v, p, r, low, high):
    forces, slopes = momentum(tile, s, r, low, high)
    h, k, m = p(PH, r), p(PK, r), p(PM, r)
    out = []
    for i in range(3):
        g = -(slopes[i] + m * v(WX + i, r))
        out.append(v(VX + i, r) + h * (3.0 * forces[i] - g))
        if i == 0:
            drive = v(WX, r) + h * (k * g - forces[0])
    return [s(XX, r), s(XY, r), s(XZ, r), s(PP, r)] + out + [drive]


def adjoint_stress(p, a, r):
    trace = a(XX, r) + a(YY, r) + a(ZZ, r)
    b, pi = p(PB, r), a(PP, r)
    cross = p(PA, r) * b
    common = p(PL, r) * trace - cross * pi
    s = p(PS, r)
    s2 = 2.0 * s
    return {
        XX: common + s2 * a(XX, r),
        YY: common + s2 * a(YY, r),
        ZZ: common + s2 * a(ZZ, r),
        YZ: s * a(YZ, r),
        XZ: s * a(XZ, r),
        XY: s * a(XY, r),
        PP: cross * trace - b * pi,
    }


def adjoint_edge(tile, q, a, p, r, low, high):
    forces, slopes = momentum(tile, q, r, low, high)
    h, k = p(PH, r), p(PK, r)
    out = []
    for i in range(3):
        lv, lw = a(VX + i, r) - forces[i], a(WX + i, r) - slopes[i]
        out.append(h * (3.0 * lv - lw))
        if i == 0:
            drive = h * (k * lw - lv)
    return [q(XX, r), q(XY, r), q(XZ, r), q(PP, r)] + out + [drive]


def send(tile, even, first_rows, last_rows, a_ref, b_ref):
    ups = [w.m for w in first_rows] + tile.pack([w.h for w in first_rows])
    downs = [w.m for w in last_rows] + tile.pack([w.h for w in last_rows])
    for n, (up, down) in enumerate(zip(ups, downs)):
        a_ref[n] = jnp.where(even, down, up)
        b_ref[n] = jnp.where(even, up, down)


def receive(tile, axis, a_ref, b_ref, count):
    total = a_ref.shape[0]
    at = lax.axis_index(axis)
    even = lax.rem(at, 2) == 0
    before, after = at > 0, at < lax.axis_size(axis) - 1
    first = [jnp.where(before, jnp.where(even, b_ref[n], a_ref[n]), 0.0) for n in range(total)]
    last = [jnp.where(after, jnp.where(even, a_ref[n], b_ref[n]), 0.0) for n in range(total)]
    sides = []
    for got in (first, last):
        sides.append([W(got[n], tile.unpack(got[count:], n)) for n in range(count)])
    return sides


def start_kernel(halo, my_axis, inputs, outs, scratch):
    par_hbm, (mask_hbm, index_hbm, table_hbm), rest_hbm = inputs[:7], inputs[7:10], inputs[10:]
    p_ref, a_ref, b_ref, *rest = outs
    par_ref, mask_ref, index_ref, table_ref, sems = scratch
    fields_ref, cot_ref = rest[:2]
    copies = [pltpu.make_async_copy(src, par_ref.at[n], sems.at[n]) for n, src in enumerate(par_hbm)]
    for src, dst in zip((table_hbm, mask_hbm, index_hbm, *rest_hbm), (table_ref, mask_ref, index_ref, *rest)):
        copies.append(pltpu.make_async_copy(src, dst, sems.at[len(copies)]))
    for copy in copies:
        copy.start()
    for copy in copies[:10]:
        copy.wait()

    even = lax.rem(lax.axis_index(my_axis), 2) == 0
    rows = p_ref.shape[1]
    planes, columns = p_ref.shape[2], p_ref.shape[3]
    lane = lax.broadcasted_iota(jnp.int32, (planes, columns), 1)
    group = lane // halo
    per = columns // halo

    def at(r):
        return pl.ds(r, planes, stride=rows)

    for r in range(rows):
        density, fluid, mobility, lame, shear, modulus, coupling = [par_ref[n, 0, at(r), :] for n in range(7)]
        lookup = jnp.zeros((planes, columns), jnp.float32)
        index = index_ref[0, at(r), :]
        for n in range(table_ref.shape[1]):
            lookup = jnp.where(index == n, table_ref[0, n], lookup)
        p_ref[PH, r] = 0.25 / (3.0 * density - fluid)
        p_ref[PK, r] = density / fluid
        p_ref[PM, r] = 2.0 * mobility
        p_ref[PL, r] = 0.25 * lame
        p_ref[PS, r] = 0.25 * shear
        p_ref[PB, r] = 0.25 * modulus
        p_ref[PA, r] = coupling
        p_ref[PF, r] = 1.0 - mask_ref[0, at(r), :].astype(jnp.float32) * lookup
    sources = []
    for f in range(p_ref.shape[0]):
        for r in range(rows):
            sources.append(lambda f=f, r=r: p_ref[f, r])
    for ref in (fields_ref, cot_ref):
        for f in range(ref.shape[0]):
            for r in range(rows):
                sources.append(lambda ref=ref, f=f, r=r: ref[f, at(r), :])
    waited = False
    for n in range(a_ref.shape[0]):
        if (n + 1) * per > p_ref.shape[0] * rows and not waited:
            for copy in copies[10:]:
                copy.wait()
            waited = True
        left = jnp.zeros((planes, columns), jnp.float32)
        right = left
        for g in range(per):
            if n * per + g < len(sources):
                x = sources[n * per + g]()
                left = jnp.where(group == g, roll(x, halo * g, 1), left)
                right = jnp.where(group == g, roll(x, halo * g + halo, 1), right)
        a_ref[n] = jnp.where(even, right, left)
        b_ref[n] = jnp.where(even, left, right)


def inject_kernel(halo, gx_axis, gy_axis, rec_ref, cot_ref, src_ref, amp_ref, rec_out, src_out):
    for cells_ref, amounts_ref, out in ((rec_ref, cot_ref, rec_out), (src_ref, amp_ref, src_out)):
        steps, rows, planes2, columns = out.shape
        planes = planes2 // 2
        count = amounts_ref.shape[1]
        total_x, total_y = rows * lax.axis_size(gx_axis), columns * lax.axis_size(gy_axis)
        cells = cells_ref[...]
        line = lax.div(cells, jnp.full_like(cells, total_y))
        depth = lax.div(line, jnp.full_like(cells, total_x))
        col = cells - line * total_y - lax.axis_index(gy_axis) * columns
        x = line - depth * total_x - lax.axis_index(gx_axis) * rows
        row = jnp.where((x >= 0) & (x < rows), x * planes + depth, -1)
        row_at = lax.broadcasted_iota(jnp.int32, (rows * planes, count), 0)
        here = row_at == row
        lhs = jnp.concatenate([jnp.where(here, amounts_ref[t : t + 1, :], 0.0) for t in range(steps)], axis=0)
        lane = lax.broadcasted_iota(jnp.int32, (columns, count), 0)
        side = jnp.where(lane < halo, lane + columns, jnp.where(lane >= columns - halo, lane - columns, -columns))
        for half, where in enumerate((lane, side)):
            rhs = (where == col).astype(jnp.float32)
            got = lax.dot_general(
                lhs, rhs, (((1,), (1,)), ((), ())), precision=lax.Precision.HIGHEST, preferred_element_type=jnp.float32
            )
            for t in range(steps):
                for r in range(rows):
                    base = (t * rows + r) * planes
                    out[t, r, pl.ds(half * planes, planes)] = got[base : base + planes]


def spreader(halo, gy_axis, ay_ref, by_ref, rows, tile):
    at_y = lax.axis_index(gy_axis)
    even_y = lax.rem(at_y, 2) == 0
    columns = tile.columns
    per = columns // halo
    on_right = (tile.lane < halo) & (at_y < lax.axis_size(gy_axis) - 1)
    on_left = (tile.lane >= columns - halo) & (at_y > 0)

    @memo
    def packs(n):
        a, b = ay_ref[n], by_ref[n]
        return jnp.where(even_y, a, b), jnp.where(even_y, b, a)

    def side(f, r):
        n = f * rows + r
        g = n % per
        right, left = packs(n // per)
        a, b = roll(right, -halo * g, 1), roll(left, -halo * (g + 1), 1)
        return jnp.where(on_right, a, jnp.where(on_left, b, 0.0))

    return side


def spread_forward(halo, gx_axis, gy_axis, fields_ref, pm_ref, ay_ref, by_ref, rec_ref, f_out, p_out, a_msg, b_msg):
    even = lax.rem(lax.axis_index(gx_axis), 2) == 0
    rows, planes, columns = pm_ref.shape[1:]
    tile = Tile(planes, columns, halo)
    side = spreader(halo, gy_axis, ay_ref, by_ref, rows, tile)
    base = p_out.shape[0]
    for f in range(base):
        for r in range(rows):
            write(p_out, W(pm_ref[f, r], side(f, r)), f, r)
    for f in range(fields_ref.shape[0]):
        for r in range(rows):
            write(f_out, W(fields_ref[f, pl.ds(r, planes, stride=rows), :], side(base + f, r)), f, r)
    forward_messages(tile, even, f_out, p_out, a_msg, b_msg, True)


def spread_adjoint(halo, gx_axis, gy_axis, cot_ref, p_ref, ay_ref, by_ref, rec_ref, a_out, a_msg, b_msg):
    even = lax.rem(lax.axis_index(gx_axis), 2) == 0
    rows, planes, columns = p_ref.shape[1], p_ref.shape[2] // 2, p_ref.shape[3]
    tile = Tile(planes, columns, halo)
    side = spreader(halo, gy_axis, ay_ref, by_ref, rows, tile)
    count = cot_ref.shape[0]
    for f in range(count):
        for r in range(rows):
            value = W(cot_ref[f, pl.ds(r, planes, stride=rows), :], side(p_ref.shape[0] + count + f, r))
            if f == PP:
                value = value + read(rec_ref, rec_ref.shape[0] - 1, r)
            write(a_out, value * read(p_ref, PF, r), f, r)
    adjoint_messages(tile, even, a_out, p_ref, a_msg, b_msg)


def forward_messages(tile, even, f_ref, p_ref, a_msg, b_msg, with_params):
    rows = f_ref.shape[1]
    s = lambda f, r: read(f_ref, f, r)
    p = lambda f, r: read(p_ref, f, r)
    sides = []
    for r, low, high in ((0, False, True), (rows - 1, True, False)):
        got = forward_edge(tile, s, s, p, r, low, high)
        sides.append(got + [p(PH, r), p(PK, r)] if with_params else got)
    send(tile, even, *sides, a_msg, b_msg)


def adjoint_messages(tile, even, a_ref, p_ref, a_msg, b_msg):
    rows = a_ref.shape[1]
    a = lambda f, r: read(a_ref, f, r)
    p = lambda f, r: read(p_ref, f, r)
    qs = memo(lambda r: adjoint_stress(p, a, r))
    q = lambda f, r: qs(r)[f]
    send(tile, even, *[
        adjoint_edge(tile, q, a, p, r, low, high) for r, low, high in ((0, False, True), (rows - 1, True, False))
    ], a_msg, b_msg)


SLOT = {XX: 0, XY: 1, XZ: 2, PP: 3}


def end(r):
    return 0 if r < 0 else 1


def sums(ff, aa):
    fo, pu, wo, ee, gg, w_ = ff[0:3], ff[3:6], ff[6:9], ff[9:12], ff[12:15], ff[15]
    af, ag, sg, pi = aa[0:3], aa[3:6], aa[6:12], aa[12]
    tr, dd = sg[0] + sg[1] + sg[2], ee[0] + ee[1] + ee[2]
    dot = lambda x, y: x[0] * y[0] + x[1] * y[1] + x[2] * y[2]
    return [
        dot(af, fo), dot(ag, pu), dot(af, pu), dot(ag, wo),
        tr * dd, tr * w_, 2.0 * dot(sg[0:3], ee) + dot(sg[3:6], gg), pi * dd, pi * w_,
    ]


def sums_kernel(*refs):
    out, pairs = refs[-1], refs[:-1]
    for r in range(out.shape[1]):
        acc = [0.0] * 9
        for n in range(0, len(pairs), 2):
            adds = sums([pairs[n][m, r] for m in range(16)], [pairs[n + 1][m, r] for m in range(13)])
            acc = [x + y for x, y in zip(acc, adds)]
        for n, x in enumerate(acc):
            out[n, r] = x


def forward_kernel(gx_axis, halo, j, steps, *refs):
    refs = list(refs)
    take = lambda n: [refs.pop(0) for _ in range(n)]
    f_ref, p_ref, am_ref, bm_ref = take(4)
    first, final = j == 0, j == steps - 1
    if not first:
        (hk_ref,) = take(1)
    if final:
        old_ref, acc_ref, acc_out = take(3)
    else:
        src_ref, f_out, a_msg, b_msg, save = take(5)
    if first:
        (hk_out,) = take(1)
    assert not refs
    rows, planes, columns = f_ref.shape[1], f_ref.shape[2] // 2, f_ref.shape[3]
    tile = Tile(planes, columns, halo)
    sides = receive(tile, gx_axis, am_ref, bm_ref, EDGE + (2 if first else 0))
    p = lambda f, r: read(p_ref, f, r)
    old = lambda f, r: read(f_ref, f, r)
    hk = []
    for n in range(2):
        if first:
            pair = sides[n][EDGE : EDGE + 2]
            for m in range(2):
                write(hk_out, pair[m], n, m)
        else:
            pair = [read(hk_ref, n, m) for m in range(2)]
        hk.append(pair)

    def s(f, r):
        return old(f, r) if 0 <= r < rows else sides[end(r)][SLOT[f]]

    @memo
    def velocity(r):
        if 0 <= r < rows:
            forces, slopes = momentum(tile, s, r)
            h, k, m = p(PH, r), p(PK, r), p(PM, r)
            out, pushes = {}, []
            for i in range(3):
                w = old(WX + i, r)
                g = -(slopes[i] + m * w)
                pushes.append(g)
                out[VX + i] = old(VX + i, r) + h * (3.0 * forces[i] - g)
                out[WX + i] = w + h * (k * g - forces[i])
            return out, forces, pushes
        n = end(r)
        got = sides[n][4:8]
        edge = 0 if n == 0 else rows - 1
        h, k = hk[n]
        t = h if n == 0 else -h
        xx, pp = t * old(XX, edge), t * old(PP, edge)
        return {
            VX: got[0] + (3.0 * xx + pp),
            VY: got[1] + 3.0 * (t * old(XY, edge)),
            VZ: got[2] + 3.0 * (t * old(XZ, edge)),
            WX: got[3] - (k * pp + xx),
        }, None, None

    v = lambda f, r: velocity(r)[0][f]
    for r in range(rows):
        e = [dx(v, VX, r), tile.dy(v(VY, r)), tile.dz(v(VZ, r))]
        g = [
            tile.dz(v(VY, r)) + tile.dy(v(VZ, r)),
            tile.dz(v(VX, r)) + dx(v, VZ, r),
            tile.dy(v(VX, r)) + dx(v, VY, r),
        ]
        dw = dx(v, WX, r) + tile.dy(v(WY, r)) + tile.dz(v(WZ, r))
        new, forces, pushes = velocity(r)
        here = [x.m for x in forces + pushes] + [old(WX + i, r).m for i in range(3)]
        here += [x.m for x in e + g] + [dw.m]
        if final:
            adds = sums(here, [old_ref[n, r] for n in range(13)])
            for n, x in enumerate(adds):
                acc_out[n, r] = acc_ref[n, r] + x
            continue
        for n, x in enumerate(here):
            save[n, r] = x
        new = dict(new)
        dv = e[0] + e[1] + e[2]
        sh, b = p(PS, r), p(PB, r)
        ab = p(PA, r) * b
        common = p(PL, r) * dv + ab * dw
        for i in range(3):
            new[XX + i] = old(XX + i, r) + (common + 2.0 * (sh * e[i]))
            new[YZ + i] = old(YZ + i, r) + sh * g[i]
        new[PP] = old(PP, r) - (ab * dv + b * dw) + read(src_ref, j, r)
        factor = p(PF, r)
        for f, value in new.items():
            write(f_out, value * factor, f, r)
    if not final:
        even = lax.rem(lax.axis_index(gx_axis), 2) == 0
        forward_messages(tile, even, f_out, p_ref, a_msg, b_msg, False)


def adjoint_kernel(gx_axis, halo, j, steps, *refs):
    refs = list(refs)
    take = lambda n: [refs.pop(0) for _ in range(n)]
    a_ref, p_ref, am_ref, bm_ref, hk_ref = take(5)
    final = j == steps - 1
    if final:
        old_ref, acc_ref, grad_out, par_out = take(4)
    else:
        rec_ref, a_out, a_msg, b_msg, save = take(5)
    assert not refs
    rows, planes, columns = a_ref.shape[1], a_ref.shape[2] // 2, a_ref.shape[3]
    tile = Tile(planes, columns, halo)
    sides = receive(tile, gx_axis, am_ref, bm_ref, EDGE)
    p = lambda f, r: read(p_ref, f, r)
    lam = lambda f, r: read(a_ref, f, r)
    qs = memo(lambda r: adjoint_stress(p, lam, r))

    def q(f, r):
        return qs(r)[f] if 0 <= r < rows else sides[end(r)][SLOT[f]]

    @memo
    def cots(r):
        if 0 <= r < rows:
            forces, slopes = momentum(tile, q, r)
            h, k = p(PH, r), p(PK, r)
            cf, cg, vel = [], [], {}
            for i in range(3):
                lv, lw = lam(VX + i, r) - forces[i], lam(WX + i, r) - slopes[i]
                cf.append(h * (3.0 * lv - lw))
                cg.append(h * (k * lw - lv))
                vel[VX + i] = lv
                vel[WX + i] = lw - p(PM, r) * cg[i]
            return cf, cg, vel
        n = end(r)
        got = sides[n][4:8]
        edge = 0 if n == 0 else rows - 1
        h, k = [read(hk_ref, n, m) for m in range(2)]
        t = -h if n == 0 else h
        xx, pp = t * q(XX, edge), t * q(PP, edge)
        return [
            got[0] + (3.0 * xx - pp),
            got[1] + 3.0 * (t * q(XY, edge)),
            got[2] + 3.0 * (t * q(XZ, edge)),
        ], [got[3] + (k * pp - xx)], None

    cF = lambda i, r: cots(r)[0][i]
    cG = lambda i, r: cots(r)[1][i]
    for r in range(rows):
        cf, cg, vel = cots(r)
        out = dict(vel)
        out[XX] = lam(XX, r) - dx(cF, 0, r)
        out[YY] = lam(YY, r) - tile.dy(cF(1, r))
        out[ZZ] = lam(ZZ, r) - tile.dz(cF(2, r))
        out[YZ] = lam(YZ, r) - (tile.dz(cF(1, r)) + tile.dy(cF(2, r)))
        out[XZ] = lam(XZ, r) - (tile.dz(cF(0, r)) + dx(cF, 2, r))
        out[XY] = lam(XY, r) - (tile.dy(cF(0, r)) + dx(cF, 1, r))
        out[PP] = lam(PP, r) + (dx(cG, 0, r) + tile.dy(cG(1, r)) + tile.dz(cG(2, r)))
        here = [x.m for x in cf + cg] + [lam(f, r).m for f in (XX, YY, ZZ, YZ, XZ, XY, PP)]
        if not final:
            for n, x in enumerate(here):
                save[n, r] = x
            out[PP] = out[PP] + read(rec_ref, steps - 2 - j, r)
            for f, value in out.items():
                write(a_out, value * p(PF, r), f, r)
            continue
        for f, value in out.items():
            grad_out[f, pl.ds(r, planes, stride=rows), :] = value.m
        adds = sums([old_ref[n, r] for n in range(16)], here)
        a1, a2, a3, a4, b1, b2, b3, b4, b5 = [acc_ref[n, r] + x for n, x in enumerate(adds)]
        h, k, b, al = [p_ref[n, r, pl.ds(0, planes)] for n in (PH, PK, PB, PA)]
        h4 = 4.0 * h
        grads = [
            h4 * (a3 - 3.0 * a1),
            h4 * (a1 + a2 - k * (3.0 * a2 + a3)),
            -2.0 * a4,
            0.25 * b1,
            0.25 * b3,
            0.25 * (al * (b2 - b4) - b5),
            b * (b2 - b4),
        ]
        for n, x in enumerate(grads):
            par_out[n, pl.ds(r, planes, stride=rows), :] = x
    if not final:
        even = lax.rem(lax.axis_index(gx_axis), 2) == 0
        adjoint_messages(tile, even, a_out, p_ref, a_msg, b_msg)


def swaps(axis, odd):
    nx, ny = lax.axis_size("gx"), lax.axis_size("gy")
    count, other = (nx, ny) if axis == "gx" else (ny, nx)
    place = (lambda i, k: i * ny + k) if axis == "gx" else (lambda i, k: k * ny + i)
    out, met = [], set()
    for i in range(odd, count - 1, 2):
        met |= {i, i + 1}
        for k in range(other):
            out += [(place(i, k), place(i + 1, k)), (place(i + 1, k), place(i, k))]
    for i in set(range(count)) - met:
        for k in range(0, other - 1, 2):
            out += [(place(i, k), place(i, k + 1)), (place(i, k + 1), place(i, k))]
    return sorted(out)


def exchange(axis, a, b):
    mesh = ("gx", "gy")
    b = lax.ppermute(b, mesh, swaps(axis, 1))
    a = lax.ppermute(a, mesh, swaps(axis, 0))
    return a, b


def call(kernel, outs, *args):
    shapes = [o if isinstance(o, jax.ShapeDtypeStruct) else jax.ShapeDtypeStruct(o, jnp.float32) for o in outs]
    return pl.pallas_call(
        kernel,
        out_shape=shapes,
        in_specs=[pl.BlockSpec(memory_space=pltpu.VMEM)] * len(args),
        out_specs=[pl.BlockSpec(memory_space=pltpu.VMEM)] * len(outs),
        compiler_params=pltpu.CompilerParams(vmem_limit_bytes=48 << 20),
    )(*args)


def per_device(
    fields, density, fluid_density, mobility, lame_lambda, shear_modulus, biot_modulus, biot_coef,
    region_mask, profile_index, profile_table, source_cells, source_amp, receiver_cells, field_cot, receiver_cot,
):
    planes, rows, columns = region_mask.shape
    steps = source_amp.shape[0]
    count = fields.shape[0]
    halo = 2 * steps
    assert steps > 2 and planes == 8 and columns == 128 and columns % (2 * halo) == 0 and rows > 1
    flat = lambda x: x.reshape(-1, planes * rows, columns)
    fields, field_cot = flat(fields), flat(field_cot)
    raw = [flat(x) for x in (density, fluid_density, mobility, lame_lambda, shear_modulus, biot_modulus, biot_coef)]
    packs = -(-(2 * count + 8) * rows * halo // columns)
    own, wide = (rows, planes, columns), (rows, 2 * planes, columns)

    table = profile_table[None]
    small = [receiver_cells[None], receiver_cot, source_cells[None], source_amp]
    inputs = [*raw, table, flat(region_mask), flat(profile_index), fields, field_cot, *small]
    whole = [fields, field_cot, *small]
    plane = (planes * rows, columns)

    def start(*refs):
        refs = list(refs)
        hbm = refs[:7] + refs[8:10] + refs[7:8] + refs[10:16]
        start_kernel(halo, "gy", hbm, refs[16:25], refs[25:])

    p_own, ay, by, fields, field_cot, *small = pl.pallas_call(
        start,
        out_shape=[jax.ShapeDtypeStruct(s, jnp.float32) for s in [(8, *own)] + [(packs, planes, columns)] * 2]
        + [jax.ShapeDtypeStruct(x.shape, x.dtype) for x in whole],
        in_specs=[pl.BlockSpec(memory_space=pltpu.HBM)] * 16,
        out_specs=[pl.BlockSpec(memory_space=pltpu.VMEM)] * 9,
        scratch_shapes=[
            pltpu.VMEM((7, 1, *plane), jnp.float32), pltpu.VMEM((1, *plane), jnp.int32),
            pltpu.VMEM((1, *plane), jnp.int32), pltpu.SMEM(table.shape, jnp.float32),
            pltpu.SemaphoreType.DMA((16,)),
        ],
        compiler_params=pltpu.CompilerParams(vmem_limit_bytes=48 << 20),
    )(*[pltpu.with_memory_space_constraint(x, pltpu.HBM) for x in inputs])
    ay, by = exchange("gy", ay, by)
    rec, src = call(functools.partial(inject_kernel, halo, "gx", "gy"), [(steps, *wide)] * 2, *small)
    tiles = lambda n: (n + -(-n * 2 * halo // columns), planes, columns)
    names = (halo, "gx", "gy")
    f, p, am, bm = call(
        functools.partial(spread_forward, *names),
        [(count, *wide), (8, *wide)] + [tiles(EDGE + 2)] * 2, fields, p_own, ay, by,
        rec,
    )
    forward = exchange("gx", am, bm)
    a, am, bm = call(
        functools.partial(spread_adjoint, *names), [(count, *wide)] + [tiles(EDGE)] * 2, field_cot, p, ay, by, rec,
    )
    adjoint = exchange("gx", am, bm)
    saved_f, saved_a, hk = [], [], None
    for j in range(steps - 1):
        args = [f, p, *forward] + ([src] if j == 0 else [hk, src])
        outs = [(count, *wide)] + [tiles(EDGE)] * 2 + [(16, *own)] + ([(2, 2, 2 * planes, columns)] if j == 0 else [])
        f, am, bm, save, *rest = call(functools.partial(forward_kernel, "gx", halo, j, steps), outs, *args)
        forward = exchange("gx", am, bm)
        saved_f.append(save)
        hk = rest[0] if j == 0 else hk
        outs = [(count, *wide)] + [tiles(EDGE)] * 2 + [(13, *own)]
        a, am, bm, save = call(
            functools.partial(adjoint_kernel, "gx", halo, j, steps), outs, a, p, *adjoint, hk, rec
        )
        adjoint = exchange("gx", am, bm)
        saved_a.append(save)
    middle = [x for t in range(1, steps - 1) for x in (saved_f[t], saved_a[steps - 1 - t])]
    (acc,) = call(sums_kernel, [(9, *own)], *middle)
    (acc,) = call(
        functools.partial(forward_kernel, "gx", halo, steps - 1, steps), [(9, *own)], f, p, *forward, hk, saved_a[0], acc
    )
    grad, par = call(
        functools.partial(adjoint_kernel, "gx", halo, steps - 1, steps),
        [(count, *plane), (7, *plane)], a, p, *adjoint, hk, saved_f[0], acc,
    )
    return grad.reshape(count, planes, rows, columns), par.reshape(7, planes, rows, columns)


def solution(mesh):
    plane, field = P(None, "gx", "gy"), P(None, None, "gx", "gy")
    in_specs = (field,) + (plane,) * 9 + (P(),) * 4 + (field, P())
    return jax.shard_map(per_device, mesh=mesh, in_specs=in_specs, out_specs=(field, field), check_vma=False)
```

```python
import functools

import jax
import jax.numpy as jnp
from jax import lax
from jax.experimental import pallas as pl
from jax.experimental.pallas import tpu as pltpu
from jax.sharding import PartitionSpec as P


VX, VY, VZ, WX, WY, WZ, XX, YY, ZZ, YZ, XZ, XY, PP = range(13)
PH, PK, PM, PL, PS, PB, PA, PF = range(8)
EDGE = 8


class W:
    __slots__ = ("m", "h")

    def __init__(self, m, h):
        self.m, self.h = m, h

    def __add__(self, o):
        return W(self.m + o.m, self.h + o.h)

    def __sub__(self, o):
        return W(self.m - o.m, self.h - o.h)

    def __mul__(self, o):
        if isinstance(o, W):
            return W(self.m * o.m, self.h * o.h)
        return W(self.m * o, self.h * o)

    __rmul__ = __mul__

    def __neg__(self):
        return W(-self.m, -self.h)


def roll(x, shift, axis):
    shift %= x.shape[axis]
    return pltpu.roll(x, shift, axis) if shift else x


class Tile:
    def __init__(self, planes, columns, halo):
        self.shape = (planes, columns)
        self.planes, self.columns, self.halo = planes, columns, halo
        self.lane = lax.broadcasted_iota(jnp.int32, self.shape, 1)
        sub = lax.broadcasted_iota(jnp.int32, self.shape, 0)
        self.first, self.last = self.lane == 0, self.lane == columns - 1
        self.bottom, self.top = sub == 0, sub == planes - 1
        self.zero = jnp.zeros(self.shape, jnp.float32)

    def dy(self, w):
        a, b = roll(w.m, -1, 1), roll(w.h, -1, 1)
        c, d = roll(w.m, 1, 1), roll(w.h, 1, 1)
        return W(
            jnp.where(self.last, b, a) - jnp.where(self.first, d, c),
            jnp.where(self.last, a, b) - jnp.where(self.first, c, d),
        )

    def dz1(self, a):
        return jnp.where(self.top, 0.0, roll(a, -1, 0)) - jnp.where(self.bottom, 0.0, roll(a, 1, 0))

    def dz(self, w):
        return W(self.dz1(w.m), self.dz1(w.h))

    def pack(self, tiles, reach):
        width = 2 * reach
        group = self.lane // width
        out = []
        per = self.columns // width
        for base in range(0, len(tiles), per):
            total = self.zero
            for j, tile in enumerate(tiles[base : base + per]):
                total = jnp.where(group == j, roll(tile, reach + width * j, 1), total)
            out.append(total)
        return out

    def unpack(self, tiles, index, reach):
        width = 2 * reach
        per = self.columns // width
        return roll(tiles[index // per], -(reach + width * (index % per)), 1)


def dx(get, name, r, low=True, high=True):
    if low and high:
        return get(name, r + 1) - get(name, r - 1)
    return get(name, r + 1) if high else -get(name, r - 1)


def read(ref, *at):
    planes = ref.shape[-2] // 2
    return W(ref[(*at, pl.ds(0, planes))], ref[(*at, pl.ds(planes, planes))])


def write(ref, value, *at):
    planes = ref.shape[-2] // 2
    ref[(*at, pl.ds(0, planes))] = value.m
    ref[(*at, pl.ds(planes, planes))] = value.h


def memo(fn):
    return functools.lru_cache(maxsize=None)(fn)


def momentum(tile, s, r, low=True, high=True):
    forces = [
        dx(s, XX, r, low, high) + tile.dy(s(XY, r)) + tile.dz(s(XZ, r)),
        dx(s, XY, r, low, high) + tile.dy(s(YY, r)) + tile.dz(s(YZ, r)),
        dx(s, XZ, r, low, high) + tile.dy(s(YZ, r)) + tile.dz(s(ZZ, r)),
    ]
    slopes = [dx(s, PP, r, low, high), tile.dy(s(PP, r)), tile.dz(s(PP, r))]
    return forces, slopes


def forward_edge(tile, s, v, p, r, low, high):
    forces, slopes = momentum(tile, s, r, low, high)
    h, k, m = p(PH, r), p(PK, r), p(PM, r)
    solid, fluid, pushes = [], [], []
    for i in range(3):
        w = v(WX + i, r)
        g = -(slopes[i] + m * w)
        pushes.append(g)
        solid.append(v(VX + i, r) + h * (3.0 * forces[i] - g))
        fluid.append(w + h * (k * g - forces[i]))
    sent = [s(XX, r), s(XY, r), s(XZ, r), s(PP, r)] + solid + fluid[:1]
    return sent, solid + fluid, forces + pushes


def adjoint_stress(p, a, r):
    trace = a(XX, r) + a(YY, r) + a(ZZ, r)
    b, pi = p(PB, r), a(PP, r)
    cross = p(PA, r) * b
    common = p(PL, r) * trace - cross * pi
    s = p(PS, r)
    s2 = 2.0 * s
    return {
        XX: common + s2 * a(XX, r),
        YY: common + s2 * a(YY, r),
        ZZ: common + s2 * a(ZZ, r),
        YZ: s * a(YZ, r),
        XZ: s * a(XZ, r),
        XY: s * a(XY, r),
        PP: cross * trace - b * pi,
    }


def adjoint_edge(tile, q, a, p, r, low, high):
    forces, slopes = momentum(tile, q, r, low, high)
    h, k = p(PH, r), p(PK, r)
    lv = [a(VX + i, r) - forces[i] for i in range(3)]
    lw = [a(WX + i, r) - slopes[i] for i in range(3)]
    sent = [q(XX, r), q(XY, r), q(XZ, r), q(PP, r)]
    sent += [h * (3.0 * lv[i] - lw[i]) for i in range(3)] + [h * (k * lw[0] - lv[0])]
    return sent, lv + lw


def send(tile, even, reach, first_rows, last_rows, a_ref, b_ref):
    ups = [w.m for w in first_rows] + tile.pack([w.h for w in first_rows], reach)
    downs = [w.m for w in last_rows] + tile.pack([w.h for w in last_rows], reach)
    for n, (up, down) in enumerate(zip(ups, downs)):
        a_ref[n] = jnp.where(even, down, up)
        b_ref[n] = jnp.where(even, up, down)


def receive(tile, axis, a_ref, b_ref, count, reach):
    total = a_ref.shape[0]
    at = lax.axis_index(axis)
    even = lax.rem(at, 2) == 0
    before, after = at > 0, at < lax.axis_size(axis) - 1
    first = [jnp.where(before, jnp.where(even, b_ref[n], a_ref[n]), 0.0) for n in range(total)]
    last = [jnp.where(after, jnp.where(even, a_ref[n], b_ref[n]), 0.0) for n in range(total)]
    sides = []
    for got in (first, last):
        sides.append([W(got[n], tile.unpack(got[count:], n, reach)) for n in range(count)])
    return sides


def start_kernel(halo, my_axis, inputs, outs, scratch):
    par_hbm, (mask_hbm, index_hbm, table_hbm), rest_hbm = inputs[:7], inputs[7:10], inputs[10:]
    p_ref, a_ref, b_ref, *rest = outs
    par_ref, mask_ref, index_ref, table_ref, sems = scratch
    fields_ref, cot_ref = rest[:2]
    copies = [pltpu.make_async_copy(src, par_ref.at[n], sems.at[n]) for n, src in enumerate(par_hbm)]
    for src, dst in zip((table_hbm, mask_hbm, index_hbm, *rest_hbm), (table_ref, mask_ref, index_ref, *rest)):
        copies.append(pltpu.make_async_copy(src, dst, sems.at[len(copies)]))
    for copy in copies:
        copy.start()
    for copy in copies[:10]:
        copy.wait()

    even = lax.rem(lax.axis_index(my_axis), 2) == 0
    rows = p_ref.shape[1]
    planes, columns = p_ref.shape[2], p_ref.shape[3]
    lane = lax.broadcasted_iota(jnp.int32, (planes, columns), 1)
    group = lane // halo
    per = columns // halo

    def at(r):
        return pl.ds(r, planes, stride=rows)

    for r in range(rows):
        density, fluid, mobility, lame, shear, modulus, coupling = [par_ref[n, 0, at(r), :] for n in range(7)]
        lookup = jnp.zeros((planes, columns), jnp.float32)
        index = index_ref[0, at(r), :]
        for n in range(table_ref.shape[1]):
            lookup = jnp.where(index == n, table_ref[0, n], lookup)
        p_ref[PH, r] = 0.25 / (3.0 * density - fluid)
        p_ref[PK, r] = density / fluid
        p_ref[PM, r] = 2.0 * mobility
        p_ref[PL, r] = 0.25 * lame
        p_ref[PS, r] = 0.25 * shear
        p_ref[PB, r] = 0.25 * modulus
        p_ref[PA, r] = coupling
        p_ref[PF, r] = 1.0 - mask_ref[0, at(r), :].astype(jnp.float32) * lookup
    sources = []
    for f in range(p_ref.shape[0]):
        for r in range(rows):
            sources.append(lambda f=f, r=r: p_ref[f, r])
    for ref in (fields_ref, cot_ref):
        for f in range(ref.shape[0]):
            for r in range(rows):
                sources.append(lambda ref=ref, f=f, r=r: ref[f, at(r), :])
    waited = False
    for n in range(a_ref.shape[0]):
        if (n + 1) * per > p_ref.shape[0] * rows and not waited:
            for copy in copies[10:]:
                copy.wait()
            waited = True
        left = jnp.zeros((planes, columns), jnp.float32)
        right = left
        for g in range(per):
            if n * per + g < len(sources):
                x = sources[n * per + g]()
                left = jnp.where(group == g, roll(x, halo * g, 1), left)
                right = jnp.where(group == g, roll(x, halo * g + halo, 1), right)
        a_ref[n] = jnp.where(even, right, left)
        b_ref[n] = jnp.where(even, left, right)


def inject_kernel(halo, gx_axis, gy_axis, rec_ref, cot_ref, src_ref, amp_ref, rec_out, src_out):
    for cells_ref, amounts_ref, out in ((rec_ref, cot_ref, rec_out), (src_ref, amp_ref, src_out)):
        steps, rows, planes2, columns = out.shape
        planes = planes2 // 2
        count = amounts_ref.shape[1]
        total_x, total_y = rows * lax.axis_size(gx_axis), columns * lax.axis_size(gy_axis)
        cells = cells_ref[...]
        line = lax.div(cells, jnp.full_like(cells, total_y))
        depth = lax.div(line, jnp.full_like(cells, total_x))
        col = cells - line * total_y - lax.axis_index(gy_axis) * columns
        x = line - depth * total_x - lax.axis_index(gx_axis) * rows
        row = jnp.where((x >= 0) & (x < rows), x * planes + depth, -1)
        row_at = lax.broadcasted_iota(jnp.int32, (rows * planes, count), 0)
        here = row_at == row
        lhs = jnp.concatenate([jnp.where(here, amounts_ref[t : t + 1, :], 0.0) for t in range(steps)], axis=0)
        lane = lax.broadcasted_iota(jnp.int32, (columns, count), 0)
        side = jnp.where(lane < halo, lane + columns, jnp.where(lane >= columns - halo, lane - columns, -columns))
        for half, where in enumerate((lane, side)):
            rhs = (where == col).astype(jnp.float32)
            got = lax.dot_general(
                lhs, rhs, (((1,), (1,)), ((), ())), precision=lax.Precision.HIGHEST, preferred_element_type=jnp.float32
            )
            for t in range(steps):
                for r in range(rows):
                    base = (t * rows + r) * planes
                    out[t, r, pl.ds(half * planes, planes)] = got[base : base + planes]


def spreader(halo, gy_axis, ay_ref, by_ref, rows, tile):
    at_y = lax.axis_index(gy_axis)
    even_y = lax.rem(at_y, 2) == 0
    columns = tile.columns
    per = columns // halo
    on_right = (tile.lane < halo) & (at_y < lax.axis_size(gy_axis) - 1)
    on_left = (tile.lane >= columns - halo) & (at_y > 0)

    @memo
    def packs(n):
        a, b = ay_ref[n], by_ref[n]
        return jnp.where(even_y, a, b), jnp.where(even_y, b, a)

    def side(f, r):
        n = f * rows + r
        g = n % per
        right, left = packs(n // per)
        a, b = roll(right, -halo * g, 1), roll(left, -halo * (g + 1), 1)
        return jnp.where(on_right, a, jnp.where(on_left, b, 0.0))

    return side


def place(r, depth, rows):
    if r < depth:
        return 1, r
    return (1, r - rows + 2 * depth) if r >= rows - depth else (0, r - depth)


def getter(pair, depth, rows, both=True):
    def get(f, r):
        which, at = place(r, depth, rows)
        return read(pair[which], f, at) if both else pair[which][f, at]

    return get


def putter(pair, depth, rows):
    def put(value, f, r):
        which, at = place(r, depth, rows)
        if isinstance(value, W):
            write(pair[which], value, f, at)
        else:
            pair[which][f, at] = value

    return put


STRESS = (XX, YY, ZZ, YZ, XZ, XY, PP)
SLOT = {XX: 0, XY: 1, XZ: 2, PP: 3}


def messages(tile, axis, reach, s, a, p, rows, a_msg, b_msg, part_f, part_g, part_a, with_params):
    even = lax.rem(lax.axis_index(axis), 2) == 0
    qs = memo(lambda r: adjoint_stress(p, a, r))
    q = lambda f, r: qs(r)[f]
    sides = []
    for n, (r, low, high) in enumerate(((0, False, True), (rows - 1, True, False))):
        got, new, drives = forward_edge(tile, s, s, p, r, low, high)
        more, lam = adjoint_edge(tile, q, a, p, r, low, high)
        for m in range(6):
            write(part_f, new[m], m, n)
            part_g[m, n] = drives[m].m
            write(part_a, lam[m], m, n)
        sides.append(got + more + ([p(PH, r), p(PK, r)] if with_params else []))
    send(tile, even, reach, *sides, a_msg, b_msg)


def spread_kernel(halo, gx_axis, gy_axis, fields_ref, cot_ref, pm_ref, ay_ref, by_ref, rec_ref, p_out, *outs):
    rows, planes, columns = pm_ref.shape[1:]
    tile = Tile(planes, columns, halo)
    side = spreader(halo, gy_axis, ay_ref, by_ref, rows, tile)
    base, count = p_out.shape[0], fields_ref.shape[0]
    for f in range(base):
        for r in range(rows):
            write(p_out, W(pm_ref[f, r], side(f, r)), f, r)
    put_f, put_a = putter(outs[0:2], 2, rows), putter(outs[2:4], 2, rows)
    for f in range(count):
        for r in range(rows):
            at = pl.ds(r, planes, stride=rows)
            put_f(W(fields_ref[f, at, :], side(base + f, r)), f, r)
            value = W(cot_ref[f, at, :], side(base + count + f, r))
            if f == PP:
                value = value + read(rec_ref, rec_ref.shape[0] - 1, r)
            put_a(value * read(p_out, PF, r), f, r)
    p = lambda f, r: read(p_out, f, r)
    messages(tile, gx_axis, halo, getter(outs[0:2], 2, rows), getter(outs[2:4], 2, rows), p, rows, *outs[4:], True)


def sums(ff, aa):
    fo, pu, wo, ee, gg, w_ = ff[0:3], ff[3:6], ff[6:9], ff[9:12], ff[12:15], ff[15]
    af, ag, sg, pi = aa[0:3], aa[3:6], aa[6:12], aa[12]
    tr, dd = sg[0] + sg[1] + sg[2], ee[0] + ee[1] + ee[2]
    dot = lambda x, y: x[0] * y[0] + x[1] * y[1] + x[2] * y[2]
    return [
        dot(af, fo), dot(ag, pu), dot(af, pu), dot(ag, wo),
        tr * dd, tr * w_, 2.0 * dot(sg[0:3], ee) + dot(sg[3:6], gg), pi * dd, pi * w_,
    ]


def saved_forward(refs, rows):
    vel, strain = getter(refs[0:2], 1, rows, False), getter(refs[2:4], 2, rows, False)
    return lambda r: [vel(n, r) for n in range(9)] + [strain(n, r) for n in range(7)]


def saved_adjoint(refs, rows):
    cot = getter(refs[0:2], 1, rows, False)
    return lambda r: [cot(n, r) for n in range(6)] + [refs[2][n, r] for n in range(7)]


def sums_kernel(rows, *refs):
    out, pairs = refs[-1], refs[:-1]
    for r in range(rows):
        acc = [0.0] * 9
        for n in range(0, len(pairs), 7):
            ff, aa = saved_forward(pairs[n : n + 4], rows), saved_adjoint(pairs[n + 4 : n + 7], rows)
            acc = [x + y for x, y in zip(acc, sums(ff(r), aa(r)))]
        for n, x in enumerate(acc):
            out[n, r] = x


def gradients(acc, p, r):
    a1, a2, a3, a4, b1, b2, b3, b4, b5 = acc
    h, k, b, al = [p(n, r).m for n in (PH, PK, PB, PA)]
    h4 = 4.0 * h
    return [
        h4 * (a3 - 3.0 * a1),
        h4 * (a1 + a2 - k * (3.0 * a2 + a3)),
        -2.0 * a4,
        0.25 * b1,
        0.25 * b3,
        0.25 * (al * (b2 - b4) - b5),
        b * (b2 - b4),
    ]


def strains(tile, v, r):
    e = [dx(v, VX, r), tile.dy(v(VY, r)), tile.dz(v(VZ, r))]
    g = [
        tile.dz(v(VY, r)) + tile.dy(v(VZ, r)),
        tile.dz(v(VX, r)) + dx(v, VZ, r),
        tile.dy(v(VX, r)) + dx(v, VY, r),
    ]
    return e, g, dx(v, WX, r) + tile.dy(v(WY, r)) + tile.dz(v(WZ, r))


def new_fields(p, old, v, e, g, dw, source, r):
    dv = e[0] + e[1] + e[2]
    sh, b = p(PS, r), p(PB, r)
    ab = p(PA, r) * b
    common = p(PL, r) * dv + ab * dw
    new = {f: v(f, r) for f in range(6)}
    for i in range(3):
        new[XX + i] = old(XX + i, r) + (common + 2.0 * (sh * e[i]))
        new[YZ + i] = old(YZ + i, r) + sh * g[i]
    new[PP] = old(PP, r) - (ab * dv + b * dw) + source
    factor = p(PF, r)
    return {f: value * factor for f, value in new.items()}


def back_fields(tile, lam, c, vel, r):
    out = dict(vel)
    out[XX] = lam(XX, r) - dx(c, 0, r)
    out[YY] = lam(YY, r) - tile.dy(c(1, r))
    out[ZZ] = lam(ZZ, r) - tile.dz(c(2, r))
    out[YZ] = lam(YZ, r) - (tile.dz(c(1, r)) + tile.dy(c(2, r)))
    out[XZ] = lam(XZ, r) - (tile.dz(c(0, r)) + dx(c, 2, r))
    out[XY] = lam(XY, r) - (tile.dy(c(0, r)) + dx(c, 1, r))
    out[PP] = lam(PP, r) + (dx(c, 3, r) + tile.dy(c(4, r)) + tile.dz(c(5, r)))
    return out


def push_cots(p, r, lv, lw):
    h, k, m = p(PH, r), p(PK, r), p(PM, r)
    cf = [h * (3.0 * lv[i] - lw[i]) for i in range(3)]
    cg = [h * (k * lw[i] - lv[i]) for i in range(3)]
    vel = {VX + i: lv[i] for i in range(3)} | {WX + i: lw[i] - m * cg[i] for i in range(3)}
    return cf + cg, vel


def near(rows):
    return (1, 2, rows - 3, rows - 2)


def interior_kernel(halo, j, steps, *refs):
    refs = list(refs)
    take = lambda n: [refs.pop(0) for _ in range(n)]
    final = j == steps - 1
    f_pair, a_pair, (p_ref,) = take(2), take(2), take(1)
    if final:
        old_f, old_a, (acc_ref,) = take(4), take(3), take(1)
        grad_out, par_out, vel_near = take(3)
    else:
        src_ref, rec_ref, f_out, a_out, save_vel, save_str, save_cot, save_sig = take(8)
    v_near, c_near, l_near = take(3)
    assert not refs
    rows, planes, columns = p_ref.shape[1], p_ref.shape[2] // 2, p_ref.shape[3]
    tile = Tile(planes, columns, halo)
    p = lambda f, r: read(p_ref, f, r)
    old, lam = getter(f_pair, 2, rows), getter(a_pair, 2, rows)

    @memo
    def velocity(r):
        _, new, drives = forward_edge(tile, old, old, p, r, True, True)
        return new, [x.m for x in drives] + [old(WX + i, r).m for i in range(3)]

    qs = memo(lambda r: adjoint_stress(p, lam, r))
    q = lambda f, r: qs(r)[f]

    @memo
    def cots(r):
        forces, slopes = momentum(tile, q, r)
        return push_cots(
            p, r, [lam(VX + i, r) - forces[i] for i in range(3)], [lam(WX + i, r) - slopes[i] for i in range(3)]
        )

    v = lambda f, r: velocity(r)[0][f]
    c = lambda i, r: cots(r)[0][i]
    for r in range(1, rows - 1):
        if r in near(rows):
            at = near(rows).index(r)
            for n in range(6):
                write(v_near, v(n, r), n, at)
                write(c_near, c(n, r), n, at)
                write(l_near, cots(r)[1][n], n, at)
        inner = 2 <= r < rows - 2
        if not final:
            for n, x in enumerate(velocity(r)[1]):
                save_vel[n, r - 1] = x
            for n in range(6):
                save_cot[n, r - 1] = c(n, r).m
        elif not inner:
            for n, x in enumerate(velocity(r)[1]):
                vel_near[n, 0 if r == 1 else 1] = x
        if not inner:
            continue
        e, g, dw = strains(tile, v, r)
        strain = [x.m for x in e + g] + [dw.m]
        back = back_fields(tile, lam, c, cots(r)[1], r)
        if final:
            ff = velocity(r)[1] + strain
            aa = [c(n, r).m for n in range(6)] + [lam(f, r).m for f in STRESS]
            one = sums(ff, saved_adjoint(old_a, rows)(r))
            two = sums(saved_forward(old_f, rows)(r), aa)
            acc = [acc_ref[n, r] + (x + y) for n, (x, y) in enumerate(zip(one, two))]
            for n, x in enumerate(gradients(acc, p, r)):
                par_out[n, r - 2] = x
            for f, value in back.items():
                grad_out[f, r - 2] = value.m
            continue
        for n, x in enumerate(strain):
            save_str[n, r - 2] = x
        for f, value in new_fields(p, old, v, e, g, dw, read(src_ref, j, r), r).items():
            write(f_out, value, f, r - 2)
        back[PP] = back[PP] + read(rec_ref, steps - 2 - j, r)
        for f, value in back.items():
            write(a_out, value * p(PF, r), f, r - 2)
    if not final:
        for r in range(rows):
            for n, f in enumerate(STRESS):
                save_sig[n, r] = lam(f, r).m


def edge_kernel(gx_axis, halo, j, steps, *refs):
    refs = list(refs)
    take = lambda n: [refs.pop(0) for _ in range(n)]
    first, final = j == 0, j == steps - 1
    f_ref, a_ref, p_ref, am_ref, bm_ref, part_f, part_g, part_a, v_near, c_near, l_near = take(11)
    if not first:
        (hk_ref,) = take(1)
    if final:
        old_f, old_a, (acc_ref, grad_mid, par_mid, vel_near, grad_out, par_out) = take(4), take(3), take(6)
    else:
        src_ref, rec_ref, f_out, a_out, save_vel, save_str, save_cot = take(7)
        outs = take(5)
    if first:
        (hk_out,) = take(1)
    assert not refs
    rows, planes, columns = p_ref.shape[1], p_ref.shape[2] // 2, p_ref.shape[3]
    tile = Tile(planes, columns, halo)
    sides = receive(tile, gx_axis, am_ref, bm_ref, 2 * EDGE + (2 if first else 0), halo - 2 * j)
    p = lambda f, r: read(p_ref, f, r)
    old, lam = getter((None, f_ref), 2, rows), getter((None, a_ref), 2, rows)
    hk = []
    for n in range(2):
        if first:
            pair = sides[n][2 * EDGE :]
            for m in range(2):
                write(hk_out, pair[m], n, m)
        else:
            pair = [read(hk_ref, n, m) for m in range(2)]
        hk.append(pair)

    def add_forward(base, h, k, values):
        xx, xy, xz, pp = [h * x for x in values]
        adds = [3.0 * xx + pp, 3.0 * xy, 3.0 * xz, -(k * pp + xx), -xy, -xz]
        return [x + y for x, y in zip(base, adds)]

    velocities, drives, cots, vels = {}, {}, {}, {}
    qs = memo(lambda r: adjoint_stress(p, lam, r))
    for n, r, out in ((0, 0, -1), (1, rows - 1, rows)):
        h, k = p(PH, r), p(PK, r)
        near_s, near_v = sides[n][0:4], sides[n][4:8]
        velocities[r] = add_forward([read(part_f, m, n) for m in range(6)], -h if n == 0 else h, k, near_s)
        own = [old(f, r) for f in SLOT]
        h2, k2 = hk[n]
        velocities[out] = add_forward(near_v, h2 if n == 0 else -h2, k2, own)
        sign = -1.0 if n == 0 else 1.0
        xx, xy, xz, pp = [sign * x.m for x in near_s]
        part = [part_g[m, n] for m in range(6)]
        drives[r] = [part[0] + xx, part[1] + xy, part[2] + xz, part[3] - pp, part[4], part[5]]
        drives[r] += [old(WX + i, r).m for i in range(3)]
        near_q, near_c = sides[n][EDGE : EDGE + 4], sides[n][EDGE + 4 : EDGE + 8]
        base = [read(part_a, m, n) for m in range(6)]
        for m in range(4):
            base[m] = base[m] - sign * near_q[m]
        cots[r], vels[r] = push_cots(p, r, base[0:3], base[3:6])
        t = -h2 if n == 0 else h2
        xx, xy, xz, pp = [t * qs(r)[f] for f in SLOT]
        cots[out] = [near_c[0] + (3.0 * xx - pp), near_c[1] + 3.0 * xy, near_c[2] + 3.0 * xz, near_c[3] + (k2 * pp - xx)]
    for at, r in enumerate(near(rows)):
        velocities[r] = [read(v_near, n, at) for n in range(6)]
        cots[r] = [read(c_near, n, at) for n in range(6)]
        vels[r] = {n: read(l_near, n, at) for n in range(6)}
    v = lambda f, r: velocities[r][f]
    c = lambda i, r: cots[r][i]
    new_f, new_a = {}, {}
    for r in (0, rows - 1, 1, rows - 2):
        e, g, dw = strains(tile, v, r)
        strain = [x.m for x in e + g] + [dw.m]
        back = back_fields(tile, lam, c, vels[r], r)
        at = place(r, 2, rows)[1]
        outer = r in (0, rows - 1)
        side = 0 if r < 2 else 1
        if final:
            drive = drives[r] if outer else [vel_near[n, side] for n in range(9)]
            aa = [c(n, r).m for n in range(6)] + [lam(f, r).m for f in STRESS]
            one = sums(drive + strain, saved_adjoint(old_a, rows)(r))
            two = sums(saved_forward(old_f, rows)(r), aa)
            acc = [acc_ref[n, r] + (x + y) for n, (x, y) in enumerate(zip(one, two))]
            for n, x in enumerate(gradients(acc, p, r)):
                par_out[n, pl.ds(r, planes, stride=rows), :] = x
            for f, value in back.items():
                grad_out[f, pl.ds(r, planes, stride=rows), :] = value.m
            continue
        if outer:
            for n, x in enumerate(drives[r]):
                save_vel[n, side] = x
            for n in range(6):
                save_cot[n, side] = c(n, r).m
        for n, x in enumerate(strain):
            save_str[n, at] = x
        new_f[r] = new_fields(p, old, v, e, g, dw, read(src_ref, j, r), r)
        back[PP] = back[PP] + read(rec_ref, steps - 2 - j, r)
        new_a[r] = {f: value * p(PF, r) for f, value in back.items()}
        for f in range(f_out.shape[0]):
            write(f_out, new_f[r][f], f, at)
            write(a_out, new_a[r][f], f, at)
    if final:
        for r in range(2, rows - 2):
            for n in range(par_mid.shape[0]):
                par_out[n, pl.ds(r, planes, stride=rows), :] = par_mid[n, r - 2]
            for f in range(grad_mid.shape[0]):
                grad_out[f, pl.ds(r, planes, stride=rows), :] = grad_mid[f, r - 2]
        return
    messages(
        tile, gx_axis, halo - 2 * (j + 1), getter((None, f_out), 2, rows), getter((None, a_out), 2, rows), p, rows, *outs, False
    )


def swaps(axis, odd):
    nx, ny = lax.axis_size("gx"), lax.axis_size("gy")
    count, other = (nx, ny) if axis == "gx" else (ny, nx)
    place = (lambda i, k: i * ny + k) if axis == "gx" else (lambda i, k: k * ny + i)
    out, met = [], set()
    for i in range(odd, count - 1, 2):
        met |= {i, i + 1}
        for k in range(other):
            out += [(place(i, k), place(i + 1, k)), (place(i + 1, k), place(i, k))]
    for i in set(range(count)) - met:
        for k in range(0, other - 1, 2):
            out += [(place(i, k), place(i, k + 1)), (place(i, k + 1), place(i, k))]
    return sorted(out)


def exchange(axis, a, b):
    mesh = ("gx", "gy")
    b = lax.ppermute(b, mesh, swaps(axis, 1))
    a = lax.ppermute(a, mesh, swaps(axis, 0))
    return a, b


def call(kernel, outs, *args):
    shapes = [o if isinstance(o, jax.ShapeDtypeStruct) else jax.ShapeDtypeStruct(o, jnp.float32) for o in outs]
    return pl.pallas_call(
        kernel,
        out_shape=shapes,
        in_specs=[pl.BlockSpec(memory_space=pltpu.VMEM)] * len(args),
        out_specs=[pl.BlockSpec(memory_space=pltpu.VMEM)] * len(outs),
        compiler_params=pltpu.CompilerParams(vmem_limit_bytes=48 << 20),
    )(*args)


def per_device(
    fields, density, fluid_density, mobility, lame_lambda, shear_modulus, biot_modulus, biot_coef,
    region_mask, profile_index, profile_table, source_cells, source_amp, receiver_cells, field_cot, receiver_cot,
):
    planes, rows, columns = region_mask.shape
    steps = source_amp.shape[0]
    count = fields.shape[0]
    halo = 2 * steps
    assert steps > 2 and planes == 8 and columns == 128 and columns % (2 * halo) == 0 and rows > 1
    flat = lambda x: x.reshape(-1, planes * rows, columns)
    fields, field_cot = flat(fields), flat(field_cot)
    raw = [flat(x) for x in (density, fluid_density, mobility, lame_lambda, shear_modulus, biot_modulus, biot_coef)]
    packs = -(-(2 * count + 8) * rows * halo // columns)
    own, wide = (rows, planes, columns), (rows, 2 * planes, columns)

    table = profile_table[None]
    small = [receiver_cells[None], receiver_cot, source_cells[None], source_amp]
    inputs = [*raw, table, flat(region_mask), flat(profile_index), fields, field_cot, *small]
    whole = [fields, field_cot, *small]
    plane = (planes * rows, columns)

    def start(*refs):
        refs = list(refs)
        hbm = refs[:7] + refs[8:10] + refs[7:8] + refs[10:16]
        start_kernel(halo, "gy", hbm, refs[16:25], refs[25:])

    p_own, ay, by, fields, field_cot, *small = pl.pallas_call(
        start,
        out_shape=[jax.ShapeDtypeStruct(s, jnp.float32) for s in [(8, *own)] + [(packs, planes, columns)] * 2]
        + [jax.ShapeDtypeStruct(x.shape, x.dtype) for x in whole],
        in_specs=[pl.BlockSpec(memory_space=pltpu.HBM)] * 16,
        out_specs=[pl.BlockSpec(memory_space=pltpu.VMEM)] * 9,
        scratch_shapes=[
            pltpu.VMEM((7, 1, *plane), jnp.float32), pltpu.VMEM((1, *plane), jnp.int32),
            pltpu.VMEM((1, *plane), jnp.int32), pltpu.SMEM(table.shape, jnp.float32),
            pltpu.SemaphoreType.DMA((16,)),
        ],
        compiler_params=pltpu.CompilerParams(vmem_limit_bytes=48 << 20),
    )(*[pltpu.with_memory_space_constraint(x, pltpu.HBM) for x in inputs])
    ay, by = exchange("gy", ay, by)
    rec, src = call(functools.partial(inject_kernel, halo, "gx", "gy"), [(steps, *wide)] * 2, *small)
    def tiles(n, reach):
        return n + -(-n // (columns // (2 * reach))), planes, columns

    assert rows >= 6
    part = lambda k, r, shape: (k, r, *shape[1:])
    w, m = wide, own
    parts = [part(6, 2, w), part(6, 2, m), part(6, 2, w)]
    mid, end = part(count, rows - 4, w), part(count, 4, w)
    p, fm, fe, am, ae, ma, mb, *part_refs = call(
        functools.partial(spread_kernel, halo, "gx", "gy"),
        [(8, *wide), mid, end, mid, end] + [tiles(2 * EDGE + 2, halo)] * 2 + parts,
        fields, field_cot, p_own, ay, by, rec,
    )
    saved_f, saved_a, hk, acc = [], [], [], []
    nears = [part(6, 4, w)] * 3
    for j in range(steps - 1):
        ma, mb = exchange("gx", ma, mb)
        outs = [mid, mid, part(9, rows - 2, m), part(7, rows - 4, m), part(6, rows - 2, m), (7, *own)] + nears
        nfm, nam, vel, strain, cot, sig, *near_refs = call(
            functools.partial(interior_kernel, halo, j, steps), outs, fm, fe, am, ae, p, src, rec
        )
        outs = [end, end, part(9, 2, m), part(7, 4, m), part(6, 2, m)] + [tiles(2 * EDGE, halo - 2 * (j + 1))] * 2 + parts
        outs += [] if j else [(2, 2, 2 * planes, columns)]
        fe, ae, vel2, strain2, cot2, ma, mb, *rest = call(
            functools.partial(edge_kernel, "gx", halo, j, steps), outs,
            fe, ae, p, ma, mb, *part_refs, *near_refs, *hk, src, rec,
        )
        fm, am, part_refs = nfm, nam, rest[:3]
        hk = hk or rest[3:]
        saved_f.append([vel, vel2, strain, strain2])
        saved_a.append([cot, cot2, sig])
    ma, mb = exchange("gx", ma, mb)
    middle = [x for t in range(1, steps - 1) for x in saved_f[t] + saved_a[steps - 1 - t]]
    (acc,) = call(functools.partial(sums_kernel, rows), [(9, *own)], *middle)
    outs = [part(count, rows - 4, m), part(7, rows - 4, m), part(9, 2, m)] + nears
    grad_mid, par_mid, vel_near, *near_refs = call(
        functools.partial(interior_kernel, halo, steps - 1, steps), outs, fm, fe, am, ae, p, *saved_f[0], *saved_a[0], acc
    )
    grad, par = call(
        functools.partial(edge_kernel, "gx", halo, steps - 1, steps), [(count, *plane), (7, *plane)],
        fe, ae, p, ma, mb, *part_refs, *near_refs, *hk, *saved_f[0], *saved_a[0], acc, grad_mid, par_mid, vel_near,
    )
    return grad.reshape(count, planes, rows, columns), par.reshape(7, planes, rows, columns)


def solution(mesh):
    plane, field = P(None, "gx", "gy"), P(None, None, "gx", "gy")
    in_specs = (field,) + (plane,) * 9 + (P(),) * 4 + (field, P())
    return jax.shard_map(per_device, mesh=mesh, in_specs=in_specs, out_specs=(field, field), check_vma=False)
```

```python
import functools

import jax
import jax.numpy as jnp
from jax import lax
from jax.experimental import pallas as pl
from jax.experimental.pallas import tpu as pltpu
from jax.sharding import PartitionSpec as P


VX, VY, VZ, WX, WY, WZ, XX, YY, ZZ, YZ, XZ, XY, PP = range(13)
PH, PK, PM, PL, PS, PB, PA, PF = range(8)
EDGE = 8


class W:
    __slots__ = ("m", "h")

    def __init__(self, m, h):
        self.m, self.h = m, h

    def __add__(self, o):
        return W(self.m + o.m, self.h + o.h)

    def __sub__(self, o):
        return W(self.m - o.m, self.h - o.h)

    def __mul__(self, o):
        if isinstance(o, W):
            return W(self.m * o.m, self.h * o.h)
        return W(self.m * o, self.h * o)

    __rmul__ = __mul__

    def __neg__(self):
        return W(-self.m, -self.h)


def roll(x, shift, axis):
    shift %= x.shape[axis]
    return pltpu.roll(x, shift, axis) if shift else x


class Tile:
    def __init__(self, planes, columns, halo, flip=None):
        self.flip = flip
        self.shape = (planes, columns)
        self.planes, self.columns, self.halo = planes, columns, halo
        self.lane = lax.broadcasted_iota(jnp.int32, self.shape, 1)
        sub = lax.broadcasted_iota(jnp.int32, self.shape, 0)
        self.first, self.last = self.lane == 0, self.lane == columns - 1
        self.bottom, self.top = sub == 0, sub == planes - 1
        self.zero = jnp.zeros(self.shape, jnp.float32)

    def dx(self, get, name, r, low=True, high=True):
        if low and high:
            d = get(name, r + 1) - get(name, r - 1)
        else:
            d = get(name, r + 1) if high else -get(name, r - 1)
        return d if self.flip is None else self.flip * d

    def dy(self, w):
        a, b = roll(w.m, -1, 1), roll(w.h, -1, 1)
        c, d = roll(w.m, 1, 1), roll(w.h, 1, 1)
        return W(
            jnp.where(self.last, b, a) - jnp.where(self.first, d, c),
            jnp.where(self.last, a, b) - jnp.where(self.first, c, d),
        )

    def dz1(self, a):
        return jnp.where(self.top, 0.0, roll(a, -1, 0)) - jnp.where(self.bottom, 0.0, roll(a, 1, 0))

    def dz(self, w):
        return W(self.dz1(w.m), self.dz1(w.h))

    def pack(self, tiles, reach):
        width = 2 * reach
        group = self.lane // width
        out = []
        per = self.columns // width
        for base in range(0, len(tiles), per):
            total = self.zero
            for j, tile in enumerate(tiles[base : base + per]):
                total = jnp.where(group == j, roll(tile, reach + width * j, 1), total)
            out.append(total)
        return out

    def unpack(self, tiles, index, reach):
        width = 2 * reach
        per = self.columns // width
        return roll(tiles[index // per], -(reach + width * (index % per)), 1)


def read(ref, *at):
    planes = ref.shape[-2] // 2
    return W(ref[(*at, pl.ds(0, planes))], ref[(*at, pl.ds(planes, planes))])


def write(ref, value, *at):
    planes = ref.shape[-2] // 2
    ref[(*at, pl.ds(0, planes))] = value.m
    ref[(*at, pl.ds(planes, planes))] = value.h


def memo(fn):
    return functools.lru_cache(maxsize=None)(fn)


def momentum(tile, s, r, low=True, high=True):
    forces = [
        tile.dx(s, XX, r, low, high) + tile.dy(s(XY, r)) + tile.dz(s(XZ, r)),
        tile.dx(s, XY, r, low, high) + tile.dy(s(YY, r)) + tile.dz(s(YZ, r)),
        tile.dx(s, XZ, r, low, high) + tile.dy(s(YZ, r)) + tile.dz(s(ZZ, r)),
    ]
    slopes = [tile.dx(s, PP, r, low, high), tile.dy(s(PP, r)), tile.dz(s(PP, r))]
    return forces, slopes


def forward_edge(tile, s, v, p, r, low, high):
    forces, slopes = momentum(tile, s, r, low, high)
    h, k, m = p(PH, r), p(PK, r), p(PM, r)
    solid, fluid, pushes = [], [], []
    for i in range(3):
        w = v(WX + i, r)
        g = -(slopes[i] + m * w)
        pushes.append(g)
        solid.append(v(VX + i, r) + h * (3.0 * forces[i] - g))
        fluid.append(w + h * (k * g - forces[i]))
    sent = [s(XX, r), s(XY, r), s(XZ, r), s(PP, r)] + solid + fluid[:1]
    return sent, solid + fluid, forces + pushes


def adjoint_stress(p, a, r):
    trace = a(XX, r) + a(YY, r) + a(ZZ, r)
    b, pi = p(PB, r), a(PP, r)
    cross = p(PA, r) * b
    common = p(PL, r) * trace - cross * pi
    s = p(PS, r)
    s2 = 2.0 * s
    return {
        XX: common + s2 * a(XX, r),
        YY: common + s2 * a(YY, r),
        ZZ: common + s2 * a(ZZ, r),
        YZ: s * a(YZ, r),
        XZ: s * a(XZ, r),
        XY: s * a(XY, r),
        PP: cross * trace - b * pi,
    }


def adjoint_edge(tile, q, a, p, r, low, high):
    forces, slopes = momentum(tile, q, r, low, high)
    h, k = p(PH, r), p(PK, r)
    lv = [a(VX + i, r) - forces[i] for i in range(3)]
    lw = [a(WX + i, r) - slopes[i] for i in range(3)]
    sent = [q(XX, r), q(XY, r), q(XZ, r), q(PP, r)]
    sent += [h * (3.0 * lv[i] - lw[i]) for i in range(3)] + [h * (k * lw[0] - lv[0])]
    return sent, lv + lw


class Side:
    def __init__(self, axis, swap, rows):
        at, size = lax.axis_index(axis), lax.axis_size(axis)
        self.last = lax.rem(at, 2) == swap
        self.met = jnp.where(self.last, at < size - 1, at > 0)
        self.base = jnp.where(self.last, rows - 1, 0)
        self.step = jnp.where(self.last, -1, 1)
        self.flip = jnp.where(self.last, -1.0, 1.0)

    def row(self, r):
        return self.base + self.step * r

    def near(self, r):
        return jnp.where(self.last, 4 - r, r - 1)


def receive(tile, side, msg, count, reach):
    tiles = [jnp.where(side.met, msg[n], 0.0) for n in range(msg.shape[0])]
    return [W(tiles[n], tile.unpack(tiles[count:], n, reach)) for n in range(count)]


def start_kernel(halo, my_axis, inputs, outs, scratch):
    par_hbm, (mask_hbm, index_hbm, table_hbm), rest_hbm = inputs[:7], inputs[7:10], inputs[10:]
    p_ref, a_ref, b_ref, *rest = outs
    par_ref, mask_ref, index_ref, table_ref, sems = scratch
    fields_ref, cot_ref = rest[:2]
    copies = [pltpu.make_async_copy(src, par_ref.at[n], sems.at[n]) for n, src in enumerate(par_hbm)]
    for src, dst in zip((table_hbm, mask_hbm, index_hbm, *rest_hbm), (table_ref, mask_ref, index_ref, *rest)):
        copies.append(pltpu.make_async_copy(src, dst, sems.at[len(copies)]))
    for copy in copies:
        copy.start()
    for copy in copies[:10]:
        copy.wait()

    even = lax.rem(lax.axis_index(my_axis), 2) == 0
    rows = p_ref.shape[1]
    planes, columns = p_ref.shape[2], p_ref.shape[3]
    lane = lax.broadcasted_iota(jnp.int32, (planes, columns), 1)
    group = lane // halo
    per = columns // halo

    def at(r):
        return pl.ds(r, planes, stride=rows)

    for r in range(rows):
        density, fluid, mobility, lame, shear, modulus, coupling = [par_ref[n, 0, at(r), :] for n in range(7)]
        lookup = jnp.zeros((planes, columns), jnp.float32)
        index = index_ref[0, at(r), :]
        for n in range(table_ref.shape[1]):
            lookup = jnp.where(index == n, table_ref[0, n], lookup)
        p_ref[PH, r] = 0.25 / (3.0 * density - fluid)
        p_ref[PK, r] = density / fluid
        p_ref[PM, r] = 2.0 * mobility
        p_ref[PL, r] = 0.25 * lame
        p_ref[PS, r] = 0.25 * shear
        p_ref[PB, r] = 0.25 * modulus
        p_ref[PA, r] = coupling
        p_ref[PF, r] = 1.0 - mask_ref[0, at(r), :].astype(jnp.float32) * lookup
    sources = []
    for f in range(p_ref.shape[0]):
        for r in range(rows):
            sources.append(lambda f=f, r=r: p_ref[f, r])
    for ref in (fields_ref, cot_ref):
        for f in range(ref.shape[0]):
            for r in range(rows):
                sources.append(lambda ref=ref, f=f, r=r: ref[f, at(r), :])
    waited = False
    for n in range(a_ref.shape[0]):
        if (n + 1) * per > p_ref.shape[0] * rows and not waited:
            for copy in copies[10:]:
                copy.wait()
            waited = True
        left = jnp.zeros((planes, columns), jnp.float32)
        right = left
        for g in range(per):
            if n * per + g < len(sources):
                x = sources[n * per + g]()
                left = jnp.where(group == g, roll(x, halo * g, 1), left)
                right = jnp.where(group == g, roll(x, halo * g + halo, 1), right)
        a_ref[n] = jnp.where(even, right, left)
        b_ref[n] = jnp.where(even, left, right)


def inject_kernel(halo, gx_axis, gy_axis, rec_ref, cot_ref, src_ref, amp_ref, rec_out, src_out):
    for cells_ref, amounts_ref, out in ((rec_ref, cot_ref, rec_out), (src_ref, amp_ref, src_out)):
        steps, rows, planes2, columns = out.shape
        planes = planes2 // 2
        count = amounts_ref.shape[1]
        total_x, total_y = rows * lax.axis_size(gx_axis), columns * lax.axis_size(gy_axis)
        cells = cells_ref[...]
        line = lax.div(cells, jnp.full_like(cells, total_y))
        depth = lax.div(line, jnp.full_like(cells, total_x))
        col = cells - line * total_y - lax.axis_index(gy_axis) * columns
        x = line - depth * total_x - lax.axis_index(gx_axis) * rows
        row = jnp.where((x >= 0) & (x < rows), x * planes + depth, -1)
        row_at = lax.broadcasted_iota(jnp.int32, (rows * planes, count), 0)
        here = row_at == row
        lhs = jnp.concatenate([jnp.where(here, amounts_ref[t : t + 1, :], 0.0) for t in range(steps)], axis=0)
        lane = lax.broadcasted_iota(jnp.int32, (columns, count), 0)
        side = jnp.where(lane < halo, lane + columns, jnp.where(lane >= columns - halo, lane - columns, -columns))
        for half, where in enumerate((lane, side)):
            rhs = (where == col).astype(jnp.float32)
            got = lax.dot_general(
                lhs, rhs, (((1,), (1,)), ((), ())), precision=lax.Precision.HIGHEST, preferred_element_type=jnp.float32
            )
            for t in range(steps):
                for r in range(rows):
                    base = (t * rows + r) * planes
                    out[t, r, pl.ds(half * planes, planes)] = got[base : base + planes]


def spreader(halo, gy_axis, ay_ref, by_ref, rows, tile):
    at_y = lax.axis_index(gy_axis)
    even_y = lax.rem(at_y, 2) == 0
    columns = tile.columns
    per = columns // halo
    on_right = (tile.lane < halo) & (at_y < lax.axis_size(gy_axis) - 1)
    on_left = (tile.lane >= columns - halo) & (at_y > 0)

    @memo
    def packs(n):
        a, b = ay_ref[n], by_ref[n]
        return jnp.where(even_y, a, b), jnp.where(even_y, b, a)

    def side(f, r):
        n = f * rows + r
        g = n % per
        right, left = packs(n // per)
        a, b = roll(right, -halo * g, 1), roll(left, -halo * (g + 1), 1)
        return jnp.where(on_right, a, jnp.where(on_left, b, 0.0))

    return side


STRESS = (XX, YY, ZZ, YZ, XZ, XY, PP)
SLOT = {XX: 0, XY: 1, XZ: 2, PP: 3}


def whole(mid, ends, axis, rows):
    last = lax.rem(lax.axis_index(axis), 2) == 0

    @memo
    def get(f, r):
        if 2 <= r < rows - 2:
            return read(mid, f, r - 2)
        top = r >= rows - 2
        at = rows - 1 - r if top else r
        a, b = read(ends[0], f, at), read(ends[1], f, at)
        if not top:
            a, b = b, a
        return W(jnp.where(last, a.m, b.m), jnp.where(last, a.h, b.h))

    return get


def message(tile, side, reach, s, a, p, msg, part_f, part_g, part_a, with_params):
    qs = memo(lambda r: adjoint_stress(p, a, r))
    q = lambda f, r: qs(r)[f]
    got, new, drives = forward_edge(tile, s, s, p, 0, False, True)
    more, lam = adjoint_edge(tile, q, a, p, 0, False, True)
    for m in range(6):
        write(part_f, new[m], m)
        part_g[m] = drives[m].m
        write(part_a, lam[m], m)
    got = got + more + ([p(PH, 0), p(PK, 0)] if with_params else [])
    for n, x in enumerate([w.m for w in got] + tile.pack([w.h for w in got], reach)):
        msg[n] = x


def spread_kernel(halo, gx_axis, gy_axis, fields_ref, cot_ref, pm_ref, ay_ref, by_ref, rec_ref, p_out, f_mid, a_mid, *outs):
    rows, planes, columns = pm_ref.shape[1:]
    tile = Tile(planes, columns, halo)
    side = spreader(halo, gy_axis, ay_ref, by_ref, rows, tile)
    base, count = p_out.shape[0], fields_ref.shape[0]
    for f in range(base):
        for r in range(rows):
            write(p_out, W(pm_ref[f, r], side(f, r)), f, r)
    ends = [Side(gx_axis, swap, rows) for swap in (0, 1)]
    groups = outs[:6], outs[6:]
    for f in range(count):
        for which, mid in enumerate((f_mid, a_mid)):
            values = []
            for r in range(rows):
                at = pl.ds(r, planes, stride=rows)
                if which:
                    value = W(cot_ref[f, at, :], side(base + count + f, r))
                    if f == PP:
                        value = value + read(rec_ref, rec_ref.shape[0] - 1, r)
                    values.append(value * read(p_out, PF, r))
                else:
                    values.append(W(fields_ref[f, at, :], side(base + f, r)))
            for r in range(2, rows - 2):
                write(mid, values[r], f, r - 2)
            for end, group in zip(ends, groups):
                for r in range(2):
                    x, y = values[rows - 1 - r], values[r]
                    write(group[which], W(jnp.where(end.last, x.m, y.m), jnp.where(end.last, x.h, y.h)), f, r)
    for end, group in zip(ends, groups):
        local = Tile(planes, columns, halo, end.flip)
        s, a = (lambda f, r, ref=ref: read(ref, f, r) for ref in group[:2])
        p = lambda f, r, end=end: read(p_out, f, end.row(r))
        message(local, end, halo, s, a, p, *group[2:], True)


def sums(ff, aa):
    fo, pu, wo, ee, gg, w_ = ff[0:3], ff[3:6], ff[6:9], ff[9:12], ff[12:15], ff[15]
    af, ag, sg, pi = aa[0:3], aa[3:6], aa[6:12], aa[12]
    tr, dd = sg[0] + sg[1] + sg[2], ee[0] + ee[1] + ee[2]
    dot = lambda x, y: x[0] * y[0] + x[1] * y[1] + x[2] * y[2]
    return [
        dot(af, fo), dot(ag, pu), dot(af, pu), dot(ag, wo),
        tr * dd, tr * w_, 2.0 * dot(sg[0:3], ee) + dot(sg[3:6], gg), pi * dd, pi * w_,
    ]


def kept_rows(refs, rows, r):
    vel, strain, cot, sig = refs
    return (
        [vel[n, r - 1] for n in range(9)] + [strain[n, r - 2] for n in range(7)],
        [cot[n, r - 1] for n in range(6)] + [sig[n, r] for n in range(7)],
    )


def kept_end(refs, end_refs, side, r):
    vel, _, cot, sig = refs
    vel_end, strain_end, cot_end = end_refs
    at = side.row(r)
    first, third = (vel_end, cot_end) if r == 0 else (vel, cot)
    where = (lambda n, ref: ref[n]) if r == 0 else (lambda n, ref: ref[n, at - 1])
    return (
        [where(n, first) for n in range(9)] + [strain_end[n, r] for n in range(7)],
        [where(n, third) for n in range(6)] + [sig[n, at] for n in range(7)],
    )


def sums_kernel(axis, rows, count, *refs):
    out_mid, out_a, out_b = refs[-3:]
    pairs = [(refs[n : n + 10], refs[n + 10 : n + 20]) for n in range(0, 20 * count, 20)]
    def total(pick):
        acc = [0.0] * 9
        for fwd, adj in pairs:
            acc = [x + y for x, y in zip(acc, sums(pick(fwd)[0], pick(adj)[1]))]
        return acc
    for r in range(2, rows - 2):
        for n, x in enumerate(total(lambda refs: kept_rows(refs[:4], rows, r))):
            out_mid[n, r - 2] = x
    for swap, out in enumerate((out_a, out_b)):
        side = Side(axis, swap, rows)
        for r in range(2):
            for n, x in enumerate(total(lambda refs: kept_end(refs[:4], refs[4 + 3 * swap : 7 + 3 * swap], side, r))):
                out[n, r] = x


def gradients(acc, p, r):
    a1, a2, a3, a4, b1, b2, b3, b4, b5 = acc
    h, k, b, al = [p(n, r).m for n in (PH, PK, PB, PA)]
    h4 = 4.0 * h
    return [
        h4 * (a3 - 3.0 * a1),
        h4 * (a1 + a2 - k * (3.0 * a2 + a3)),
        -2.0 * a4,
        0.25 * b1,
        0.25 * b3,
        0.25 * (al * (b2 - b4) - b5),
        b * (b2 - b4),
    ]


def strains(tile, v, r):
    e = [tile.dx(v, VX, r), tile.dy(v(VY, r)), tile.dz(v(VZ, r))]
    g = [
        tile.dz(v(VY, r)) + tile.dy(v(VZ, r)),
        tile.dz(v(VX, r)) + tile.dx(v, VZ, r),
        tile.dy(v(VX, r)) + tile.dx(v, VY, r),
    ]
    return e, g, tile.dx(v, WX, r) + tile.dy(v(WY, r)) + tile.dz(v(WZ, r))


def new_fields(p, old, v, e, g, dw, source, r):
    dv = e[0] + e[1] + e[2]
    sh, b = p(PS, r), p(PB, r)
    ab = p(PA, r) * b
    common = p(PL, r) * dv + ab * dw
    new = {f: v(f, r) for f in range(6)}
    for i in range(3):
        new[XX + i] = old(XX + i, r) + (common + 2.0 * (sh * e[i]))
        new[YZ + i] = old(YZ + i, r) + sh * g[i]
    new[PP] = old(PP, r) - (ab * dv + b * dw) + source
    factor = p(PF, r)
    return {f: value * factor for f, value in new.items()}


def back_fields(tile, lam, c, vel, r):
    out = dict(vel)
    out[XX] = lam(XX, r) - tile.dx(c, 0, r)
    out[YY] = lam(YY, r) - tile.dy(c(1, r))
    out[ZZ] = lam(ZZ, r) - tile.dz(c(2, r))
    out[YZ] = lam(YZ, r) - (tile.dz(c(1, r)) + tile.dy(c(2, r)))
    out[XZ] = lam(XZ, r) - (tile.dz(c(0, r)) + tile.dx(c, 2, r))
    out[XY] = lam(XY, r) - (tile.dy(c(0, r)) + tile.dx(c, 1, r))
    out[PP] = lam(PP, r) + (tile.dx(c, 3, r) + tile.dy(c(4, r)) + tile.dz(c(5, r)))
    return out


def push_cots(p, r, lv, lw):
    h, k, m = p(PH, r), p(PK, r), p(PM, r)
    cf = [h * (3.0 * lv[i] - lw[i]) for i in range(3)]
    cg = [h * (k * lw[i] - lv[i]) for i in range(3)]
    vel = {VX + i: lv[i] for i in range(3)} | {WX + i: lw[i] - m * cg[i] for i in range(3)}
    return cf + cg, vel


def near(rows):
    return (1, 2, rows - 3, rows - 2)


def interior_kernel(gx_axis, halo, j, steps, *refs):
    refs = list(refs)
    take = lambda n: [refs.pop(0) for _ in range(n)]
    final = j == steps - 1
    f_mid, fa, fb, a_mid, aa, ab, p_ref = take(7)
    if final:
        kept, (acc_ref,) = take(4), take(1)
        grad_out, par_out = take(2)
    else:
        src_ref, rec_ref, f_out, a_out = take(4)
    save_vel, save_str, save_cot, save_sig = take(4)
    v_near, c_near, l_near = take(3)
    assert not refs
    rows, planes, columns = p_ref.shape[1], p_ref.shape[2] // 2, p_ref.shape[3]
    tile = Tile(planes, columns, halo)
    p = lambda f, r: read(p_ref, f, r)
    old, lam = whole(f_mid, (fa, fb), gx_axis, rows), whole(a_mid, (aa, ab), gx_axis, rows)

    @memo
    def velocity(r):
        _, new, drives = forward_edge(tile, old, old, p, r, True, True)
        return new, [x.m for x in drives] + [old(WX + i, r).m for i in range(3)]

    qs = memo(lambda r: adjoint_stress(p, lam, r))
    q = lambda f, r: qs(r)[f]

    @memo
    def cots(r):
        forces, slopes = momentum(tile, q, r)
        return push_cots(
            p, r, [lam(VX + i, r) - forces[i] for i in range(3)], [lam(WX + i, r) - slopes[i] for i in range(3)]
        )

    v = lambda f, r: velocity(r)[0][f]
    c = lambda i, r: cots(r)[0][i]
    for r in range(1, rows - 1):
        if r in near(rows):
            at = near(rows).index(r)
            for n in range(6):
                write(v_near, v(n, r), n, at)
                write(c_near, c(n, r), n, at)
                write(l_near, cots(r)[1][n], n, at)
        for n, x in enumerate(velocity(r)[1]):
            save_vel[n, r - 1] = x
        for n in range(6):
            save_cot[n, r - 1] = c(n, r).m
        if not 2 <= r < rows - 2:
            continue
        e, g, dw = strains(tile, v, r)
        strain = [x.m for x in e + g] + [dw.m]
        back = back_fields(tile, lam, c, cots(r)[1], r)
        if final:
            ff = velocity(r)[1] + strain
            cc = [c(n, r).m for n in range(6)] + [lam(f, r).m for f in STRESS]
            kept_f, kept_a = kept_rows(kept, rows, r)
            acc = [acc_ref[n, r - 2] + (x + y) for n, (x, y) in enumerate(zip(sums(ff, kept_a), sums(kept_f, cc)))]
            for n, x in enumerate(gradients(acc, p, r)):
                par_out[n, r - 2] = x
            for f, value in back.items():
                grad_out[f, r - 2] = value.m
            continue
        for n, x in enumerate(strain):
            save_str[n, r - 2] = x
        for f, value in new_fields(p, old, v, e, g, dw, read(src_ref, j, r), r).items():
            write(f_out, value, f, r - 2)
        back[PP] = back[PP] + read(rec_ref, steps - 2 - j, r)
        for f, value in back.items():
            write(a_out, value * p(PF, r), f, r - 2)
    for r in range(rows):
        for n, f in enumerate(STRESS):
            save_sig[n, r] = lam(f, r).m


def end_kernel(gx_axis, swap, halo, j, steps, *refs):
    refs = list(refs)
    take = lambda n: [refs.pop(0) for _ in range(n)]
    first, final = j == 0, j == steps - 1
    f_ref, a_ref, p_ref, msg_ref, part_f, part_g, part_a, v_near, c_near, l_near = take(10)
    if not first:
        (hk_ref,) = take(1)
    if final:
        kept, kept_ends, (acc_ref, now_vel) = take(4), take(3), take(2)
        if swap:
            grad_mid, par_mid, grad_other, par_other = take(4)
        grad_out, par_out = take(2)
    else:
        src_ref, rec_ref, f_out, a_out, save_vel, save_str, save_cot = take(7)
        outs = take(4)
    if first:
        (hk_out,) = take(1)
    assert not refs
    rows, planes, columns = p_ref.shape[1], p_ref.shape[2] // 2, p_ref.shape[3]
    side = Side(gx_axis, swap, rows)
    tile = Tile(planes, columns, halo, side.flip)
    got = receive(tile, side, msg_ref, 2 * EDGE + (2 if first else 0), halo - 2 * j)
    p = lambda f, r: read(p_ref, f, side.row(r))
    old, lam = (lambda f, r: read(f_ref, f, r)), (lambda f, r: read(a_ref, f, r))
    if first:
        h2, k2 = got[2 * EDGE :]
        write(hk_out, h2, 0)
        write(hk_out, k2, 1)
    else:
        h2, k2 = read(hk_ref, 0), read(hk_ref, 1)

    def add_forward(base, h, k, values):
        xx, xy, xz, pp = [h * x for x in values]
        adds = [3.0 * xx + pp, 3.0 * xy, 3.0 * xz, -(k * pp + xx), -xy, -xz]
        return [x + y for x, y in zip(base, adds)]

    qs = memo(lambda r: adjoint_stress(p, lam, r))
    near_s, near_v, near_q, near_c = [got[n : n + 4] for n in range(0, 16, 4)]
    velocities, cots, vels = {}, {}, {}
    sign = -side.flip
    velocities[0] = add_forward([read(part_f, m) for m in range(6)], p(PH, 0) * sign, p(PK, 0), near_s)
    velocities[-1] = add_forward(near_v, h2 * side.flip, k2, [old(f, 0) for f in SLOT])
    xx, xy, xz, pp = [x.m * sign for x in near_s]
    drives = [part_g[0] + xx, part_g[1] + xy, part_g[2] + xz, part_g[3] - pp, part_g[4], part_g[5]]
    drives += [old(WX + i, 0).m for i in range(3)]
    base = [read(part_a, m) for m in range(6)]
    for m in range(4):
        base[m] = base[m] - near_q[m] * sign
    cots[0], vels[0] = push_cots(p, 0, base[0:3], base[3:6])
    t = h2 * sign
    xx, xy, xz, pp = [t * qs(0)[f] for f in SLOT]
    cots[-1] = [near_c[0] + (3.0 * xx - pp), near_c[1] + 3.0 * xy, near_c[2] + 3.0 * xz, near_c[3] + (k2 * pp - xx)]
    for r in (1, 2):
        at = side.near(r)
        velocities[r] = [read(v_near, n, at) for n in range(6)]
        cots[r] = [read(c_near, n, at) for n in range(6)]
        vels[r] = {n: read(l_near, n, at) for n in range(6)}
    v = lambda f, r: velocities[r][f]
    c = lambda i, r: cots[r][i]
    finals = []
    for r in range(2):
        e, g, dw = strains(tile, v, r)
        strain = [x.m for x in e + g] + [dw.m]
        back = back_fields(tile, lam, c, vels[r], r)
        if final:
            drive = drives if r == 0 else [now_vel[n, side.row(r) - 1] for n in range(9)]
            cc = [c(n, r).m for n in range(6)] + [lam(f, r).m for f in STRESS]
            kept_f, kept_a = kept_end(kept, kept_ends, side, r)
            adds = zip(sums(drive + strain, kept_a), sums(kept_f, cc))
            acc = [acc_ref[n, r] + (x + y) for n, (x, y) in enumerate(adds)]
            finals.append(([back[f].m for f in range(len(back))], gradients(acc, p, r)))
            continue
        if r == 0:
            for n, x in enumerate(drives):
                save_vel[n] = x
            for n in range(6):
                save_cot[n] = c(n, 0).m
        for n, x in enumerate(strain):
            save_str[n, r] = x
        new = new_fields(p, old, v, e, g, dw, read(src_ref, j, side.row(r)), r)
        back[PP] = back[PP] + read(rec_ref, steps - 2 - j, side.row(r))
        factor = p(PF, r)
        for f in range(f_out.shape[0]):
            write(f_out, new[f], f, r)
            write(a_out, back[f] * factor, f, r)
    if not final:
        s, a = (lambda f, r: read(f_out, f, r)), (lambda f, r: read(a_out, f, r))
        message(tile, side, halo - 2 * (j + 1), s, a, p, *outs, False)
        return
    for which, out in enumerate((grad_out, par_out)):
        for n in range(out.shape[0]):
            if not swap:
                for r in range(2):
                    out[n, r] = finals[r][which][n]
                continue
            mid, other = ((grad_mid, grad_other), (par_mid, par_other))[which]
            for r in range(2):
                mine, its = finals[r][which][n], other[n, r]
                out[n, pl.ds(r, planes, stride=rows), :] = jnp.where(side.last, its, mine)
                out[n, pl.ds(rows - 1 - r, planes, stride=rows), :] = jnp.where(side.last, mine, its)
            for r in range(2, rows - 2):
                out[n, pl.ds(r, planes, stride=rows), :] = mid[n, r - 2]


def swaps(axis, odd):
    nx, ny = lax.axis_size("gx"), lax.axis_size("gy")
    count, other = (nx, ny) if axis == "gx" else (ny, nx)
    place = (lambda i, k: i * ny + k) if axis == "gx" else (lambda i, k: k * ny + i)
    out, met = [], set()
    for i in range(odd, count - 1, 2):
        met |= {i, i + 1}
        for k in range(other):
            out += [(place(i, k), place(i + 1, k)), (place(i + 1, k), place(i, k))]
    for i in set(range(count)) - met:
        for k in range(0, other - 1, 2):
            out += [(place(i, k), place(i, k + 1)), (place(i, k + 1), place(i, k))]
    return sorted(out)


def swap_rows(axis, number, message):
    return lax.ppermute(message, ("gx", "gy"), swaps(axis, number))


def call(kernel, outs, *args):
    shapes = [o if isinstance(o, jax.ShapeDtypeStruct) else jax.ShapeDtypeStruct(o, jnp.float32) for o in outs]
    return pl.pallas_call(
        kernel,
        out_shape=shapes,
        in_specs=[pl.BlockSpec(memory_space=pltpu.VMEM)] * len(args),
        out_specs=[pl.BlockSpec(memory_space=pltpu.VMEM)] * len(outs),
        compiler_params=pltpu.CompilerParams(vmem_limit_bytes=48 << 20),
    )(*args)


def per_device(
    fields, density, fluid_density, mobility, lame_lambda, shear_modulus, biot_modulus, biot_coef,
    region_mask, profile_index, profile_table, source_cells, source_amp, receiver_cells, field_cot, receiver_cot,
):
    planes, rows, columns = region_mask.shape
    steps = source_amp.shape[0]
    count = fields.shape[0]
    halo = 2 * steps
    assert steps > 2 and planes == 8 and columns == 128 and columns % (2 * halo) == 0 and rows > 1
    flat = lambda x: x.reshape(-1, planes * rows, columns)
    fields, field_cot = flat(fields), flat(field_cot)
    raw = [flat(x) for x in (density, fluid_density, mobility, lame_lambda, shear_modulus, biot_modulus, biot_coef)]
    packs = -(-(2 * count + 8) * rows * halo // columns)
    own, wide = (rows, planes, columns), (rows, 2 * planes, columns)

    table = profile_table[None]
    small = [receiver_cells[None], receiver_cot, source_cells[None], source_amp]
    inputs = [*raw, table, flat(region_mask), flat(profile_index), fields, field_cot, *small]
    whole = [fields, field_cot, *small]
    plane = (planes * rows, columns)

    def start(*refs):
        refs = list(refs)
        hbm = refs[:7] + refs[8:10] + refs[7:8] + refs[10:16]
        start_kernel(halo, "gy", hbm, refs[16:25], refs[25:])

    p_own, ay, by, fields, field_cot, *small = pl.pallas_call(
        start,
        out_shape=[jax.ShapeDtypeStruct(s, jnp.float32) for s in [(8, *own)] + [(packs, planes, columns)] * 2]
        + [jax.ShapeDtypeStruct(x.shape, x.dtype) for x in whole],
        in_specs=[pl.BlockSpec(memory_space=pltpu.HBM)] * 16,
        out_specs=[pl.BlockSpec(memory_space=pltpu.VMEM)] * 9,
        scratch_shapes=[
            pltpu.VMEM((7, 1, *plane), jnp.float32), pltpu.VMEM((1, *plane), jnp.int32),
            pltpu.VMEM((1, *plane), jnp.int32), pltpu.SMEM(table.shape, jnp.float32),
            pltpu.SemaphoreType.DMA((16,)),
        ],
        compiler_params=pltpu.CompilerParams(vmem_limit_bytes=48 << 20),
    )(*[pltpu.with_memory_space_constraint(x, pltpu.HBM) for x in inputs])
    ay, by = swap_rows("gy", 0, ay), swap_rows("gy", 1, by)
    rec, src = call(functools.partial(inject_kernel, halo, "gx", "gy"), [(steps, *wide)] * 2, *small)
    def tiles(n, reach):
        return n + -(-n // (columns // (2 * reach))), planes, columns

    assert rows >= 6
    w, m = wide[1:], own[1:]
    parts = [(6, *w), (6, *m), (6, *w)]
    mid, end = (count, rows - 4, *w), (count, 2, *w)
    group = [end, end, tiles(2 * EDGE + 2, halo)] + parts
    p, fm, am, *rest = call(
        functools.partial(spread_kernel, halo, "gx", "gy"), [(8, *wide), mid, mid] + group * 2,
        fields, field_cot, p_own, ay, by, rec,
    )
    ends = [rest[:6], rest[6:]]
    coming = [swap_rows("gx", swap, ends[swap][2]) for swap in (0, 1)]
    hk, kept = [[], []], []
    saves = [(9, rows - 2, *m), (7, rows - 4, *m), (6, rows - 2, *m), (7, *own)]
    nears = [(6, 4, *w)] * 3
    for j in range(steps - 1):
        fm, am, *rest = call(
            functools.partial(interior_kernel, "gx", halo, j, steps), [mid, mid] + saves + nears,
            fm, ends[0][0], ends[1][0], am, ends[0][1], ends[1][1], p, src, rec,
        )
        kept.append(rest[:4])
        near_refs = rest[4:]
        for swap in (0, 1):
            f, a, _, *part_refs = ends[swap]
            outs = [end, end, (9, *m), (7, 2, *m), (6, *m), tiles(2 * EDGE, halo - 2 * (j + 1))] + parts
            outs += [] if j else [(2, *w)]
            f, a, vel, strain, cot, message_out, *rest = call(
                functools.partial(end_kernel, "gx", swap, halo, j, steps), outs,
                f, a, p, coming[swap], *part_refs, *near_refs, *hk[swap], src, rec,
            )
            ends[swap] = [f, a, message_out, *rest[:3]]
            coming[swap] = swap_rows("gx", swap, message_out)
            hk[swap] = hk[swap] or rest[3:]
            kept[j] = kept[j] + [vel, strain, cot]
    middle = [x for t in range(1, steps - 1) for x in kept[t] + kept[steps - 1 - t]]
    accs = call(
        functools.partial(sums_kernel, "gx", rows, steps - 2), [(9, rows - 4, *m), (9, 2, *m), (9, 2, *m)], *middle
    )
    grad_mid, par_mid, vel, _, _, _, *near_refs = call(
        functools.partial(interior_kernel, "gx", halo, steps - 1, steps),
        [(count, rows - 4, *m), (7, rows - 4, *m)] + saves + nears,
        fm, ends[0][0], ends[1][0], am, ends[0][1], ends[1][1], p, *kept[0][:4], accs[0],
    )
    done = []
    for swap in (0, 1):
        f, a, _, *part_refs = ends[swap]
        outs = [(count, *plane), (7, *plane)] if swap else [(count, 2, *m), (7, 2, *m)]
        done = call(
            functools.partial(end_kernel, "gx", swap, halo, steps - 1, steps), outs,
            f, a, p, coming[swap], *part_refs, *near_refs, *hk[swap], *kept[0][:4],
            *kept[0][4 + 3 * swap : 7 + 3 * swap], accs[1 + swap], vel, *([grad_mid, par_mid] * swap), *done,
        )
    return done[0].reshape(count, planes, rows, columns), done[1].reshape(7, planes, rows, columns)


def solution(mesh):
    plane, field = P(None, "gx", "gy"), P(None, None, "gx", "gy")
    in_specs = (field,) + (plane,) * 9 + (P(),) * 4 + (field, P())
    return jax.shard_map(per_device, mesh=mesh, in_specs=in_specs, out_specs=(field, field), check_vma=False)
```

```python
import functools

import jax
import jax.numpy as jnp
from jax import lax
from jax.experimental import pallas as pl
from jax.experimental.pallas import tpu as pltpu
from jax.sharding import PartitionSpec as P


VX, VY, VZ, WX, WY, WZ, XX, YY, ZZ, YZ, XZ, XY, PP = range(13)
PH, PK, PM, PL, PS, PB, PA, PF = range(8)
EDGE = 8


class W:
    __slots__ = ("m", "h")

    def __init__(self, m, h):
        self.m, self.h = m, h

    def __add__(self, o):
        return W(self.m + o.m, self.h + o.h)

    def __sub__(self, o):
        return W(self.m - o.m, self.h - o.h)

    def __mul__(self, o):
        if isinstance(o, W):
            return W(self.m * o.m, self.h * o.h)
        return W(self.m * o, self.h * o)

    __rmul__ = __mul__

    def __neg__(self):
        return W(-self.m, -self.h)


def roll(x, shift, axis):
    shift %= x.shape[axis]
    return pltpu.roll(x, shift, axis) if shift else x


class Tile:
    def __init__(self, planes, columns, halo, flip=None):
        self.flip = flip
        self.shape = (planes, columns)
        self.planes, self.columns, self.halo = planes, columns, halo
        self.lane = lax.broadcasted_iota(jnp.int32, self.shape, 1)
        sub = lax.broadcasted_iota(jnp.int32, self.shape, 0)
        self.first, self.last = self.lane == 0, self.lane == columns - 1
        self.bottom, self.top = sub == 0, sub == planes - 1
        self.zero = jnp.zeros(self.shape, jnp.float32)

    def dx(self, get, name, r, low=True, high=True):
        if low and high:
            d = get(name, r + 1) - get(name, r - 1)
        else:
            d = get(name, r + 1) if high else -get(name, r - 1)
        return d if self.flip is None else self.flip * d

    def dy(self, w):
        a, b = roll(w.m, -1, 1), roll(w.h, -1, 1)
        c, d = roll(w.m, 1, 1), roll(w.h, 1, 1)
        return W(
            jnp.where(self.last, b, a) - jnp.where(self.first, d, c),
            jnp.where(self.last, a, b) - jnp.where(self.first, c, d),
        )

    def dz1(self, a):
        return jnp.where(self.top, 0.0, roll(a, -1, 0)) - jnp.where(self.bottom, 0.0, roll(a, 1, 0))

    def dz(self, w):
        return W(self.dz1(w.m), self.dz1(w.h))

    def pack(self, tiles, reach):
        width = 2 * reach
        group = self.lane // width
        out = []
        per = self.columns // width
        for base in range(0, len(tiles), per):
            total = self.zero
            for j, tile in enumerate(tiles[base : base + per]):
                total = jnp.where(group == j, roll(tile, reach + width * j, 1), total)
            out.append(total)
        return out

    def unpack(self, tiles, index, reach):
        width = 2 * reach
        per = self.columns // width
        return roll(tiles[index // per], -(reach + width * (index % per)), 1)


def read(ref, *at):
    planes = ref.shape[-2] // 2
    return W(ref[(*at, pl.ds(0, planes))], ref[(*at, pl.ds(planes, planes))])


def write(ref, value, *at):
    planes = ref.shape[-2] // 2
    ref[(*at, pl.ds(0, planes))] = value.m
    ref[(*at, pl.ds(planes, planes))] = value.h


def memo(fn):
    return functools.lru_cache(maxsize=None)(fn)


def momentum(tile, s, r, low=True, high=True):
    forces = [
        tile.dx(s, XX, r, low, high) + tile.dy(s(XY, r)) + tile.dz(s(XZ, r)),
        tile.dx(s, XY, r, low, high) + tile.dy(s(YY, r)) + tile.dz(s(YZ, r)),
        tile.dx(s, XZ, r, low, high) + tile.dy(s(YZ, r)) + tile.dz(s(ZZ, r)),
    ]
    slopes = [tile.dx(s, PP, r, low, high), tile.dy(s(PP, r)), tile.dz(s(PP, r))]
    return forces, slopes


def forward_edge(tile, s, v, p, r, low, high):
    forces, slopes = momentum(tile, s, r, low, high)
    h, k, m = p(PH, r), p(PK, r), p(PM, r)
    solid, fluid, pushes = [], [], []
    for i in range(3):
        w = v(WX + i, r)
        g = -(slopes[i] + m * w)
        pushes.append(g)
        solid.append(v(VX + i, r) + h * (3.0 * forces[i] - g))
        fluid.append(w + h * (k * g - forces[i]))
    sent = [s(XX, r), s(XY, r), s(XZ, r), s(PP, r)] + solid + fluid[:1]
    return sent, solid + fluid, forces + pushes


def adjoint_stress(p, a, r):
    trace = a(XX, r) + a(YY, r) + a(ZZ, r)
    b, pi = p(PB, r), a(PP, r)
    cross = p(PA, r) * b
    common = p(PL, r) * trace - cross * pi
    s = p(PS, r)
    s2 = 2.0 * s
    return {
        XX: common + s2 * a(XX, r),
        YY: common + s2 * a(YY, r),
        ZZ: common + s2 * a(ZZ, r),
        YZ: s * a(YZ, r),
        XZ: s * a(XZ, r),
        XY: s * a(XY, r),
        PP: cross * trace - b * pi,
    }


def adjoint_edge(tile, q, a, p, r, low, high):
    forces, slopes = momentum(tile, q, r, low, high)
    h, k = p(PH, r), p(PK, r)
    lv = [a(VX + i, r) - forces[i] for i in range(3)]
    lw = [a(WX + i, r) - slopes[i] for i in range(3)]
    sent = [q(XX, r), q(XY, r), q(XZ, r), q(PP, r)]
    sent += [h * (3.0 * lv[i] - lw[i]) for i in range(3)] + [h * (k * lw[0] - lv[0])]
    return sent, lv + lw


class Side:
    def __init__(self, axis, swap, rows):
        at, size = lax.axis_index(axis), lax.axis_size(axis)
        self.last = lax.rem(at, 2) == swap
        self.met = jnp.where(self.last, at < size - 1, at > 0)
        self.base = jnp.where(self.last, rows - 1, 0)
        self.step = jnp.where(self.last, -1, 1)
        self.flip = jnp.where(self.last, -1.0, 1.0)

    def row(self, r):
        return self.base + self.step * r

    def near(self, r):
        return jnp.where(self.last, 4 - r, r - 1)


def receive(tile, side, msg, count, reach):
    tiles = [jnp.where(side.met, msg[n], 0.0) for n in range(msg.shape[0])]
    return [W(tiles[n], tile.unpack(tiles[count:], n, reach)) for n in range(count)]


def start_kernel(halo, my_axis, inputs, outs, scratch):
    par_hbm, (mask_hbm, index_hbm, table_hbm), rest_hbm = inputs[:7], inputs[7:10], inputs[10:]
    p_ref, a_ref, b_ref, *rest = outs
    par_ref, mask_ref, index_ref, table_ref, sems = scratch
    fields_ref, cot_ref = rest[:2]
    copies = [pltpu.make_async_copy(src, par_ref.at[n], sems.at[n]) for n, src in enumerate(par_hbm)]
    for src, dst in zip((table_hbm, mask_hbm, index_hbm, *rest_hbm), (table_ref, mask_ref, index_ref, *rest)):
        copies.append(pltpu.make_async_copy(src, dst, sems.at[len(copies)]))
    for copy in copies:
        copy.start()
    for copy in copies[:10]:
        copy.wait()

    even = lax.rem(lax.axis_index(my_axis), 2) == 0
    rows = p_ref.shape[1]
    planes, columns = p_ref.shape[2], p_ref.shape[3]
    lane = lax.broadcasted_iota(jnp.int32, (planes, columns), 1)
    width = 2 * halo
    group = lane // width
    early = lax.rem(lane, width) < halo
    per = columns // width

    def at(r):
        return pl.ds(r, planes, stride=rows)

    for r in range(rows):
        density, fluid, mobility, lame, shear, modulus, coupling = [par_ref[n, 0, at(r), :] for n in range(7)]
        lookup = jnp.zeros((planes, columns), jnp.float32)
        index = index_ref[0, at(r), :]
        for n in range(table_ref.shape[1]):
            lookup = jnp.where(index == n, table_ref[0, n], lookup)
        p_ref[PH, r] = 0.25 / (3.0 * density - fluid)
        p_ref[PK, r] = density / fluid
        p_ref[PM, r] = 2.0 * mobility
        p_ref[PL, r] = 0.25 * lame
        p_ref[PS, r] = 0.25 * shear
        p_ref[PB, r] = 0.25 * modulus
        p_ref[PA, r] = coupling
        p_ref[PF, r] = 1.0 - mask_ref[0, at(r), :].astype(jnp.float32) * lookup
    sources = []
    for f in range(p_ref.shape[0]):
        for r in range(rows):
            sources.append(lambda f=f, r=r: p_ref[f, r])
    for ref in (fields_ref, cot_ref):
        for f in range(ref.shape[0]):
            for r in range(rows):
                sources.append(lambda ref=ref, f=f, r=r: ref[f, at(r), :])
    zero = jnp.zeros((planes, columns), jnp.float32)

    def edges(n):
        total = zero
        for g, source in enumerate(sources[n * per : (n + 1) * per]):
            total = jnp.where(group == g, roll(source(), halo + width * g, 1), total)
        return total

    waited = False
    for n in range(a_ref.shape[0]):
        if (n + 1) * 2 * per > p_ref.shape[0] * rows and not waited:
            for copy in copies[10:]:
                copy.wait()
            waited = True
        x, y = edges(2 * n), edges(2 * n + 1)
        right = jnp.where(early, x, roll(y, halo, 1))
        left = jnp.where(early, roll(x, -halo, 1), y)
        a_ref[n] = jnp.where(even, right, left)
        b_ref[n] = jnp.where(even, left, right)


def inject_kernel(halo, gx_axis, gy_axis, rec_ref, cot_ref, src_ref, amp_ref, rec_out, src_out):
    for cells_ref, amounts_ref, out in ((rec_ref, cot_ref, rec_out), (src_ref, amp_ref, src_out)):
        steps, rows, planes2, columns = out.shape
        planes = planes2 // 2
        count = amounts_ref.shape[1]
        total_x, total_y = rows * lax.axis_size(gx_axis), columns * lax.axis_size(gy_axis)
        cells = cells_ref[...]
        line = lax.div(cells, jnp.full_like(cells, total_y))
        depth = lax.div(line, jnp.full_like(cells, total_x))
        col = cells - line * total_y - lax.axis_index(gy_axis) * columns
        x = line - depth * total_x - lax.axis_index(gx_axis) * rows
        row = jnp.where((x >= 0) & (x < rows), x * planes + depth, -1)
        row_at = lax.broadcasted_iota(jnp.int32, (rows * planes, count), 0)
        here = row_at == row
        lhs = jnp.concatenate([jnp.where(here, amounts_ref[t : t + 1, :], 0.0) for t in range(steps)], axis=0)
        lane = lax.broadcasted_iota(jnp.int32, (columns, count), 0)
        side = jnp.where(lane < halo, lane + columns, jnp.where(lane >= columns - halo, lane - columns, -columns))
        for half, where in enumerate((lane, side)):
            rhs = (where == col).astype(jnp.float32)
            got = lax.dot_general(
                lhs, rhs, (((1,), (1,)), ((), ())), precision=lax.Precision.HIGHEST, preferred_element_type=jnp.float32
            )
            for t in range(steps):
                for r in range(rows):
                    base = (t * rows + r) * planes
                    out[t, r, pl.ds(half * planes, planes)] = got[base : base + planes]


def spreader(halo, gy_axis, ay_ref, by_ref, rows, tile):
    at_y = lax.axis_index(gy_axis)
    even_y = lax.rem(at_y, 2) == 0
    columns, width = tile.columns, 2 * halo
    per = columns // width
    early = lax.rem(tile.lane, width) < halo
    on = ((tile.lane < halo) & (at_y < lax.axis_size(gy_axis) - 1)) | ((tile.lane >= columns - halo) & (at_y > 0))

    @memo
    def packs(n):
        a, b = ay_ref[n], by_ref[n]
        right, left = jnp.where(even_y, a, b), jnp.where(even_y, b, a)
        return jnp.where(early, left, roll(right, halo, 1)), jnp.where(early, roll(left, -halo, 1), right)

    def side(f, r):
        n = f * rows + r
        tiles = packs(n // (2 * per))
        return jnp.where(on, roll(tiles[n // per % 2], -(halo + width * (n % per)), 1), 0.0)

    return side


STRESS = (XX, YY, ZZ, YZ, XZ, XY, PP)
SLOT = {XX: 0, XY: 1, XZ: 2, PP: 3}


def whole(mid, ends, axis, rows):
    last = lax.rem(lax.axis_index(axis), 2) == 0

    @memo
    def get(f, r):
        if 2 <= r < rows - 2:
            return read(mid, f, r - 2)
        top = r >= rows - 2
        at = rows - 1 - r if top else r
        a, b = read(ends[0], f, at), read(ends[1], f, at)
        if not top:
            a, b = b, a
        return W(jnp.where(last, a.m, b.m), jnp.where(last, a.h, b.h))

    return get


def message(tile, side, reach, s, a, p, msg, part_f, part_g, part_a, with_params):
    qs = memo(lambda r: adjoint_stress(p, a, r))
    q = lambda f, r: qs(r)[f]
    got, new, drives = forward_edge(tile, s, s, p, 0, False, True)
    more, lam = adjoint_edge(tile, q, a, p, 0, False, True)
    for m in range(6):
        write(part_f, new[m], m)
        part_g[m] = drives[m].m
        write(part_a, lam[m], m)
    got = got + more + ([p(PH, 0), p(PK, 0)] if with_params else [])
    for n, x in enumerate([w.m for w in got] + tile.pack([w.h for w in got], reach)):
        msg[n] = x


def spread_kernel(halo, gx_axis, gy_axis, fields_ref, cot_ref, pm_ref, ay_ref, by_ref, rec_ref, p_out, f_mid, a_mid, *outs):
    rows, planes, columns = pm_ref.shape[1:]
    tile = Tile(planes, columns, halo)
    side = spreader(halo, gy_axis, ay_ref, by_ref, rows, tile)
    base, count = p_out.shape[0], fields_ref.shape[0]
    for f in range(base):
        for r in range(rows):
            write(p_out, W(pm_ref[f, r], side(f, r)), f, r)
    ends = [Side(gx_axis, swap, rows) for swap in (0, 1)]
    groups = outs[:6], outs[6:]
    for f in range(count):
        for which, mid in enumerate((f_mid, a_mid)):
            values = []
            for r in range(rows):
                at = pl.ds(r, planes, stride=rows)
                if which:
                    value = W(cot_ref[f, at, :], side(base + count + f, r))
                    if f == PP:
                        value = value + read(rec_ref, rec_ref.shape[0] - 1, r)
                    values.append(value * read(p_out, PF, r))
                else:
                    values.append(W(fields_ref[f, at, :], side(base + f, r)))
            for r in range(2, rows - 2):
                write(mid, values[r], f, r - 2)
            for end, group in zip(ends, groups):
                for r in range(2):
                    x, y = values[rows - 1 - r], values[r]
                    write(group[which], W(jnp.where(end.last, x.m, y.m), jnp.where(end.last, x.h, y.h)), f, r)
    for end, group in zip(ends, groups):
        local = Tile(planes, columns, halo, end.flip)
        s, a = (lambda f, r, ref=ref: read(ref, f, r) for ref in group[:2])
        p = lambda f, r, end=end: read(p_out, f, end.row(r))
        message(local, end, halo - 1, s, a, p, *group[2:], True)


def sums(ff, aa):
    fo, pu, wo, ee, gg, w_ = ff[0:3], ff[3:6], ff[6:9], ff[9:12], ff[12:15], ff[15]
    af, ag, sg, pi = aa[0:3], aa[3:6], aa[6:12], aa[12]
    tr, dd = sg[0] + sg[1] + sg[2], ee[0] + ee[1] + ee[2]
    dot = lambda x, y: x[0] * y[0] + x[1] * y[1] + x[2] * y[2]
    return [
        dot(af, fo), dot(ag, pu), dot(af, pu), dot(ag, wo),
        tr * dd, tr * w_, 2.0 * dot(sg[0:3], ee) + dot(sg[3:6], gg), pi * dd, pi * w_,
    ]


def kept_rows(refs, rows, r):
    vel, strain, cot, sig = refs
    return (
        [vel[n, r - 1] for n in range(9)] + [strain[n, r - 2] for n in range(7)],
        [cot[n, r - 1] for n in range(6)] + [sig[n, r] for n in range(7)],
    )


def kept_end(refs, end_refs, side, r):
    vel, _, cot, sig = refs
    vel_end, strain_end, cot_end = end_refs
    at = side.row(r)
    first, third = (vel_end, cot_end) if r == 0 else (vel, cot)
    where = (lambda n, ref: ref[n]) if r == 0 else (lambda n, ref: ref[n, at - 1])
    return (
        [where(n, first) for n in range(9)] + [strain_end[n, r] for n in range(7)],
        [where(n, third) for n in range(6)] + [sig[n, at] for n in range(7)],
    )


def sums_kernel(axis, rows, count, *refs):
    out_mid, out_a, out_b = refs[-3:]
    pairs = [(refs[n : n + 10], refs[n + 10 : n + 20]) for n in range(0, 20 * count, 20)]
    def total(pick):
        acc = [0.0] * 9
        for fwd, adj in pairs:
            acc = [x + y for x, y in zip(acc, sums(pick(fwd)[0], pick(adj)[1]))]
        return acc
    for r in range(2, rows - 2):
        for n, x in enumerate(total(lambda refs: kept_rows(refs[:4], rows, r))):
            out_mid[n, r - 2] = x
    for swap, out in enumerate((out_a, out_b)):
        side = Side(axis, swap, rows)
        for r in range(2):
            for n, x in enumerate(total(lambda refs: kept_end(refs[:4], refs[4 + 3 * swap : 7 + 3 * swap], side, r))):
                out[n, r] = x


def gradients(acc, p, r):
    a1, a2, a3, a4, b1, b2, b3, b4, b5 = acc
    h, k, b, al = [p(n, r).m for n in (PH, PK, PB, PA)]
    h4 = 4.0 * h
    return [
        h4 * (a3 - 3.0 * a1),
        h4 * (a1 + a2 - k * (3.0 * a2 + a3)),
        -2.0 * a4,
        0.25 * b1,
        0.25 * b3,
        0.25 * (al * (b2 - b4) - b5),
        b * (b2 - b4),
    ]


def strains(tile, v, r):
    e = [tile.dx(v, VX, r), tile.dy(v(VY, r)), tile.dz(v(VZ, r))]
    g = [
        tile.dz(v(VY, r)) + tile.dy(v(VZ, r)),
        tile.dz(v(VX, r)) + tile.dx(v, VZ, r),
        tile.dy(v(VX, r)) + tile.dx(v, VY, r),
    ]
    return e, g, tile.dx(v, WX, r) + tile.dy(v(WY, r)) + tile.dz(v(WZ, r))


def new_fields(p, old, v, e, g, dw, source, r):
    dv = e[0] + e[1] + e[2]
    sh, b = p(PS, r), p(PB, r)
    ab = p(PA, r) * b
    common = p(PL, r) * dv + ab * dw
    new = {f: v(f, r) for f in range(6)}
    for i in range(3):
        new[XX + i] = old(XX + i, r) + (common + 2.0 * (sh * e[i]))
        new[YZ + i] = old(YZ + i, r) + sh * g[i]
    new[PP] = old(PP, r) - (ab * dv + b * dw) + source
    factor = p(PF, r)
    return {f: value * factor for f, value in new.items()}


def back_fields(tile, lam, c, vel, r):
    out = dict(vel)
    out[XX] = lam(XX, r) - tile.dx(c, 0, r)
    out[YY] = lam(YY, r) - tile.dy(c(1, r))
    out[ZZ] = lam(ZZ, r) - tile.dz(c(2, r))
    out[YZ] = lam(YZ, r) - (tile.dz(c(1, r)) + tile.dy(c(2, r)))
    out[XZ] = lam(XZ, r) - (tile.dz(c(0, r)) + tile.dx(c, 2, r))
    out[XY] = lam(XY, r) - (tile.dy(c(0, r)) + tile.dx(c, 1, r))
    out[PP] = lam(PP, r) + (tile.dx(c, 3, r) + tile.dy(c(4, r)) + tile.dz(c(5, r)))
    return out


def push_cots(p, r, lv, lw):
    h, k, m = p(PH, r), p(PK, r), p(PM, r)
    cf = [h * (3.0 * lv[i] - lw[i]) for i in range(3)]
    cg = [h * (k * lw[i] - lv[i]) for i in range(3)]
    vel = {VX + i: lv[i] for i in range(3)} | {WX + i: lw[i] - m * cg[i] for i in range(3)}
    return cf + cg, vel


def near(rows):
    return (1, 2, rows - 3, rows - 2)


def interior_kernel(gx_axis, halo, j, steps, *refs):
    refs = list(refs)
    take = lambda n: [refs.pop(0) for _ in range(n)]
    final = j == steps - 1
    f_mid, fa, fb, a_mid, aa, ab, p_ref = take(7)
    if final:
        kept, (acc_ref,) = take(4), take(1)
        grad_out, par_out = take(2)
    else:
        src_ref, rec_ref, f_out, a_out = take(4)
    save_vel, save_str, save_cot, save_sig = take(4)
    v_near, c_near, l_near = take(3)
    assert not refs
    rows, planes, columns = p_ref.shape[1], p_ref.shape[2] // 2, p_ref.shape[3]
    tile = Tile(planes, columns, halo)
    p = lambda f, r: read(p_ref, f, r)
    old, lam = whole(f_mid, (fa, fb), gx_axis, rows), whole(a_mid, (aa, ab), gx_axis, rows)

    @memo
    def velocity(r):
        _, new, drives = forward_edge(tile, old, old, p, r, True, True)
        return new, [x.m for x in drives] + [old(WX + i, r).m for i in range(3)]

    qs = memo(lambda r: adjoint_stress(p, lam, r))
    q = lambda f, r: qs(r)[f]

    @memo
    def cots(r):
        forces, slopes = momentum(tile, q, r)
        return push_cots(
            p, r, [lam(VX + i, r) - forces[i] for i in range(3)], [lam(WX + i, r) - slopes[i] for i in range(3)]
        )

    v = lambda f, r: velocity(r)[0][f]
    c = lambda i, r: cots(r)[0][i]
    for r in range(1, rows - 1):
        if r in near(rows):
            at = near(rows).index(r)
            for n in range(6):
                write(v_near, v(n, r), n, at)
                write(c_near, c(n, r), n, at)
                write(l_near, cots(r)[1][n], n, at)
        for n, x in enumerate(velocity(r)[1]):
            save_vel[n, r - 1] = x
        for n in range(6):
            save_cot[n, r - 1] = c(n, r).m
        if not 2 <= r < rows - 2:
            continue
        e, g, dw = strains(tile, v, r)
        strain = [x.m for x in e + g] + [dw.m]
        back = back_fields(tile, lam, c, cots(r)[1], r)
        if final:
            ff = velocity(r)[1] + strain
            cc = [c(n, r).m for n in range(6)] + [lam(f, r).m for f in STRESS]
            kept_f, kept_a = kept_rows(kept, rows, r)
            acc = [acc_ref[n, r - 2] + (x + y) for n, (x, y) in enumerate(zip(sums(ff, kept_a), sums(kept_f, cc)))]
            for n, x in enumerate(gradients(acc, p, r)):
                par_out[n, r - 2] = x
            for f, value in back.items():
                grad_out[f, r - 2] = value.m
            continue
        for n, x in enumerate(strain):
            save_str[n, r - 2] = x
        for f, value in new_fields(p, old, v, e, g, dw, read(src_ref, j, r), r).items():
            write(f_out, value, f, r - 2)
        back[PP] = back[PP] + read(rec_ref, steps - 2 - j, r)
        for f, value in back.items():
            write(a_out, value * p(PF, r), f, r - 2)
    for r in range(rows):
        for n, f in enumerate(STRESS):
            save_sig[n, r] = lam(f, r).m


def end_kernel(gx_axis, swap, halo, j, steps, *refs):
    refs = list(refs)
    take = lambda n: [refs.pop(0) for _ in range(n)]
    first, final = j == 0, j == steps - 1
    f_ref, a_ref, p_ref, msg_ref, part_f, part_g, part_a, v_near, c_near, l_near = take(10)
    if not first:
        (hk_ref,) = take(1)
    if final:
        kept, kept_ends, (acc_ref, now_vel) = take(4), take(3), take(2)
        if swap:
            grad_mid, par_mid, grad_other, par_other = take(4)
        grad_out, par_out = take(2)
    else:
        src_ref, rec_ref, f_out, a_out, save_vel, save_str, save_cot = take(7)
        outs = take(4)
    if first:
        (hk_out,) = take(1)
    assert not refs
    rows, planes, columns = p_ref.shape[1], p_ref.shape[2] // 2, p_ref.shape[3]
    side = Side(gx_axis, swap, rows)
    tile = Tile(planes, columns, halo, side.flip)
    got = receive(tile, side, msg_ref, 2 * EDGE + (2 if first else 0), halo - 1 - 2 * j)
    p = lambda f, r: read(p_ref, f, side.row(r))
    old, lam = (lambda f, r: read(f_ref, f, r)), (lambda f, r: read(a_ref, f, r))
    if first:
        h2, k2 = got[2 * EDGE :]
        write(hk_out, h2, 0)
        write(hk_out, k2, 1)
    else:
        h2, k2 = read(hk_ref, 0), read(hk_ref, 1)

    def add_forward(base, h, k, values):
        xx, xy, xz, pp = [h * x for x in values]
        adds = [3.0 * xx + pp, 3.0 * xy, 3.0 * xz, -(k * pp + xx), -xy, -xz]
        return [x + y for x, y in zip(base, adds)]

    qs = memo(lambda r: adjoint_stress(p, lam, r))
    near_s, near_v, near_q, near_c = [got[n : n + 4] for n in range(0, 16, 4)]
    velocities, cots, vels = {}, {}, {}
    sign = -side.flip
    velocities[0] = add_forward([read(part_f, m) for m in range(6)], p(PH, 0) * sign, p(PK, 0), near_s)
    velocities[-1] = add_forward(near_v, h2 * side.flip, k2, [old(f, 0) for f in SLOT])
    xx, xy, xz, pp = [x.m * sign for x in near_s]
    drives = [part_g[0] + xx, part_g[1] + xy, part_g[2] + xz, part_g[3] - pp, part_g[4], part_g[5]]
    drives += [old(WX + i, 0).m for i in range(3)]
    base = [read(part_a, m) for m in range(6)]
    for m in range(4):
        base[m] = base[m] - near_q[m] * sign
    cots[0], vels[0] = push_cots(p, 0, base[0:3], base[3:6])
    t = h2 * sign
    xx, xy, xz, pp = [t * qs(0)[f] for f in SLOT]
    cots[-1] = [near_c[0] + (3.0 * xx - pp), near_c[1] + 3.0 * xy, near_c[2] + 3.0 * xz, near_c[3] + (k2 * pp - xx)]
    for r in (1, 2):
        at = side.near(r)
        velocities[r] = [read(v_near, n, at) for n in range(6)]
        cots[r] = [read(c_near, n, at) for n in range(6)]
        vels[r] = {n: read(l_near, n, at) for n in range(6)}
    v = lambda f, r: velocities[r][f]
    c = lambda i, r: cots[r][i]
    finals = []
    for r in range(2):
        e, g, dw = strains(tile, v, r)
        strain = [x.m for x in e + g] + [dw.m]
        back = back_fields(tile, lam, c, vels[r], r)
        if final:
            drive = drives if r == 0 else [now_vel[n, side.row(r) - 1] for n in range(9)]
            cc = [c(n, r).m for n in range(6)] + [lam(f, r).m for f in STRESS]
            kept_f, kept_a = kept_end(kept, kept_ends, side, r)
            adds = zip(sums(drive + strain, kept_a), sums(kept_f, cc))
            acc = [acc_ref[n, r] + (x + y) for n, (x, y) in enumerate(adds)]
            finals.append(([back[f].m for f in range(len(back))], gradients(acc, p, r)))
            continue
        if r == 0:
            for n, x in enumerate(drives):
                save_vel[n] = x
            for n in range(6):
                save_cot[n] = c(n, 0).m
        for n, x in enumerate(strain):
            save_str[n, r] = x
        new = new_fields(p, old, v, e, g, dw, read(src_ref, j, side.row(r)), r)
        back[PP] = back[PP] + read(rec_ref, steps - 2 - j, side.row(r))
        factor = p(PF, r)
        for f in range(f_out.shape[0]):
            write(f_out, new[f], f, r)
            write(a_out, back[f] * factor, f, r)
    if not final:
        s, a = (lambda f, r: read(f_out, f, r)), (lambda f, r: read(a_out, f, r))
        message(tile, side, halo - 1 - 2 * (j + 1), s, a, p, *outs, False)
        return
    for which, out in enumerate((grad_out, par_out)):
        for n in range(out.shape[0]):
            if not swap:
                for r in range(2):
                    out[n, r] = finals[r][which][n]
                continue
            mid, other = ((grad_mid, grad_other), (par_mid, par_other))[which]
            for r in range(2):
                mine, its = finals[r][which][n], other[n, r]
                out[n, pl.ds(r, planes, stride=rows), :] = jnp.where(side.last, its, mine)
                out[n, pl.ds(rows - 1 - r, planes, stride=rows), :] = jnp.where(side.last, mine, its)
            for r in range(2, rows - 2):
                out[n, pl.ds(r, planes, stride=rows), :] = mid[n, r - 2]


def swaps(axis, odd):
    nx, ny = lax.axis_size("gx"), lax.axis_size("gy")
    count, other = (nx, ny) if axis == "gx" else (ny, nx)
    place = (lambda i, k: i * ny + k) if axis == "gx" else (lambda i, k: k * ny + i)
    out, met = [], set()
    for i in range(odd, count - 1, 2):
        met |= {i, i + 1}
        for k in range(other):
            out += [(place(i, k), place(i + 1, k)), (place(i + 1, k), place(i, k))]
    for i in set(range(count)) - met:
        for k in range(0, other - 1, 2):
            out += [(place(i, k), place(i, k + 1)), (place(i, k + 1), place(i, k))]
    return sorted(out)


def swap_rows(axis, number, message):
    return lax.ppermute(message, ("gx", "gy"), swaps(axis, number))


def call(kernel, outs, *args):
    shapes = [o if isinstance(o, jax.ShapeDtypeStruct) else jax.ShapeDtypeStruct(o, jnp.float32) for o in outs]
    return pl.pallas_call(
        kernel,
        out_shape=shapes,
        in_specs=[pl.BlockSpec(memory_space=pltpu.VMEM)] * len(args),
        out_specs=[pl.BlockSpec(memory_space=pltpu.VMEM)] * len(outs),
        compiler_params=pltpu.CompilerParams(vmem_limit_bytes=48 << 20),
    )(*args)


def per_device(
    fields, density, fluid_density, mobility, lame_lambda, shear_modulus, biot_modulus, biot_coef,
    region_mask, profile_index, profile_table, source_cells, source_amp, receiver_cells, field_cot, receiver_cot,
):
    planes, rows, columns = region_mask.shape
    steps = source_amp.shape[0]
    count = fields.shape[0]
    halo = 2 * steps
    assert steps > 2 and planes == 8 and columns == 128 and columns % (2 * halo) == 0 and rows > 1
    flat = lambda x: x.reshape(-1, planes * rows, columns)
    fields, field_cot = flat(fields), flat(field_cot)
    raw = [flat(x) for x in (density, fluid_density, mobility, lame_lambda, shear_modulus, biot_modulus, biot_coef)]
    packs = -(-(2 * count + 8) * rows * halo // columns)
    own, wide = (rows, planes, columns), (rows, 2 * planes, columns)

    table = profile_table[None]
    small = [receiver_cells[None], receiver_cot, source_cells[None], source_amp]
    inputs = [*raw, table, flat(region_mask), flat(profile_index), fields, field_cot, *small]
    whole = [fields, field_cot, *small]
    plane = (planes * rows, columns)

    def start(*refs):
        refs = list(refs)
        hbm = refs[:7] + refs[8:10] + refs[7:8] + refs[10:16]
        start_kernel(halo, "gy", hbm, refs[16:25], refs[25:])

    p_own, ay, by, fields, field_cot, *small = pl.pallas_call(
        start,
        out_shape=[jax.ShapeDtypeStruct(s, jnp.float32) for s in [(8, *own)] + [(packs, planes, columns)] * 2]
        + [jax.ShapeDtypeStruct(x.shape, x.dtype) for x in whole],
        in_specs=[pl.BlockSpec(memory_space=pltpu.HBM)] * 16,
        out_specs=[pl.BlockSpec(memory_space=pltpu.VMEM)] * 9,
        scratch_shapes=[
            pltpu.VMEM((7, 1, *plane), jnp.float32), pltpu.VMEM((1, *plane), jnp.int32),
            pltpu.VMEM((1, *plane), jnp.int32), pltpu.SMEM(table.shape, jnp.float32),
            pltpu.SemaphoreType.DMA((16,)),
        ],
        compiler_params=pltpu.CompilerParams(vmem_limit_bytes=48 << 20),
    )(*[pltpu.with_memory_space_constraint(x, pltpu.HBM) for x in inputs])
    ay, by = swap_rows("gy", 0, ay), swap_rows("gy", 1, by)
    rec, src = call(functools.partial(inject_kernel, halo, "gx", "gy"), [(steps, *wide)] * 2, *small)
    def tiles(n, reach):
        return n + -(-n // (columns // (2 * reach))), planes, columns

    assert rows >= 6
    w, m = wide[1:], own[1:]
    parts = [(6, *w), (6, *m), (6, *w)]
    mid, end = (count, rows - 4, *w), (count, 2, *w)
    group = [end, end, tiles(2 * EDGE + 2, halo - 1)] + parts
    p, fm, am, *rest = call(
        functools.partial(spread_kernel, halo, "gx", "gy"), [(8, *wide), mid, mid] + group * 2,
        fields, field_cot, p_own, ay, by, rec,
    )
    ends = [rest[:6], rest[6:]]
    coming = [swap_rows("gx", swap, ends[swap][2]) for swap in (0, 1)]
    hk, kept = [[], []], []
    saves = [(9, rows - 2, *m), (7, rows - 4, *m), (6, rows - 2, *m), (7, *own)]
    nears = [(6, 4, *w)] * 3
    for j in range(steps - 1):
        fm, am, *rest = call(
            functools.partial(interior_kernel, "gx", halo, j, steps), [mid, mid] + saves + nears,
            fm, ends[0][0], ends[1][0], am, ends[0][1], ends[1][1], p, src, rec,
        )
        kept.append(rest[:4])
        near_refs = rest[4:]
        for swap in (0, 1):
            f, a, _, *part_refs = ends[swap]
            outs = [end, end, (9, *m), (7, 2, *m), (6, *m), tiles(2 * EDGE, halo - 1 - 2 * (j + 1))] + parts
            outs += [] if j else [(2, *w)]
            f, a, vel, strain, cot, message_out, *rest = call(
                functools.partial(end_kernel, "gx", swap, halo, j, steps), outs,
                f, a, p, coming[swap], *part_refs, *near_refs, *hk[swap], src, rec,
            )
            ends[swap] = [f, a, message_out, *rest[:3]]
            coming[swap] = swap_rows("gx", swap, message_out)
            hk[swap] = hk[swap] or rest[3:]
            kept[j] = kept[j] + [vel, strain, cot]
    middle = [x for t in range(1, steps - 1) for x in kept[t] + kept[steps - 1 - t]]
    accs = call(
        functools.partial(sums_kernel, "gx", rows, steps - 2), [(9, rows - 4, *m), (9, 2, *m), (9, 2, *m)], *middle
    )
    grad_mid, par_mid, vel, _, _, _, *near_refs = call(
        functools.partial(interior_kernel, "gx", halo, steps - 1, steps),
        [(count, rows - 4, *m), (7, rows - 4, *m)] + saves + nears,
        fm, ends[0][0], ends[1][0], am, ends[0][1], ends[1][1], p, *kept[0][:4], accs[0],
    )
    done = []
    for swap in (0, 1):
        f, a, _, *part_refs = ends[swap]
        outs = [(count, *plane), (7, *plane)] if swap else [(count, 2, *m), (7, 2, *m)]
        done = call(
            functools.partial(end_kernel, "gx", swap, halo, steps - 1, steps), outs,
            f, a, p, coming[swap], *part_refs, *near_refs, *hk[swap], *kept[0][:4],
            *kept[0][4 + 3 * swap : 7 + 3 * swap], accs[1 + swap], vel, *([grad_mid, par_mid] * swap), *done,
        )
    return done[0].reshape(count, planes, rows, columns), done[1].reshape(7, planes, rows, columns)


def solution(mesh):
    plane, field = P(None, "gx", "gy"), P(None, None, "gx", "gy")
    in_specs = (field,) + (plane,) * 9 + (P(),) * 4 + (field, P())
    return jax.shard_map(per_device, mesh=mesh, in_specs=in_specs, out_specs=(field, field), check_vma=False)
```

```python
import functools

import jax
import jax.numpy as jnp
from jax import lax
from jax.experimental import pallas as pl
from jax.experimental.pallas import tpu as pltpu
from jax.sharding import PartitionSpec as P


VX, VY, VZ, WX, WY, WZ, XX, YY, ZZ, YZ, XZ, XY, PP = range(13)
PH, PK, PM, PL, PS, PB, PA, PF = range(8)
EDGE = 8


class W:
    __slots__ = ("m", "h")

    def __init__(self, m, h):
        self.m, self.h = m, h

    def __add__(self, o):
        return W(self.m + o.m, self.h + o.h)

    def __sub__(self, o):
        return W(self.m - o.m, self.h - o.h)

    def __mul__(self, o):
        if isinstance(o, W):
            return W(self.m * o.m, self.h * o.h)
        return W(self.m * o, self.h * o)

    __rmul__ = __mul__

    def __neg__(self):
        return W(-self.m, -self.h)


def roll(x, shift, axis):
    shift %= x.shape[axis]
    return pltpu.roll(x, shift, axis) if shift else x


class Tile:
    def __init__(self, planes, columns, halo, flip=None):
        self.flip = flip
        self.shape = (planes, columns)
        self.planes, self.columns, self.halo = planes, columns, halo
        self.lane = lax.broadcasted_iota(jnp.int32, self.shape, 1)
        sub = lax.broadcasted_iota(jnp.int32, self.shape, 0)
        self.first, self.last = self.lane == 0, self.lane == columns - 1
        self.bottom, self.top = sub == 0, sub == planes - 1
        self.zero = jnp.zeros(self.shape, jnp.float32)

    def dx(self, get, name, r, low=True, high=True):
        if low and high:
            d = get(name, r + 1) - get(name, r - 1)
        else:
            d = get(name, r + 1) if high else -get(name, r - 1)
        return d if self.flip is None else self.flip * d

    def dy(self, w):
        a, b = roll(w.m, -1, 1), roll(w.h, -1, 1)
        c, d = roll(w.m, 1, 1), roll(w.h, 1, 1)
        return W(
            jnp.where(self.last, b, a) - jnp.where(self.first, d, c),
            jnp.where(self.last, a, b) - jnp.where(self.first, c, d),
        )

    def dz1(self, a):
        return jnp.where(self.top, 0.0, roll(a, -1, 0)) - jnp.where(self.bottom, 0.0, roll(a, 1, 0))

    def dz(self, w):
        return W(self.dz1(w.m), self.dz1(w.h))

    def pack(self, tiles, reach):
        width = 2 * reach
        group = self.lane // width
        out = []
        per = self.columns // width
        for base in range(0, len(tiles), per):
            total = self.zero
            for j, tile in enumerate(tiles[base : base + per]):
                total = jnp.where(group == j, roll(tile, reach + width * j, 1), total)
            out.append(total)
        return out

    def unpack(self, tiles, index, reach):
        width = 2 * reach
        per = self.columns // width
        return roll(tiles[index // per], -(reach + width * (index % per)), 1)


def read(ref, *at):
    planes = ref.shape[-2] // 2
    return W(ref[(*at, pl.ds(0, planes))], ref[(*at, pl.ds(planes, planes))])


def write(ref, value, *at):
    planes = ref.shape[-2] // 2
    ref[(*at, pl.ds(0, planes))] = value.m
    ref[(*at, pl.ds(planes, planes))] = value.h


def memo(fn):
    return functools.lru_cache(maxsize=None)(fn)


def momentum(tile, s, r, low=True, high=True):
    forces = [
        tile.dx(s, XX, r, low, high) + tile.dy(s(XY, r)) + tile.dz(s(XZ, r)),
        tile.dx(s, XY, r, low, high) + tile.dy(s(YY, r)) + tile.dz(s(YZ, r)),
        tile.dx(s, XZ, r, low, high) + tile.dy(s(YZ, r)) + tile.dz(s(ZZ, r)),
    ]
    slopes = [tile.dx(s, PP, r, low, high), tile.dy(s(PP, r)), tile.dz(s(PP, r))]
    return forces, slopes


def forward_edge(tile, s, v, p, r, low, high):
    forces, slopes = momentum(tile, s, r, low, high)
    h, k, m = p(PH, r), p(PK, r), p(PM, r)
    solid, fluid, pushes = [], [], []
    for i in range(3):
        w = v(WX + i, r)
        g = -(slopes[i] + m * w)
        pushes.append(g)
        solid.append(v(VX + i, r) + h * (3.0 * forces[i] - g))
        fluid.append(w + h * (k * g - forces[i]))
    sent = [s(XX, r), s(XY, r), s(XZ, r), s(PP, r)] + solid + fluid[:1]
    return sent, solid + fluid, forces + pushes


def adjoint_stress(p, a, r):
    trace = a(XX, r) + a(YY, r) + a(ZZ, r)
    b, pi = p(PB, r), a(PP, r)
    cross = p(PA, r) * b
    common = p(PL, r) * trace - cross * pi
    s = p(PS, r)
    s2 = 2.0 * s
    return {
        XX: common + s2 * a(XX, r),
        YY: common + s2 * a(YY, r),
        ZZ: common + s2 * a(ZZ, r),
        YZ: s * a(YZ, r),
        XZ: s * a(XZ, r),
        XY: s * a(XY, r),
        PP: cross * trace - b * pi,
    }


def adjoint_edge(tile, q, a, p, r, low, high):
    forces, slopes = momentum(tile, q, r, low, high)
    h, k = p(PH, r), p(PK, r)
    lv = [a(VX + i, r) - forces[i] for i in range(3)]
    lw = [a(WX + i, r) - slopes[i] for i in range(3)]
    sent = [q(XX, r), q(XY, r), q(XZ, r), q(PP, r)]
    sent += [h * (3.0 * lv[i] - lw[i]) for i in range(3)] + [h * (k * lw[0] - lv[0])]
    return sent, lv + lw


class Side:
    def __init__(self, axis, swap, rows):
        at, size = lax.axis_index(axis), lax.axis_size(axis)
        self.last = lax.rem(at, 2) != swap
        self.met = jnp.where(self.last, at < size - 1, at > 0)
        self.base = jnp.where(self.last, rows - 1, 0)
        self.step = jnp.where(self.last, -1, 1)
        self.flip = jnp.where(self.last, -1.0, 1.0)

    def row(self, r):
        return self.base + self.step * r

    def near(self, r):
        return jnp.where(self.last, 4 - r, r - 1)


def receive(tile, side, msg, count, reach):
    tiles = [jnp.where(side.met, msg[n], 0.0) for n in range(msg.shape[0])]
    return [W(tiles[n], tile.unpack(tiles[count:], n, reach)) for n in range(count)]


def start_kernel(halo, my_axis, inputs, outs, scratch):
    par_hbm, (mask_hbm, index_hbm, table_hbm), rest_hbm = inputs[:7], inputs[7:10], inputs[10:]
    p_ref, a_ref, b_ref, *rest = outs
    par_ref, mask_ref, index_ref, table_ref, sems = scratch
    fields_ref, cot_ref = rest[:2]
    copies = [pltpu.make_async_copy(src, par_ref.at[n], sems.at[n]) for n, src in enumerate(par_hbm)]
    for src, dst in zip((table_hbm, mask_hbm, index_hbm, *rest_hbm), (table_ref, mask_ref, index_ref, *rest)):
        copies.append(pltpu.make_async_copy(src, dst, sems.at[len(copies)]))
    for copy in copies:
        copy.start()
    for copy in copies[:10]:
        copy.wait()

    even = lax.rem(lax.axis_index(my_axis), 2) == 0
    rows = p_ref.shape[1]
    planes, columns = p_ref.shape[2], p_ref.shape[3]
    lane = lax.broadcasted_iota(jnp.int32, (planes, columns), 1)
    group = lane // halo
    per = columns // halo

    def at(r):
        return pl.ds(r, planes, stride=rows)

    for r in range(rows):
        density, fluid, mobility, lame, shear, modulus, coupling = [par_ref[n, 0, at(r), :] for n in range(7)]
        lookup = jnp.zeros((planes, columns), jnp.float32)
        index = index_ref[0, at(r), :]
        for n in range(table_ref.shape[1]):
            lookup = jnp.where(index == n, table_ref[0, n], lookup)
        p_ref[PH, r] = 0.25 / (3.0 * density - fluid)
        p_ref[PK, r] = density / fluid
        p_ref[PM, r] = 2.0 * mobility
        p_ref[PL, r] = 0.25 * lame
        p_ref[PS, r] = 0.25 * shear
        p_ref[PB, r] = 0.25 * modulus
        p_ref[PA, r] = coupling
        p_ref[PF, r] = 1.0 - mask_ref[0, at(r), :].astype(jnp.float32) * lookup
    sources = []
    for f in range(p_ref.shape[0]):
        for r in range(rows):
            sources.append(lambda f=f, r=r: p_ref[f, r])
    for ref in (fields_ref, cot_ref):
        for f in range(ref.shape[0]):
            for r in range(rows):
                sources.append(lambda ref=ref, f=f, r=r: ref[f, at(r), :])
    waited = False
    for n in range(a_ref.shape[0]):
        if (n + 1) * per > p_ref.shape[0] * rows and not waited:
            for copy in copies[10:]:
                copy.wait()
            waited = True
        left = jnp.zeros((planes, columns), jnp.float32)
        right = left
        for g in range(per):
            if n * per + g < len(sources):
                x = sources[n * per + g]()
                left = jnp.where(group == g, roll(x, halo * g, 1), left)
                right = jnp.where(group == g, roll(x, halo * g + halo, 1), right)
        a_ref[n] = jnp.where(even, right, left)
        b_ref[n] = jnp.where(even, left, right)


def inject_kernel(halo, gx_axis, gy_axis, rec_ref, cot_ref, src_ref, amp_ref, rec_out, src_out):
    for cells_ref, amounts_ref, out in ((rec_ref, cot_ref, rec_out), (src_ref, amp_ref, src_out)):
        steps, rows, planes2, columns = out.shape
        planes = planes2 // 2
        count = amounts_ref.shape[1]
        total_x, total_y = rows * lax.axis_size(gx_axis), columns * lax.axis_size(gy_axis)
        cells = cells_ref[...]
        line = lax.div(cells, jnp.full_like(cells, total_y))
        depth = lax.div(line, jnp.full_like(cells, total_x))
        col = cells - line * total_y - lax.axis_index(gy_axis) * columns
        x = line - depth * total_x - lax.axis_index(gx_axis) * rows
        row = jnp.where((x >= 0) & (x < rows), x * planes + depth, -1)
        row_at = lax.broadcasted_iota(jnp.int32, (rows * planes, count), 0)
        here = row_at == row
        lhs = jnp.concatenate([jnp.where(here, amounts_ref[t : t + 1, :], 0.0) for t in range(steps)], axis=0)
        lane = lax.broadcasted_iota(jnp.int32, (columns, count), 0)
        side = jnp.where(lane < halo, lane + columns, jnp.where(lane >= columns - halo, lane - columns, -columns))
        for half, where in enumerate((lane, side)):
            rhs = (where == col).astype(jnp.float32)
            got = lax.dot_general(
                lhs, rhs, (((1,), (1,)), ((), ())), precision=lax.Precision.HIGHEST, preferred_element_type=jnp.float32
            )
            for t in range(steps):
                for r in range(rows):
                    base = (t * rows + r) * planes
                    out[t, r, pl.ds(half * planes, planes)] = got[base : base + planes]


def spreader(halo, gy_axis, ay_ref, by_ref, rows, tile):
    at_y = lax.axis_index(gy_axis)
    even_y = lax.rem(at_y, 2) == 0
    columns = tile.columns
    per = columns // halo
    on_right = (tile.lane < halo) & (at_y < lax.axis_size(gy_axis) - 1)
    on_left = (tile.lane >= columns - halo) & (at_y > 0)

    @memo
    def packs(n):
        a, b = ay_ref[n], by_ref[n]
        return jnp.where(even_y, a, b), jnp.where(even_y, b, a)

    def side(f, r):
        n = f * rows + r
        g = n % per
        right, left = packs(n // per)
        a, b = roll(right, -halo * g, 1), roll(left, -halo * (g + 1), 1)
        return jnp.where(on_right, a, jnp.where(on_left, b, 0.0))

    return side


STRESS = (XX, YY, ZZ, YZ, XZ, XY, PP)
SLOT = {XX: 0, XY: 1, XZ: 2, PP: 3}


def whole(mid, ends, axis, rows):
    last = lax.rem(lax.axis_index(axis), 2) == 1

    @memo
    def get(f, r):
        if 2 <= r < rows - 2:
            return read(mid, f, r - 2)
        top = r >= rows - 2
        at = rows - 1 - r if top else r
        a, b = read(ends[0], f, at), read(ends[1], f, at)
        if not top:
            a, b = b, a
        return W(jnp.where(last, a.m, b.m), jnp.where(last, a.h, b.h))

    return get


def message(tile, side, reach, s, a, p, msg, part_f, part_g, part_a, with_params):
    qs = memo(lambda r: adjoint_stress(p, a, r))
    q = lambda f, r: qs(r)[f]
    got, new, drives = forward_edge(tile, s, s, p, 0, False, True)
    more, lam = adjoint_edge(tile, q, a, p, 0, False, True)
    for m in range(6):
        write(part_f, new[m], m)
        part_g[m] = drives[m].m
        write(part_a, lam[m], m)
    got = got + more + ([p(PH, 0), p(PK, 0)] if with_params else [])
    for n, x in enumerate([w.m for w in got] + tile.pack([w.h for w in got], reach)):
        msg[n] = x


def spread_kernel(halo, gx_axis, gy_axis, fields_ref, cot_ref, pm_ref, ay_ref, by_ref, rec_ref, p_out, f_mid, a_mid, *outs):
    rows, planes, columns = pm_ref.shape[1:]
    tile = Tile(planes, columns, halo)
    side = spreader(halo, gy_axis, ay_ref, by_ref, rows, tile)
    base, count = p_out.shape[0], fields_ref.shape[0]
    for f in range(base):
        for r in range(rows):
            write(p_out, W(pm_ref[f, r], side(f, r)), f, r)
    ends = [Side(gx_axis, swap, rows) for swap in (0, 1)]
    groups = outs[:6], outs[6:]
    for f in range(count):
        for which, mid in enumerate((f_mid, a_mid)):
            values = []
            for r in range(rows):
                at = pl.ds(r, planes, stride=rows)
                if which:
                    value = W(cot_ref[f, at, :], side(base + count + f, r))
                    if f == PP:
                        value = value + read(rec_ref, rec_ref.shape[0] - 1, r)
                    values.append(value * read(p_out, PF, r))
                else:
                    values.append(W(fields_ref[f, at, :], side(base + f, r)))
            for r in range(2, rows - 2):
                write(mid, values[r], f, r - 2)
            for end, group in zip(ends, groups):
                for r in range(2):
                    x, y = values[rows - 1 - r], values[r]
                    write(group[which], W(jnp.where(end.last, x.m, y.m), jnp.where(end.last, x.h, y.h)), f, r)
    for end, group in zip(ends, groups):
        local = Tile(planes, columns, halo, end.flip)
        s, a = (lambda f, r, ref=ref: read(ref, f, r) for ref in group[:2])
        p = lambda f, r, end=end: read(p_out, f, end.row(r))
        message(local, end, halo, s, a, p, *group[2:], True)


def sums(ff, aa):
    fo, pu, wo, ee, gg, w_ = ff[0:3], ff[3:6], ff[6:9], ff[9:12], ff[12:15], ff[15]
    af, ag, sg, pi = aa[0:3], aa[3:6], aa[6:12], aa[12]
    tr, dd = sg[0] + sg[1] + sg[2], ee[0] + ee[1] + ee[2]
    dot = lambda x, y: x[0] * y[0] + x[1] * y[1] + x[2] * y[2]
    return [
        dot(af, fo), dot(ag, pu), dot(af, pu), dot(ag, wo),
        tr * dd, tr * w_, 2.0 * dot(sg[0:3], ee) + dot(sg[3:6], gg), pi * dd, pi * w_,
    ]


def kept_rows(refs, rows, r):
    vel, strain, cot, sig = refs
    return (
        [vel[n, r - 1] for n in range(9)] + [strain[n, r - 2] for n in range(7)],
        [cot[n, r - 1] for n in range(6)] + [sig[n, r] for n in range(7)],
    )


def kept_end(refs, end_refs, side, r):
    vel, _, cot, sig = refs
    vel_end, strain_end, cot_end = end_refs
    at = side.row(r)
    first, third = (vel_end, cot_end) if r == 0 else (vel, cot)
    where = (lambda n, ref: ref[n]) if r == 0 else (lambda n, ref: ref[n, at - 1])
    return (
        [where(n, first) for n in range(9)] + [strain_end[n, r] for n in range(7)],
        [where(n, third) for n in range(6)] + [sig[n, at] for n in range(7)],
    )


def sums_kernel(axis, rows, count, *refs):
    out_mid, out_a, out_b = refs[-3:]
    pairs = [(refs[n : n + 10], refs[n + 10 : n + 20]) for n in range(0, 20 * count, 20)]
    def total(pick):
        acc = [0.0] * 9
        for fwd, adj in pairs:
            acc = [x + y for x, y in zip(acc, sums(pick(fwd)[0], pick(adj)[1]))]
        return acc
    for r in range(2, rows - 2):
        for n, x in enumerate(total(lambda refs: kept_rows(refs[:4], rows, r))):
            out_mid[n, r - 2] = x
    for swap, out in enumerate((out_a, out_b)):
        side = Side(axis, swap, rows)
        for r in range(2):
            for n, x in enumerate(total(lambda refs: kept_end(refs[:4], refs[4 + 3 * swap : 7 + 3 * swap], side, r))):
                out[n, r] = x


def gradients(acc, p, r):
    a1, a2, a3, a4, b1, b2, b3, b4, b5 = acc
    h, k, b, al = [p(n, r).m for n in (PH, PK, PB, PA)]
    h4 = 4.0 * h
    return [
        h4 * (a3 - 3.0 * a1),
        h4 * (a1 + a2 - k * (3.0 * a2 + a3)),
        -2.0 * a4,
        0.25 * b1,
        0.25 * b3,
        0.25 * (al * (b2 - b4) - b5),
        b * (b2 - b4),
    ]


def strains(tile, v, r):
    e = [tile.dx(v, VX, r), tile.dy(v(VY, r)), tile.dz(v(VZ, r))]
    g = [
        tile.dz(v(VY, r)) + tile.dy(v(VZ, r)),
        tile.dz(v(VX, r)) + tile.dx(v, VZ, r),
        tile.dy(v(VX, r)) + tile.dx(v, VY, r),
    ]
    return e, g, tile.dx(v, WX, r) + tile.dy(v(WY, r)) + tile.dz(v(WZ, r))


def new_fields(p, old, v, e, g, dw, source, r):
    dv = e[0] + e[1] + e[2]
    sh, b = p(PS, r), p(PB, r)
    ab = p(PA, r) * b
    common = p(PL, r) * dv + ab * dw
    new = {f: v(f, r) for f in range(6)}
    for i in range(3):
        new[XX + i] = old(XX + i, r) + (common + 2.0 * (sh * e[i]))
        new[YZ + i] = old(YZ + i, r) + sh * g[i]
    new[PP] = old(PP, r) - (ab * dv + b * dw) + source
    factor = p(PF, r)
    return {f: value * factor for f, value in new.items()}


def back_fields(tile, lam, c, vel, r):
    out = dict(vel)
    out[XX] = lam(XX, r) - tile.dx(c, 0, r)
    out[YY] = lam(YY, r) - tile.dy(c(1, r))
    out[ZZ] = lam(ZZ, r) - tile.dz(c(2, r))
    out[YZ] = lam(YZ, r) - (tile.dz(c(1, r)) + tile.dy(c(2, r)))
    out[XZ] = lam(XZ, r) - (tile.dz(c(0, r)) + tile.dx(c, 2, r))
    out[XY] = lam(XY, r) - (tile.dy(c(0, r)) + tile.dx(c, 1, r))
    out[PP] = lam(PP, r) + (tile.dx(c, 3, r) + tile.dy(c(4, r)) + tile.dz(c(5, r)))
    return out


def push_cots(p, r, lv, lw):
    h, k, m = p(PH, r), p(PK, r), p(PM, r)
    cf = [h * (3.0 * lv[i] - lw[i]) for i in range(3)]
    cg = [h * (k * lw[i] - lv[i]) for i in range(3)]
    vel = {VX + i: lv[i] for i in range(3)} | {WX + i: lw[i] - m * cg[i] for i in range(3)}
    return cf + cg, vel


def near(rows):
    return (1, 2, rows - 3, rows - 2)


def interior_kernel(gx_axis, halo, j, steps, *refs):
    refs = list(refs)
    take = lambda n: [refs.pop(0) for _ in range(n)]
    final = j == steps - 1
    f_mid, fa, fb, a_mid, aa, ab, p_ref = take(7)
    if final:
        kept, (acc_ref,) = take(4), take(1)
        grad_out, par_out = take(2)
    else:
        src_ref, rec_ref, f_out, a_out = take(4)
    save_vel, save_str, save_cot, save_sig = take(4)
    v_near, c_near, l_near = take(3)
    assert not refs
    rows, planes, columns = p_ref.shape[1], p_ref.shape[2] // 2, p_ref.shape[3]
    tile = Tile(planes, columns, halo)
    p = lambda f, r: read(p_ref, f, r)
    old, lam = whole(f_mid, (fa, fb), gx_axis, rows), whole(a_mid, (aa, ab), gx_axis, rows)

    @memo
    def velocity(r):
        _, new, drives = forward_edge(tile, old, old, p, r, True, True)
        return new, [x.m for x in drives] + [old(WX + i, r).m for i in range(3)]

    qs = memo(lambda r: adjoint_stress(p, lam, r))
    q = lambda f, r: qs(r)[f]

    @memo
    def cots(r):
        forces, slopes = momentum(tile, q, r)
        return push_cots(
            p, r, [lam(VX + i, r) - forces[i] for i in range(3)], [lam(WX + i, r) - slopes[i] for i in range(3)]
        )

    v = lambda f, r: velocity(r)[0][f]
    c = lambda i, r: cots(r)[0][i]
    for r in range(1, rows - 1):
        if r in near(rows):
            at = near(rows).index(r)
            for n in range(6):
                write(v_near, v(n, r), n, at)
                write(c_near, c(n, r), n, at)
                write(l_near, cots(r)[1][n], n, at)
        for n, x in enumerate(velocity(r)[1]):
            save_vel[n, r - 1] = x
        for n in range(6):
            save_cot[n, r - 1] = c(n, r).m
        if not 2 <= r < rows - 2:
            continue
        e, g, dw = strains(tile, v, r)
        strain = [x.m for x in e + g] + [dw.m]
        back = back_fields(tile, lam, c, cots(r)[1], r)
        if final:
            ff = velocity(r)[1] + strain
            cc = [c(n, r).m for n in range(6)] + [lam(f, r).m for f in STRESS]
            kept_f, kept_a = kept_rows(kept, rows, r)
            acc = [acc_ref[n, r - 2] + (x + y) for n, (x, y) in enumerate(zip(sums(ff, kept_a), sums(kept_f, cc)))]
            for n, x in enumerate(gradients(acc, p, r)):
                par_out[n, r - 2] = x
            for f, value in back.items():
                grad_out[f, r - 2] = value.m
            continue
        for n, x in enumerate(strain):
            save_str[n, r - 2] = x
        for f, value in new_fields(p, old, v, e, g, dw, read(src_ref, j, r), r).items():
            write(f_out, value, f, r - 2)
        back[PP] = back[PP] + read(rec_ref, steps - 2 - j, r)
        for f, value in back.items():
            write(a_out, value * p(PF, r), f, r - 2)
    for r in range(rows):
        for n, f in enumerate(STRESS):
            save_sig[n, r] = lam(f, r).m


def end_kernel(gx_axis, swap, halo, j, steps, *refs):
    refs = list(refs)
    take = lambda n: [refs.pop(0) for _ in range(n)]
    first, final = j == 0, j == steps - 1
    f_ref, a_ref, p_ref, msg_ref, part_f, part_g, part_a, v_near, c_near, l_near = take(10)
    if not first:
        (hk_ref,) = take(1)
    if final:
        kept, kept_ends, (acc_ref, now_vel) = take(4), take(3), take(2)
        if swap:
            grad_mid, par_mid, grad_other, par_other = take(4)
        grad_out, par_out = take(2)
    else:
        src_ref, rec_ref, f_out, a_out, save_vel, save_str, save_cot = take(7)
        outs = take(4)
    if first:
        (hk_out,) = take(1)
    assert not refs
    rows, planes, columns = p_ref.shape[1], p_ref.shape[2] // 2, p_ref.shape[3]
    side = Side(gx_axis, swap, rows)
    tile = Tile(planes, columns, halo, side.flip)
    got = receive(tile, side, msg_ref, 2 * EDGE + (2 if first else 0), halo - 2 * j)
    p = lambda f, r: read(p_ref, f, side.row(r))
    old, lam = (lambda f, r: read(f_ref, f, r)), (lambda f, r: read(a_ref, f, r))
    if first:
        h2, k2 = got[2 * EDGE :]
        write(hk_out, h2, 0)
        write(hk_out, k2, 1)
    else:
        h2, k2 = read(hk_ref, 0), read(hk_ref, 1)

    def add_forward(base, h, k, values):
        xx, xy, xz, pp = [h * x for x in values]
        adds = [3.0 * xx + pp, 3.0 * xy, 3.0 * xz, -(k * pp + xx), -xy, -xz]
        return [x + y for x, y in zip(base, adds)]

    qs = memo(lambda r: adjoint_stress(p, lam, r))
    near_s, near_v, near_q, near_c = [got[n : n + 4] for n in range(0, 16, 4)]
    velocities, cots, vels = {}, {}, {}
    sign = -side.flip
    velocities[0] = add_forward([read(part_f, m) for m in range(6)], p(PH, 0) * sign, p(PK, 0), near_s)
    velocities[-1] = add_forward(near_v, h2 * side.flip, k2, [old(f, 0) for f in SLOT])
    xx, xy, xz, pp = [x.m * sign for x in near_s]
    drives = [part_g[0] + xx, part_g[1] + xy, part_g[2] + xz, part_g[3] - pp, part_g[4], part_g[5]]
    drives += [old(WX + i, 0).m for i in range(3)]
    base = [read(part_a, m) for m in range(6)]
    for m in range(4):
        base[m] = base[m] - near_q[m] * sign
    cots[0], vels[0] = push_cots(p, 0, base[0:3], base[3:6])
    t = h2 * sign
    xx, xy, xz, pp = [t * qs(0)[f] for f in SLOT]
    cots[-1] = [near_c[0] + (3.0 * xx - pp), near_c[1] + 3.0 * xy, near_c[2] + 3.0 * xz, near_c[3] + (k2 * pp - xx)]
    for r in (1, 2):
        at = side.near(r)
        velocities[r] = [read(v_near, n, at) for n in range(6)]
        cots[r] = [read(c_near, n, at) for n in range(6)]
        vels[r] = {n: read(l_near, n, at) for n in range(6)}
    v = lambda f, r: velocities[r][f]
    c = lambda i, r: cots[r][i]
    finals = []
    for r in range(2):
        e, g, dw = strains(tile, v, r)
        strain = [x.m for x in e + g] + [dw.m]
        back = back_fields(tile, lam, c, vels[r], r)
        if final:
            drive = drives if r == 0 else [now_vel[n, side.row(r) - 1] for n in range(9)]
            cc = [c(n, r).m for n in range(6)] + [lam(f, r).m for f in STRESS]
            kept_f, kept_a = kept_end(kept, kept_ends, side, r)
            adds = zip(sums(drive + strain, kept_a), sums(kept_f, cc))
            acc = [acc_ref[n, r] + (x + y) for n, (x, y) in enumerate(adds)]
            finals.append(([back[f].m for f in range(len(back))], gradients(acc, p, r)))
            continue
        if r == 0:
            for n, x in enumerate(drives):
                save_vel[n] = x
            for n in range(6):
                save_cot[n] = c(n, 0).m
        for n, x in enumerate(strain):
            save_str[n, r] = x
        new = new_fields(p, old, v, e, g, dw, read(src_ref, j, side.row(r)), r)
        back[PP] = back[PP] + read(rec_ref, steps - 2 - j, side.row(r))
        factor = p(PF, r)
        for f in range(f_out.shape[0]):
            write(f_out, new[f], f, r)
            write(a_out, back[f] * factor, f, r)
    if not final:
        s, a = (lambda f, r: read(f_out, f, r)), (lambda f, r: read(a_out, f, r))
        message(tile, side, halo - 2 * (j + 1), s, a, p, *outs, False)
        return
    for which, out in enumerate((grad_out, par_out)):
        for n in range(out.shape[0]):
            if not swap:
                for r in range(2):
                    out[n, r] = finals[r][which][n]
                continue
            mid, other = ((grad_mid, grad_other), (par_mid, par_other))[which]
            for r in range(2):
                mine, its = finals[r][which][n], other[n, r]
                out[n, pl.ds(r, planes, stride=rows), :] = jnp.where(side.last, its, mine)
                out[n, pl.ds(rows - 1 - r, planes, stride=rows), :] = jnp.where(side.last, mine, its)
            for r in range(2, rows - 2):
                out[n, pl.ds(r, planes, stride=rows), :] = mid[n, r - 2]


def swaps(axis, odd):
    nx, ny = lax.axis_size("gx"), lax.axis_size("gy")
    count, other = (nx, ny) if axis == "gx" else (ny, nx)
    place = (lambda i, k: i * ny + k) if axis == "gx" else (lambda i, k: k * ny + i)
    out, met = [], set()
    for i in range(odd, count - 1, 2):
        met |= {i, i + 1}
        for k in range(other):
            out += [(place(i, k), place(i + 1, k)), (place(i + 1, k), place(i, k))]
    for i in set(range(count)) - met:
        for k in range(0, other - 1, 2):
            out += [(place(i, k), place(i, k + 1)), (place(i, k + 1), place(i, k))]
    return sorted(out)


def swap_rows(axis, number, message):
    return lax.ppermute(message, ("gx", "gy"), swaps(axis, number))


def call(kernel, outs, *args):
    shapes = [o if isinstance(o, jax.ShapeDtypeStruct) else jax.ShapeDtypeStruct(o, jnp.float32) for o in outs]
    return pl.pallas_call(
        kernel,
        out_shape=shapes,
        in_specs=[pl.BlockSpec(memory_space=pltpu.VMEM)] * len(args),
        out_specs=[pl.BlockSpec(memory_space=pltpu.VMEM)] * len(outs),
        compiler_params=pltpu.CompilerParams(vmem_limit_bytes=48 << 20),
    )(*args)


def per_device(
    fields, density, fluid_density, mobility, lame_lambda, shear_modulus, biot_modulus, biot_coef,
    region_mask, profile_index, profile_table, source_cells, source_amp, receiver_cells, field_cot, receiver_cot,
):
    planes, rows, columns = region_mask.shape
    steps = source_amp.shape[0]
    count = fields.shape[0]
    halo = 2 * steps
    assert steps > 2 and planes == 8 and columns == 128 and columns % (2 * halo) == 0 and rows > 1
    flat = lambda x: x.reshape(-1, planes * rows, columns)
    fields, field_cot = flat(fields), flat(field_cot)
    raw = [flat(x) for x in (density, fluid_density, mobility, lame_lambda, shear_modulus, biot_modulus, biot_coef)]
    packs = -(-(2 * count + 8) * rows * halo // columns)
    own, wide = (rows, planes, columns), (rows, 2 * planes, columns)

    table = profile_table[None]
    small = [receiver_cells[None], receiver_cot, source_cells[None], source_amp]
    inputs = [*raw, table, flat(region_mask), flat(profile_index), fields, field_cot, *small]
    whole = [fields, field_cot, *small]
    plane = (planes * rows, columns)

    def start(*refs):
        refs = list(refs)
        hbm = refs[:7] + refs[8:10] + refs[7:8] + refs[10:16]
        start_kernel(halo, "gy", hbm, refs[16:25], refs[25:])

    p_own, ay, by, fields, field_cot, *small = pl.pallas_call(
        start,
        out_shape=[jax.ShapeDtypeStruct(s, jnp.float32) for s in [(8, *own)] + [(packs, planes, columns)] * 2]
        + [jax.ShapeDtypeStruct(x.shape, x.dtype) for x in whole],
        in_specs=[pl.BlockSpec(memory_space=pltpu.HBM)] * 16,
        out_specs=[pl.BlockSpec(memory_space=pltpu.VMEM)] * 9,
        scratch_shapes=[
            pltpu.VMEM((7, 1, *plane), jnp.float32), pltpu.VMEM((1, *plane), jnp.int32),
            pltpu.VMEM((1, *plane), jnp.int32), pltpu.SMEM(table.shape, jnp.float32),
            pltpu.SemaphoreType.DMA((16,)),
        ],
        compiler_params=pltpu.CompilerParams(vmem_limit_bytes=48 << 20),
    )(*[pltpu.with_memory_space_constraint(x, pltpu.HBM) for x in inputs])
    ay, by = swap_rows("gy", 0, ay), swap_rows("gy", 1, by)
    rec, src = call(functools.partial(inject_kernel, halo, "gx", "gy"), [(steps, *wide)] * 2, *small)
    def tiles(n, reach):
        return n + -(-n // (columns // (2 * reach))), planes, columns

    assert rows >= 6
    w, m = wide[1:], own[1:]
    parts = [(6, *w), (6, *m), (6, *w)]
    mid, end = (count, rows - 4, *w), (count, 2, *w)
    group = [end, end, tiles(2 * EDGE + 2, halo)] + parts
    p, fm, am, *rest = call(
        functools.partial(spread_kernel, halo, "gx", "gy"), [(8, *wide), mid, mid] + group * 2,
        fields, field_cot, p_own, ay, by, rec,
    )
    ends = [rest[:6], rest[6:]]
    coming = [swap_rows("gx", 1 - swap, ends[swap][2]) for swap in (0, 1)]
    hk, kept = [[], []], []
    saves = [(9, rows - 2, *m), (7, rows - 4, *m), (6, rows - 2, *m), (7, *own)]
    nears = [(6, 4, *w)] * 3
    for j in range(steps - 1):
        fm, am, *rest = call(
            functools.partial(interior_kernel, "gx", halo, j, steps), [mid, mid] + saves + nears,
            fm, ends[0][0], ends[1][0], am, ends[0][1], ends[1][1], p, src, rec,
        )
        kept.append(rest[:4])
        near_refs = rest[4:]
        for swap in (0, 1):
            f, a, _, *part_refs = ends[swap]
            outs = [end, end, (9, *m), (7, 2, *m), (6, *m), tiles(2 * EDGE, halo - 2 * (j + 1))] + parts
            outs += [] if j else [(2, *w)]
            f, a, vel, strain, cot, message_out, *rest = call(
                functools.partial(end_kernel, "gx", swap, halo, j, steps), outs,
                f, a, p, coming[swap], *part_refs, *near_refs, *hk[swap], src, rec,
            )
            ends[swap] = [f, a, message_out, *rest[:3]]
            coming[swap] = swap_rows("gx", 1 - swap, message_out)
            hk[swap] = hk[swap] or rest[3:]
            kept[j] = kept[j] + [vel, strain, cot]
    middle = [x for t in range(1, steps - 1) for x in kept[t] + kept[steps - 1 - t]]
    accs = call(
        functools.partial(sums_kernel, "gx", rows, steps - 2), [(9, rows - 4, *m), (9, 2, *m), (9, 2, *m)], *middle
    )
    grad_mid, par_mid, vel, _, _, _, *near_refs = call(
        functools.partial(interior_kernel, "gx", halo, steps - 1, steps),
        [(count, rows - 4, *m), (7, rows - 4, *m)] + saves + nears,
        fm, ends[0][0], ends[1][0], am, ends[0][1], ends[1][1], p, *kept[0][:4], accs[0],
    )
    done = []
    for swap in (0, 1):
        f, a, _, *part_refs = ends[swap]
        outs = [(count, *plane), (7, *plane)] if swap else [(count, 2, *m), (7, 2, *m)]
        done = call(
            functools.partial(end_kernel, "gx", swap, halo, steps - 1, steps), outs,
            f, a, p, coming[swap], *part_refs, *near_refs, *hk[swap], *kept[0][:4],
            *kept[0][4 + 3 * swap : 7 + 3 * swap], accs[1 + swap], vel, *([grad_mid, par_mid] * swap), *done,
        )
    return done[0].reshape(count, planes, rows, columns), done[1].reshape(7, planes, rows, columns)


def solution(mesh):
    plane, field = P(None, "gx", "gy"), P(None, None, "gx", "gy")
    in_specs = (field,) + (plane,) * 9 + (P(),) * 4 + (field, P())
    return jax.shard_map(per_device, mesh=mesh, in_specs=in_specs, out_specs=(field, field), check_vma=False)
```

```python
import functools

import jax
import jax.numpy as jnp
from jax import lax
from jax.experimental import pallas as pl
from jax.experimental.pallas import tpu as pltpu
from jax.sharding import PartitionSpec as P


VX, VY, VZ, WX, WY, WZ, XX, YY, ZZ, YZ, XZ, XY, PP = range(13)
PH, PK, PM, PL, PS, PB, PA, PF = range(8)
EDGE = 8


class W:
    __slots__ = ("m", "h")

    def __init__(self, m, h):
        self.m, self.h = m, h

    def __add__(self, o):
        return W(self.m + o.m, self.h + o.h)

    def __sub__(self, o):
        return W(self.m - o.m, self.h - o.h)

    def __mul__(self, o):
        if isinstance(o, W):
            return W(self.m * o.m, self.h * o.h)
        return W(self.m * o, self.h * o)

    __rmul__ = __mul__

    def __neg__(self):
        return W(-self.m, -self.h)


def roll(x, shift, axis):
    shift %= x.shape[axis]
    return pltpu.roll(x, shift, axis) if shift else x


class Tile:
    def __init__(self, planes, columns, halo, flip=None):
        self.flip = flip
        self.shape = (planes, columns)
        self.planes, self.columns, self.halo = planes, columns, halo
        self.lane = lax.broadcasted_iota(jnp.int32, self.shape, 1)
        sub = lax.broadcasted_iota(jnp.int32, self.shape, 0)
        self.first, self.last = self.lane == 0, self.lane == columns - 1
        self.bottom, self.top = sub == 0, sub == planes - 1
        self.zero = jnp.zeros(self.shape, jnp.float32)

    def dx(self, get, name, r, low=True, high=True):
        if low and high:
            d = get(name, r + 1) - get(name, r - 1)
        else:
            d = get(name, r + 1) if high else -get(name, r - 1)
        return d if self.flip is None else self.flip * d

    def dy(self, w):
        a, b = roll(w.m, -1, 1), roll(w.h, -1, 1)
        c, d = roll(w.m, 1, 1), roll(w.h, 1, 1)
        return W(
            jnp.where(self.last, b, a) - jnp.where(self.first, d, c),
            jnp.where(self.last, a, b) - jnp.where(self.first, c, d),
        )

    def dz1(self, a):
        return jnp.where(self.top, 0.0, roll(a, -1, 0)) - jnp.where(self.bottom, 0.0, roll(a, 1, 0))

    def dz(self, w):
        return W(self.dz1(w.m), self.dz1(w.h))

    def pack(self, tiles, reach):
        width = 2 * reach
        group = self.lane // width
        out = []
        per = self.columns // width
        for base in range(0, len(tiles), per):
            total = self.zero
            for j, tile in enumerate(tiles[base : base + per]):
                total = jnp.where(group == j, roll(tile, reach + width * j, 1), total)
            out.append(total)
        return out

    def unpack(self, tiles, index, reach):
        width = 2 * reach
        per = self.columns // width
        return roll(tiles[index // per], -(reach + width * (index % per)), 1)


def read(ref, *at):
    planes = ref.shape[-2] // 2
    return W(ref[(*at, pl.ds(0, planes))], ref[(*at, pl.ds(planes, planes))])


def write(ref, value, *at):
    planes = ref.shape[-2] // 2
    ref[(*at, pl.ds(0, planes))] = value.m
    ref[(*at, pl.ds(planes, planes))] = value.h


def memo(fn):
    return functools.lru_cache(maxsize=None)(fn)


def momentum(tile, s, r, low=True, high=True):
    forces = [
        tile.dx(s, XX, r, low, high) + tile.dy(s(XY, r)) + tile.dz(s(XZ, r)),
        tile.dx(s, XY, r, low, high) + tile.dy(s(YY, r)) + tile.dz(s(YZ, r)),
        tile.dx(s, XZ, r, low, high) + tile.dy(s(YZ, r)) + tile.dz(s(ZZ, r)),
    ]
    slopes = [tile.dx(s, PP, r, low, high), tile.dy(s(PP, r)), tile.dz(s(PP, r))]
    return forces, slopes


def forward_edge(tile, s, v, p, r, low, high):
    forces, slopes = momentum(tile, s, r, low, high)
    h, k, m = p(PH, r), p(PK, r), p(PM, r)
    solid, fluid, pushes = [], [], []
    for i in range(3):
        w = v(WX + i, r)
        g = -(slopes[i] + m * w)
        pushes.append(g)
        solid.append(v(VX + i, r) + h * (3.0 * forces[i] - g))
        fluid.append(w + h * (k * g - forces[i]))
    sent = [s(XX, r), s(XY, r), s(XZ, r), s(PP, r)] + solid + fluid[:1]
    return sent, solid + fluid, forces + pushes


def adjoint_stress(p, a, r):
    trace = a(XX, r) + a(YY, r) + a(ZZ, r)
    b, pi = p(PB, r), a(PP, r)
    cross = p(PA, r) * b
    common = p(PL, r) * trace - cross * pi
    s = p(PS, r)
    s2 = 2.0 * s
    return {
        XX: common + s2 * a(XX, r),
        YY: common + s2 * a(YY, r),
        ZZ: common + s2 * a(ZZ, r),
        YZ: s * a(YZ, r),
        XZ: s * a(XZ, r),
        XY: s * a(XY, r),
        PP: cross * trace - b * pi,
    }


def adjoint_edge(tile, q, a, p, r, low, high):
    forces, slopes = momentum(tile, q, r, low, high)
    h, k = p(PH, r), p(PK, r)
    lv = [a(VX + i, r) - forces[i] for i in range(3)]
    lw = [a(WX + i, r) - slopes[i] for i in range(3)]
    sent = [q(XX, r), q(XY, r), q(XZ, r), q(PP, r)]
    sent += [h * (3.0 * lv[i] - lw[i]) for i in range(3)] + [h * (k * lw[0] - lv[0])]
    return sent, lv + lw


class Side:
    def __init__(self, axis, swap, rows):
        at, size = lax.axis_index(axis), lax.axis_size(axis)
        self.last = lax.rem(at, 2) != swap
        self.met = jnp.where(self.last, at < size - 1, at > 0)
        self.base = jnp.where(self.last, rows - 1, 0)
        self.step = jnp.where(self.last, -1, 1)
        self.flip = jnp.where(self.last, -1.0, 1.0)

    def row(self, r):
        return self.base + self.step * r

    def near(self, r):
        return jnp.where(self.last, 4 - r, r - 1)


def receive(tile, side, msg, count, reach):
    tiles = [jnp.where(side.met, msg[n], 0.0) for n in range(msg.shape[0])]
    return [W(tiles[n], tile.unpack(tiles[count:], n, reach)) for n in range(count)]


def start_kernel(halo, my_axis, inputs, outs, scratch):
    par_hbm, (mask_hbm, index_hbm, table_hbm), rest_hbm = inputs[:7], inputs[7:10], inputs[10:]
    p_ref, a_ref, b_ref, *rest = outs
    par_ref, mask_ref, index_ref, table_ref, sems = scratch
    fields_ref, cot_ref = rest[:2]
    copies = [pltpu.make_async_copy(src, par_ref.at[n], sems.at[n]) for n, src in enumerate(par_hbm)]
    for src, dst in zip((table_hbm, mask_hbm, index_hbm, *rest_hbm), (table_ref, mask_ref, index_ref, *rest)):
        copies.append(pltpu.make_async_copy(src, dst, sems.at[len(copies)]))
    for copy in copies:
        copy.start()
    for copy in copies[:10]:
        copy.wait()

    even = lax.rem(lax.axis_index(my_axis), 2) == 0
    rows = p_ref.shape[1]
    planes, columns = p_ref.shape[2], p_ref.shape[3]
    lane = lax.broadcasted_iota(jnp.int32, (planes, columns), 1)
    group = lane // halo
    per = columns // halo

    def at(r):
        return pl.ds(r, planes, stride=rows)

    for r in range(rows):
        density, fluid, mobility, lame, shear, modulus, coupling = [par_ref[n, 0, at(r), :] for n in range(7)]
        lookup = jnp.zeros((planes, columns), jnp.float32)
        index = index_ref[0, at(r), :]
        for n in range(table_ref.shape[1]):
            lookup = jnp.where(index == n, table_ref[0, n], lookup)
        p_ref[PH, r] = 0.25 / (3.0 * density - fluid)
        p_ref[PK, r] = density / fluid
        p_ref[PM, r] = 2.0 * mobility
        p_ref[PL, r] = 0.25 * lame
        p_ref[PS, r] = 0.25 * shear
        p_ref[PB, r] = 0.25 * modulus
        p_ref[PA, r] = coupling
        p_ref[PF, r] = 1.0 - mask_ref[0, at(r), :].astype(jnp.float32) * lookup
    sources = []
    for f in range(p_ref.shape[0]):
        for r in range(rows):
            sources.append(lambda f=f, r=r: p_ref[f, r])
    for ref in (fields_ref, cot_ref):
        for f in range(ref.shape[0]):
            for r in range(rows):
                sources.append(lambda ref=ref, f=f, r=r: ref[f, at(r), :])
    waited = False
    for n in range(a_ref.shape[0]):
        if (n + 1) * per > p_ref.shape[0] * rows and not waited:
            for copy in copies[10:]:
                copy.wait()
            waited = True
        left = jnp.zeros((planes, columns), jnp.float32)
        right = left
        for g in range(per):
            if n * per + g < len(sources):
                x = sources[n * per + g]()
                left = jnp.where(group == g, roll(x, halo * g, 1), left)
                right = jnp.where(group == g, roll(x, halo * g + halo, 1), right)
        a_ref[n] = jnp.where(even, right, left)
        b_ref[n] = jnp.where(even, left, right)


def inject_kernel(halo, gx_axis, gy_axis, rec_ref, cot_ref, src_ref, amp_ref, rec_out, src_out):
    for cells_ref, amounts_ref, out in ((rec_ref, cot_ref, rec_out), (src_ref, amp_ref, src_out)):
        steps, rows, planes2, columns = out.shape
        planes = planes2 // 2
        count = amounts_ref.shape[1]
        total_x, total_y = rows * lax.axis_size(gx_axis), columns * lax.axis_size(gy_axis)
        cells = cells_ref[...]
        line = lax.div(cells, jnp.full_like(cells, total_y))
        depth = lax.div(line, jnp.full_like(cells, total_x))
        col = cells - line * total_y - lax.axis_index(gy_axis) * columns
        x = line - depth * total_x - lax.axis_index(gx_axis) * rows
        row = jnp.where((x >= 0) & (x < rows), x * planes + depth, -1)
        row_at = lax.broadcasted_iota(jnp.int32, (rows * planes, count), 0)
        here = row_at == row
        lhs = jnp.concatenate([jnp.where(here, amounts_ref[t : t + 1, :], 0.0) for t in range(steps)], axis=0)
        lane = lax.broadcasted_iota(jnp.int32, (columns, count), 0)
        side = jnp.where(lane < halo, lane + columns, jnp.where(lane >= columns - halo, lane - columns, -columns))
        for half, where in enumerate((lane, side)):
            rhs = (where == col).astype(jnp.float32)
            got = lax.dot_general(
                lhs, rhs, (((1,), (1,)), ((), ())), precision=lax.Precision.HIGHEST, preferred_element_type=jnp.float32
            )
            for t in range(steps):
                for r in range(rows):
                    base = (t * rows + r) * planes
                    out[t, r, pl.ds(half * planes, planes)] = got[base : base + planes]


def spreader(halo, gy_axis, ay_ref, by_ref, rows, tile):
    at_y = lax.axis_index(gy_axis)
    even_y = lax.rem(at_y, 2) == 0
    columns = tile.columns
    per = columns // halo
    on_right = (tile.lane < halo) & (at_y < lax.axis_size(gy_axis) - 1)
    on_left = (tile.lane >= columns - halo) & (at_y > 0)

    @memo
    def packs(n):
        a, b = ay_ref[n], by_ref[n]
        return jnp.where(even_y, a, b), jnp.where(even_y, b, a)

    def side(f, r):
        n = f * rows + r
        g = n % per
        right, left = packs(n // per)
        a, b = roll(right, -halo * g, 1), roll(left, -halo * (g + 1), 1)
        return jnp.where(on_right, a, jnp.where(on_left, b, 0.0))

    return side


STRESS = (XX, YY, ZZ, YZ, XZ, XY, PP)
SLOT = {XX: 0, XY: 1, XZ: 2, PP: 3}


def whole(mid, ends, axis, rows):
    last = lax.rem(lax.axis_index(axis), 2) == 1

    @memo
    def get(f, r):
        if 2 <= r < rows - 2:
            return read(mid, f, r - 2)
        top = r >= rows - 2
        at = rows - 1 - r if top else r
        a, b = read(ends[0], f, at), read(ends[1], f, at)
        if not top:
            a, b = b, a
        return W(jnp.where(last, a.m, b.m), jnp.where(last, a.h, b.h))

    return get


def message(tile, side, reach, s, a, p, msg, part_f, part_g, part_a, with_params):
    qs = memo(lambda r: adjoint_stress(p, a, r))
    q = lambda f, r: qs(r)[f]
    got, new, drives = forward_edge(tile, s, s, p, 0, False, True)
    more, lam = adjoint_edge(tile, q, a, p, 0, False, True)
    for m in range(6):
        write(part_f, new[m], m)
        part_g[m] = drives[m].m
        write(part_a, lam[m], m)
    got = got + more + ([p(PH, 0), p(PK, 0)] if with_params else [])
    for n, x in enumerate([w.m for w in got] + tile.pack([w.h for w in got], reach)):
        msg[n] = x


def spread_kernel(halo, gx_axis, gy_axis, fields_ref, cot_ref, pm_ref, ay_ref, by_ref, rec_ref, p_out, f_mid, a_mid, *outs):
    rows, planes, columns = pm_ref.shape[1:]
    tile = Tile(planes, columns, halo)
    side = spreader(halo, gy_axis, ay_ref, by_ref, rows, tile)
    base, count = p_out.shape[0], fields_ref.shape[0]
    for f in range(base):
        for r in range(rows):
            write(p_out, W(pm_ref[f, r], side(f, r)), f, r)
    ends = [Side(gx_axis, swap, rows) for swap in (0, 1)]
    groups = outs[:6], outs[6:]
    for f in range(count):
        for which, mid in enumerate((f_mid, a_mid)):
            values = []
            for r in range(rows):
                at = pl.ds(r, planes, stride=rows)
                if which:
                    value = W(cot_ref[f, at, :], side(base + count + f, r))
                    if f == PP:
                        value = value + read(rec_ref, rec_ref.shape[0] - 1, r)
                    values.append(value * read(p_out, PF, r))
                else:
                    values.append(W(fields_ref[f, at, :], side(base + f, r)))
            for r in range(2, rows - 2):
                write(mid, values[r], f, r - 2)
            for end, group in zip(ends, groups):
                for r in range(2):
                    x, y = values[rows - 1 - r], values[r]
                    write(group[which], W(jnp.where(end.last, x.m, y.m), jnp.where(end.last, x.h, y.h)), f, r)
    for end, group in zip(ends, groups):
        local = Tile(planes, columns, halo, end.flip)
        s, a = (lambda f, r, ref=ref: read(ref, f, r) for ref in group[:2])
        p = lambda f, r, end=end: read(p_out, f, end.row(r))
        message(local, end, halo - 1, s, a, p, *group[2:], True)


def sums(ff, aa):
    fo, pu, wo, ee, gg, w_ = ff[0:3], ff[3:6], ff[6:9], ff[9:12], ff[12:15], ff[15]
    af, ag, sg, pi = aa[0:3], aa[3:6], aa[6:12], aa[12]
    tr, dd = sg[0] + sg[1] + sg[2], ee[0] + ee[1] + ee[2]
    dot = lambda x, y: x[0] * y[0] + x[1] * y[1] + x[2] * y[2]
    return [
        dot(af, fo), dot(ag, pu), dot(af, pu), dot(ag, wo),
        tr * dd, tr * w_, 2.0 * dot(sg[0:3], ee) + dot(sg[3:6], gg), pi * dd, pi * w_,
    ]


def kept_rows(refs, rows, r):
    vel, strain, cot, sig = refs
    return (
        [vel[n, r - 1] for n in range(9)] + [strain[n, r - 2] for n in range(7)],
        [cot[n, r - 1] for n in range(6)] + [sig[n, r] for n in range(7)],
    )


def kept_end(refs, end_refs, side, r):
    vel, _, cot, sig = refs
    vel_end, strain_end, cot_end = end_refs
    at = side.row(r)
    first, third = (vel_end, cot_end) if r == 0 else (vel, cot)
    where = (lambda n, ref: ref[n]) if r == 0 else (lambda n, ref: ref[n, at - 1])
    return (
        [where(n, first) for n in range(9)] + [strain_end[n, r] for n in range(7)],
        [where(n, third) for n in range(6)] + [sig[n, at] for n in range(7)],
    )


def sums_kernel(axis, rows, count, *refs):
    out_mid, out_a, out_b = refs[-3:]
    pairs = [(refs[n : n + 10], refs[n + 10 : n + 20]) for n in range(0, 20 * count, 20)]
    def total(pick):
        acc = [0.0] * 9
        for fwd, adj in pairs:
            acc = [x + y for x, y in zip(acc, sums(pick(fwd)[0], pick(adj)[1]))]
        return acc
    for r in range(2, rows - 2):
        for n, x in enumerate(total(lambda refs: kept_rows(refs[:4], rows, r))):
            out_mid[n, r - 2] = x
    for swap, out in enumerate((out_a, out_b)):
        side = Side(axis, swap, rows)
        for r in range(2):
            for n, x in enumerate(total(lambda refs: kept_end(refs[:4], refs[4 + 3 * swap : 7 + 3 * swap], side, r))):
                out[n, r] = x


def gradients(acc, p, r):
    a1, a2, a3, a4, b1, b2, b3, b4, b5 = acc
    h, k, b, al = [p(n, r).m for n in (PH, PK, PB, PA)]
    h4 = 4.0 * h
    return [
        h4 * (a3 - 3.0 * a1),
        h4 * (a1 + a2 - k * (3.0 * a2 + a3)),
        -2.0 * a4,
        0.25 * b1,
        0.25 * b3,
        0.25 * (al * (b2 - b4) - b5),
        b * (b2 - b4),
    ]


def strains(tile, v, r):
    e = [tile.dx(v, VX, r), tile.dy(v(VY, r)), tile.dz(v(VZ, r))]
    g = [
        tile.dz(v(VY, r)) + tile.dy(v(VZ, r)),
        tile.dz(v(VX, r)) + tile.dx(v, VZ, r),
        tile.dy(v(VX, r)) + tile.dx(v, VY, r),
    ]
    return e, g, tile.dx(v, WX, r) + tile.dy(v(WY, r)) + tile.dz(v(WZ, r))


def new_fields(p, old, v, e, g, dw, source, r):
    dv = e[0] + e[1] + e[2]
    sh, b = p(PS, r), p(PB, r)
    ab = p(PA, r) * b
    common = p(PL, r) * dv + ab * dw
    new = {f: v(f, r) for f in range(6)}
    for i in range(3):
        new[XX + i] = old(XX + i, r) + (common + 2.0 * (sh * e[i]))
        new[YZ + i] = old(YZ + i, r) + sh * g[i]
    new[PP] = old(PP, r) - (ab * dv + b * dw) + source
    factor = p(PF, r)
    return {f: value * factor for f, value in new.items()}


def back_fields(tile, lam, c, vel, r):
    out = dict(vel)
    out[XX] = lam(XX, r) - tile.dx(c, 0, r)
    out[YY] = lam(YY, r) - tile.dy(c(1, r))
    out[ZZ] = lam(ZZ, r) - tile.dz(c(2, r))
    out[YZ] = lam(YZ, r) - (tile.dz(c(1, r)) + tile.dy(c(2, r)))
    out[XZ] = lam(XZ, r) - (tile.dz(c(0, r)) + tile.dx(c, 2, r))
    out[XY] = lam(XY, r) - (tile.dy(c(0, r)) + tile.dx(c, 1, r))
    out[PP] = lam(PP, r) + (tile.dx(c, 3, r) + tile.dy(c(4, r)) + tile.dz(c(5, r)))
    return out


def push_cots(p, r, lv, lw):
    h, k, m = p(PH, r), p(PK, r), p(PM, r)
    cf = [h * (3.0 * lv[i] - lw[i]) for i in range(3)]
    cg = [h * (k * lw[i] - lv[i]) for i in range(3)]
    vel = {VX + i: lv[i] for i in range(3)} | {WX + i: lw[i] - m * cg[i] for i in range(3)}
    return cf + cg, vel


def near(rows):
    return (1, 2, rows - 3, rows - 2)


def interior_kernel(gx_axis, halo, j, steps, *refs):
    refs = list(refs)
    take = lambda n: [refs.pop(0) for _ in range(n)]
    final = j == steps - 1
    f_mid, fa, fb, a_mid, aa, ab, p_ref = take(7)
    if final:
        kept, (acc_ref,) = take(4), take(1)
        grad_out, par_out = take(2)
    else:
        src_ref, rec_ref, f_out, a_out = take(4)
    save_vel, save_str, save_cot, save_sig = take(4)
    v_near, c_near, l_near = take(3)
    assert not refs
    rows, planes, columns = p_ref.shape[1], p_ref.shape[2] // 2, p_ref.shape[3]
    tile = Tile(planes, columns, halo)
    p = lambda f, r: read(p_ref, f, r)
    old, lam = whole(f_mid, (fa, fb), gx_axis, rows), whole(a_mid, (aa, ab), gx_axis, rows)

    @memo
    def velocity(r):
        _, new, drives = forward_edge(tile, old, old, p, r, True, True)
        return new, [x.m for x in drives] + [old(WX + i, r).m for i in range(3)]

    qs = memo(lambda r: adjoint_stress(p, lam, r))
    q = lambda f, r: qs(r)[f]

    @memo
    def cots(r):
        forces, slopes = momentum(tile, q, r)
        return push_cots(
            p, r, [lam(VX + i, r) - forces[i] for i in range(3)], [lam(WX + i, r) - slopes[i] for i in range(3)]
        )

    v = lambda f, r: velocity(r)[0][f]
    c = lambda i, r: cots(r)[0][i]
    for r in range(1, rows - 1):
        if r in near(rows):
            at = near(rows).index(r)
            for n in range(6):
                write(v_near, v(n, r), n, at)
                write(c_near, c(n, r), n, at)
                write(l_near, cots(r)[1][n], n, at)
        for n, x in enumerate(velocity(r)[1]):
            save_vel[n, r - 1] = x
        for n in range(6):
            save_cot[n, r - 1] = c(n, r).m
        if not 2 <= r < rows - 2:
            continue
        e, g, dw = strains(tile, v, r)
        strain = [x.m for x in e + g] + [dw.m]
        back = back_fields(tile, lam, c, cots(r)[1], r)
        if final:
            ff = velocity(r)[1] + strain
            cc = [c(n, r).m for n in range(6)] + [lam(f, r).m for f in STRESS]
            kept_f, kept_a = kept_rows(kept, rows, r)
            acc = [acc_ref[n, r - 2] + (x + y) for n, (x, y) in enumerate(zip(sums(ff, kept_a), sums(kept_f, cc)))]
            for n, x in enumerate(gradients(acc, p, r)):
                par_out[n, r - 2] = x
            for f, value in back.items():
                grad_out[f, r - 2] = value.m
            continue
        for n, x in enumerate(strain):
            save_str[n, r - 2] = x
        for f, value in new_fields(p, old, v, e, g, dw, read(src_ref, j, r), r).items():
            write(f_out, value, f, r - 2)
        back[PP] = back[PP] + read(rec_ref, steps - 2 - j, r)
        for f, value in back.items():
            write(a_out, value * p(PF, r), f, r - 2)
    for r in range(rows):
        for n, f in enumerate(STRESS):
            save_sig[n, r] = lam(f, r).m


def end_kernel(gx_axis, swap, halo, j, steps, *refs):
    refs = list(refs)
    take = lambda n: [refs.pop(0) for _ in range(n)]
    first, final = j == 0, j == steps - 1
    f_ref, a_ref, p_ref, msg_ref, part_f, part_g, part_a, v_near, c_near, l_near = take(10)
    if not first:
        (hk_ref,) = take(1)
    if final:
        kept, kept_ends, (acc_ref, now_vel) = take(4), take(3), take(2)
        if swap:
            grad_mid, par_mid, grad_other, par_other = take(4)
        grad_out, par_out = take(2)
    else:
        src_ref, rec_ref, f_out, a_out, save_vel, save_str, save_cot = take(7)
        outs = take(4)
    if first:
        (hk_out,) = take(1)
    assert not refs
    rows, planes, columns = p_ref.shape[1], p_ref.shape[2] // 2, p_ref.shape[3]
    side = Side(gx_axis, swap, rows)
    tile = Tile(planes, columns, halo, side.flip)
    got = receive(tile, side, msg_ref, 2 * EDGE + (2 if first else 0), halo - 1 - 2 * j)
    p = lambda f, r: read(p_ref, f, side.row(r))
    old, lam = (lambda f, r: read(f_ref, f, r)), (lambda f, r: read(a_ref, f, r))
    if first:
        h2, k2 = got[2 * EDGE :]
        write(hk_out, h2, 0)
        write(hk_out, k2, 1)
    else:
        h2, k2 = read(hk_ref, 0), read(hk_ref, 1)

    def add_forward(base, h, k, values):
        xx, xy, xz, pp = [h * x for x in values]
        adds = [3.0 * xx + pp, 3.0 * xy, 3.0 * xz, -(k * pp + xx), -xy, -xz]
        return [x + y for x, y in zip(base, adds)]

    qs = memo(lambda r: adjoint_stress(p, lam, r))
    near_s, near_v, near_q, near_c = [got[n : n + 4] for n in range(0, 16, 4)]
    velocities, cots, vels = {}, {}, {}
    sign = -side.flip
    velocities[0] = add_forward([read(part_f, m) for m in range(6)], p(PH, 0) * sign, p(PK, 0), near_s)
    velocities[-1] = add_forward(near_v, h2 * side.flip, k2, [old(f, 0) for f in SLOT])
    xx, xy, xz, pp = [x.m * sign for x in near_s]
    drives = [part_g[0] + xx, part_g[1] + xy, part_g[2] + xz, part_g[3] - pp, part_g[4], part_g[5]]
    drives += [old(WX + i, 0).m for i in range(3)]
    base = [read(part_a, m) for m in range(6)]
    for m in range(4):
        base[m] = base[m] - near_q[m] * sign
    cots[0], vels[0] = push_cots(p, 0, base[0:3], base[3:6])
    t = h2 * sign
    xx, xy, xz, pp = [t * qs(0)[f] for f in SLOT]
    cots[-1] = [near_c[0] + (3.0 * xx - pp), near_c[1] + 3.0 * xy, near_c[2] + 3.0 * xz, near_c[3] + (k2 * pp - xx)]
    for r in (1, 2):
        at = side.near(r)
        velocities[r] = [read(v_near, n, at) for n in range(6)]
        cots[r] = [read(c_near, n, at) for n in range(6)]
        vels[r] = {n: read(l_near, n, at) for n in range(6)}
    v = lambda f, r: velocities[r][f]
    c = lambda i, r: cots[r][i]
    finals = []
    for r in range(2):
        e, g, dw = strains(tile, v, r)
        strain = [x.m for x in e + g] + [dw.m]
        back = back_fields(tile, lam, c, vels[r], r)
        if final:
            drive = drives if r == 0 else [now_vel[n, side.row(r) - 1] for n in range(9)]
            cc = [c(n, r).m for n in range(6)] + [lam(f, r).m for f in STRESS]
            kept_f, kept_a = kept_end(kept, kept_ends, side, r)
            adds = zip(sums(drive + strain, kept_a), sums(kept_f, cc))
            acc = [acc_ref[n, r] + (x + y) for n, (x, y) in enumerate(adds)]
            finals.append(([back[f].m for f in range(len(back))], gradients(acc, p, r)))
            continue
        if r == 0:
            for n, x in enumerate(drives):
                save_vel[n] = x
            for n in range(6):
                save_cot[n] = c(n, 0).m
        for n, x in enumerate(strain):
            save_str[n, r] = x
        new = new_fields(p, old, v, e, g, dw, read(src_ref, j, side.row(r)), r)
        back[PP] = back[PP] + read(rec_ref, steps - 2 - j, side.row(r))
        factor = p(PF, r)
        for f in range(f_out.shape[0]):
            write(f_out, new[f], f, r)
            write(a_out, back[f] * factor, f, r)
    if not final:
        s, a = (lambda f, r: read(f_out, f, r)), (lambda f, r: read(a_out, f, r))
        message(tile, side, halo - 1 - 2 * (j + 1), s, a, p, *outs, False)
        return
    for which, out in enumerate((grad_out, par_out)):
        for n in range(out.shape[0]):
            if not swap:
                for r in range(2):
                    out[n, r] = finals[r][which][n]
                continue
            mid, other = ((grad_mid, grad_other), (par_mid, par_other))[which]
            for r in range(2):
                mine, its = finals[r][which][n], other[n, r]
                out[n, pl.ds(r, planes, stride=rows), :] = jnp.where(side.last, its, mine)
                out[n, pl.ds(rows - 1 - r, planes, stride=rows), :] = jnp.where(side.last, mine, its)
            for r in range(2, rows - 2):
                out[n, pl.ds(r, planes, stride=rows), :] = mid[n, r - 2]


def swaps(axis, odd):
    nx, ny = lax.axis_size("gx"), lax.axis_size("gy")
    count, other = (nx, ny) if axis == "gx" else (ny, nx)
    place = (lambda i, k: i * ny + k) if axis == "gx" else (lambda i, k: k * ny + i)
    out, met = [], set()
    for i in range(odd, count - 1, 2):
        met |= {i, i + 1}
        for k in range(other):
            out += [(place(i, k), place(i + 1, k)), (place(i + 1, k), place(i, k))]
    for i in set(range(count)) - met:
        for k in range(0, other - 1, 2):
            out += [(place(i, k), place(i, k + 1)), (place(i, k + 1), place(i, k))]
    return sorted(out)


def swap_rows(axis, number, message):
    return lax.ppermute(message, ("gx", "gy"), swaps(axis, number))


def call(kernel, outs, *args):
    shapes = [o if isinstance(o, jax.ShapeDtypeStruct) else jax.ShapeDtypeStruct(o, jnp.float32) for o in outs]
    return pl.pallas_call(
        kernel,
        out_shape=shapes,
        in_specs=[pl.BlockSpec(memory_space=pltpu.VMEM)] * len(args),
        out_specs=[pl.BlockSpec(memory_space=pltpu.VMEM)] * len(outs),
        compiler_params=pltpu.CompilerParams(vmem_limit_bytes=48 << 20),
    )(*args)


def per_device(
    fields, density, fluid_density, mobility, lame_lambda, shear_modulus, biot_modulus, biot_coef,
    region_mask, profile_index, profile_table, source_cells, source_amp, receiver_cells, field_cot, receiver_cot,
):
    planes, rows, columns = region_mask.shape
    steps = source_amp.shape[0]
    count = fields.shape[0]
    halo = 2 * steps
    assert steps > 2 and planes == 8 and columns == 128 and columns % (2 * halo) == 0 and rows > 1
    flat = lambda x: x.reshape(-1, planes * rows, columns)
    fields, field_cot = flat(fields), flat(field_cot)
    raw = [flat(x) for x in (density, fluid_density, mobility, lame_lambda, shear_modulus, biot_modulus, biot_coef)]
    packs = -(-(2 * count + 8) * rows * halo // columns)
    own, wide = (rows, planes, columns), (rows, 2 * planes, columns)

    table = profile_table[None]
    small = [receiver_cells[None], receiver_cot, source_cells[None], source_amp]
    inputs = [*raw, table, flat(region_mask), flat(profile_index), fields, field_cot, *small]
    whole = [fields, field_cot, *small]
    plane = (planes * rows, columns)

    def start(*refs):
        refs = list(refs)
        hbm = refs[:7] + refs[8:10] + refs[7:8] + refs[10:16]
        start_kernel(halo, "gy", hbm, refs[16:25], refs[25:])

    p_own, ay, by, fields, field_cot, *small = pl.pallas_call(
        start,
        out_shape=[jax.ShapeDtypeStruct(s, jnp.float32) for s in [(8, *own)] + [(packs, planes, columns)] * 2]
        + [jax.ShapeDtypeStruct(x.shape, x.dtype) for x in whole],
        in_specs=[pl.BlockSpec(memory_space=pltpu.HBM)] * 16,
        out_specs=[pl.BlockSpec(memory_space=pltpu.VMEM)] * 9,
        scratch_shapes=[
            pltpu.VMEM((7, 1, *plane), jnp.float32), pltpu.VMEM((1, *plane), jnp.int32),
            pltpu.VMEM((1, *plane), jnp.int32), pltpu.SMEM(table.shape, jnp.float32),
            pltpu.SemaphoreType.DMA((16,)),
        ],
        compiler_params=pltpu.CompilerParams(vmem_limit_bytes=48 << 20),
    )(*[pltpu.with_memory_space_constraint(x, pltpu.HBM) for x in inputs])
    ay, by = swap_rows("gy", 0, ay), swap_rows("gy", 1, by)
    rec, src = call(functools.partial(inject_kernel, halo, "gx", "gy"), [(steps, *wide)] * 2, *small)
    def tiles(n, reach):
        return n + -(-n // (columns // (2 * reach))), planes, columns

    assert rows >= 6
    w, m = wide[1:], own[1:]
    parts = [(6, *w), (6, *m), (6, *w)]
    mid, end = (count, rows - 4, *w), (count, 2, *w)
    group = [end, end, tiles(2 * EDGE + 2, halo - 1)] + parts
    p, fm, am, *rest = call(
        functools.partial(spread_kernel, halo, "gx", "gy"), [(8, *wide), mid, mid] + group * 2,
        fields, field_cot, p_own, ay, by, rec,
    )
    ends = [rest[:6], rest[6:]]
    coming = [swap_rows("gx", 1 - swap, ends[swap][2]) for swap in (0, 1)]
    hk, kept = [[], []], []
    saves = [(9, rows - 2, *m), (7, rows - 4, *m), (6, rows - 2, *m), (7, *own)]
    nears = [(6, 4, *w)] * 3
    for j in range(steps - 1):
        fm, am, *rest = call(
            functools.partial(interior_kernel, "gx", halo, j, steps), [mid, mid] + saves + nears,
            fm, ends[0][0], ends[1][0], am, ends[0][1], ends[1][1], p, src, rec,
        )
        kept.append(rest[:4])
        near_refs = rest[4:]
        for swap in (0, 1):
            f, a, _, *part_refs = ends[swap]
            outs = [end, end, (9, *m), (7, 2, *m), (6, *m), tiles(2 * EDGE, halo - 1 - 2 * (j + 1))] + parts
            outs += [] if j else [(2, *w)]
            f, a, vel, strain, cot, message_out, *rest = call(
                functools.partial(end_kernel, "gx", swap, halo, j, steps), outs,
                f, a, p, coming[swap], *part_refs, *near_refs, *hk[swap], src, rec,
            )
            ends[swap] = [f, a, message_out, *rest[:3]]
            coming[swap] = swap_rows("gx", 1 - swap, message_out)
            hk[swap] = hk[swap] or rest[3:]
            kept[j] = kept[j] + [vel, strain, cot]
    middle = [x for t in range(1, steps - 1) for x in kept[t] + kept[steps - 1 - t]]
    accs = call(
        functools.partial(sums_kernel, "gx", rows, steps - 2), [(9, rows - 4, *m), (9, 2, *m), (9, 2, *m)], *middle
    )
    grad_mid, par_mid, vel, _, _, _, *near_refs = call(
        functools.partial(interior_kernel, "gx", halo, steps - 1, steps),
        [(count, rows - 4, *m), (7, rows - 4, *m)] + saves + nears,
        fm, ends[0][0], ends[1][0], am, ends[0][1], ends[1][1], p, *kept[0][:4], accs[0],
    )
    done = []
    for swap in (0, 1):
        f, a, _, *part_refs = ends[swap]
        outs = [(count, *plane), (7, *plane)] if swap else [(count, 2, *m), (7, 2, *m)]
        done = call(
            functools.partial(end_kernel, "gx", swap, halo, steps - 1, steps), outs,
            f, a, p, coming[swap], *part_refs, *near_refs, *hk[swap], *kept[0][:4],
            *kept[0][4 + 3 * swap : 7 + 3 * swap], accs[1 + swap], vel, *([grad_mid, par_mid] * swap), *done,
        )
    return done[0].reshape(count, planes, rows, columns), done[1].reshape(7, planes, rows, columns)


def solution(mesh):
    plane, field = P(None, "gx", "gy"), P(None, None, "gx", "gy")
    in_specs = (field,) + (plane,) * 9 + (P(),) * 4 + (field, P())
    return jax.shard_map(per_device, mesh=mesh, in_specs=in_specs, out_specs=(field, field), check_vma=False)
```
